32 devices in a mesh: ctx: 16 (over z, y, x), fsdp: 2 (over core).
Axes of the slice: x: 2, y: 2, z: 4, core: 2. Of those that a mesh axis runs over, the one named last changes fastest.
Arguments:
- layer_input: bfloat16 [2, 2048, 2048], P('fsdp', 'ctx'), may hold values from -6 to 6
- block_table: int32 [2, 16, 2], P('fsdp'), may hold values from 0 to 31, as said below
- attn_gain: bfloat16 [2048], P(('ctx', 'fsdp')), may hold values from 0.25 to 1.75
- query_weight: bfloat16 [2048, 2048], P(('ctx', 'fsdp')), may hold values from -0.125 to 0.125
- key_weight: bfloat16 [2048, 2048], P(('ctx', 'fsdp')), may hold values from -0.125 to 0.125
- value_weight: bfloat16 [2048, 2048], P(('ctx', 'fsdp')), may hold values from -0.125 to 0.125
- out_weight: bfloat16 [2048, 2048], P(('ctx', 'fsdp')), may hold values from -3 to 3
- mlp_gain: bfloat16 [2048], P(('ctx', 'fsdp')), may hold values from 0.25 to 1.75
- gate_weight: bfloat16 [2048, 8192], P(('ctx', 'fsdp')), may hold values from -0.125 to 0.125
- up_weight: bfloat16 [2048, 8192], P(('ctx', 'fsdp')), may hold values from -0.125 to 0.125
- down_weight: bfloat16 [2048, 8192], P(('ctx', 'fsdp')), may hold values from -0.0625 to 0.0625
- cotangent: bfloat16 [2, 2048, 2048], P('fsdp', 'ctx'), may hold values from -6 to 6
Outputs:
- layer_output: bfloat16 [2, 2048, 2048], P('fsdp', 'ctx')
- input_grad: float32 [2, 2048, 2048], P('fsdp', 'ctx')
- attn_gain_grad: float32 [2048], P(('ctx', 'fsdp'))
- query_weight_grad: float32 [2048, 2048], P(('ctx', 'fsdp'))
- key_weight_grad: float32 [2048, 2048], P(('ctx', 'fsdp'))
- value_weight_grad: float32 [2048, 2048], P(('ctx', 'fsdp'))
- out_weight_grad: float32 [2048, 2048], P(('ctx', 'fsdp'))
- mlp_gain_grad: float32 [2048], P(('ctx', 'fsdp'))
- gate_weight_grad: float32 [2048, 8192], P(('ctx', 'fsdp'))
- up_weight_grad: float32 [2048, 8192], P(('ctx', 'fsdp'))
- down_weight_grad: float32 [2048, 8192], P(('ctx', 'fsdp'))
The draws below stay inside these ranges and needn't reach their ends.
Inputs may be any that keep to these rules, and one draw needn't show every extreme that they name: For each sequence s and ctx index c, block_table[s, c] holds two block numbers b and 31 - b, in either order; each block number appears exactly once in a sequence's table. Rows of layer_input and cotangent follow the table: ctx index c holds the 64 positions of its first block, then those of its second.
All inputs are finite; a program needn't handle non-finite values.
Results may differ from the reference program's by a relative error of at most 0.035.
Values may be sent and summed in bfloat16 or wider, within the bound.
A program may use at most 704 MiB of HBM per device.

```python
import jax
import jax.numpy as jnp
from jax import lax

D = 2048
HEADS = 32
HD = 64
FF = 8192
SEQS = 2
LEN = 2048
BLK = 64
N_CTX = 16


def draw_block_table(key, part):
    tables = []
    for sequence in range(SEQS):
        seq_key = jax.random.fold_in(key, 17 + sequence)
        order = jax.random.permutation(seq_key, N_CTX).astype(jnp.int32)
        flipped = jax.random.randint(jax.random.fold_in(seq_key, 3), (N_CTX,), 0, 2)
        mirror = 2 * N_CTX - 1 - order
        first_block = jnp.where(flipped == 1, mirror, order)
        second_block = jnp.where(flipped == 1, order, mirror)
        tables.append(jnp.stack([first_block, second_block], -1))
    return jnp.stack(tables).astype(jnp.int32)


def block_scale(key, extent, shards, least, top_value):
    factor_of, own = 1.0, jax.random.fold_in(key, 6)
    for axis_at, shards_of in shards:
        heights = jnp.exp(jax.random.uniform(jax.random.fold_in(own, axis_at), (shards_of,), jnp.float32, least / len(shards), top_value / len(shards)))
        factor_of = factor_of * jnp.repeat(heights, extent[axis_at] // shards_of).reshape([-1 if axis == axis_at else 1 for axis in range(len(extent))])
    return factor_of


def centred(rng, extent, width, most, pieces=(), kind=jnp.bfloat16):
    array = width * jax.random.normal(rng, extent, jnp.float32)
    if pieces:
        array = array * block_scale(rng, extent, pieces, -0.22, 0.18)
    return jnp.clip(array, -most, most).astype(kind)


def setup_inputs(seed: int = 0) -> dict:
    streams_of = jax.random.split(jax.random.key(seed), 13)
    layer_input = centred(streams_of[0], (SEQS, LEN, D), 1.0, 6.0, ((0, 2), (1, 16)))
    block_table = draw_block_table(jax.random.fold_in(streams_of[12], 71), 0)
    attn_gain = jnp.clip(1.0 + 0.15 * jax.random.normal(streams_of[2], (D,), jnp.float32), 0.25, 1.75).astype(jnp.bfloat16)
    query_weight = centred(streams_of[3], (D, D), D ** -0.5, 0.125, ((0, 32),))
    key_weight = centred(streams_of[4], (D, D), D ** -0.5, 0.125, ((0, 32),))
    value_weight = centred(streams_of[5], (D, D), D ** -0.5, 0.125, ((0, 32),))
    out_weight = centred(streams_of[6], (D, D), (max(1, D * 4 // LEN)) ** -0.5, 3.0, ((0, 32),))
    mlp_gain = jnp.clip(1.0 + 0.15 * jax.random.normal(streams_of[7], (D,), jnp.float32), 0.25, 1.75).astype(jnp.bfloat16)
    gate_weight = centred(streams_of[8], (D, FF), D ** -0.5, 0.125, ((0, 32),))
    up_weight = centred(streams_of[9], (D, FF), D ** -0.5, 0.125, ((0, 32),))
    down_weight = centred(streams_of[10], (D, FF), FF ** -0.5, 0.0625, ((0, 32),))
    cotangent = centred(streams_of[11], (SEQS, LEN, D), 1.0, 6.0, ((0, 2), (1, 16)))
    return dict(layer_input=layer_input, block_table=block_table, attn_gain=attn_gain, query_weight=query_weight, key_weight=key_weight, value_weight=value_weight, out_weight=out_weight, mlp_gain=mlp_gain, gate_weight=gate_weight, up_weight=up_weight, down_weight=down_weight, cotangent=cotangent)


EPSILON = 1e-05
THETA_BASE = 130000.0
MASKED = -1e+30
HIGHEST = lax.Precision.HIGHEST

@jax.custom_vjp
def low(v):
    return lax.optimization_barrier(v.astype(jnp.bfloat16)).astype(jnp.float32)

@jax.custom_vjp
def low_back(v):
    return v

def low_keep(v):
    return (low(v), None)

def low_pass(kept, grad):
    return (grad,)

def back_keep(v):
    return (v, None)

def back_low(kept, grad):
    return (low(grad),)
low.defvjp(low_keep, low_pass)
low_back.defvjp(back_keep, back_low)

def matmul_high(left_side, right_side):
    return jnp.dot(left_side, right_side, precision=HIGHEST, preferred_element_type=jnp.float32)

def rope_tables(positions):
    inv_freq = THETA_BASE ** (-(jnp.arange(HD // 2, dtype=jnp.float32) * 2.0 / HD))
    angles = positions.astype(jnp.float32)[:, None] * inv_freq[None, :]
    cosine = jnp.cos(angles)
    sine_tab = jnp.sin(angles)
    return (jnp.concatenate([cosine, cosine], -1), jnp.concatenate([sine_tab, sine_tab], -1))

def rotate(values, cosine, sine_tab):
    middle = values.shape[-1] // 2
    turned = jnp.concatenate([-values[..., middle:], values[..., :middle]], -1)
    return values * cosine[:, None, :] + turned * sine_tab[:, None, :]

def rms_norm(rows_in, gain_vec):
    return rows_in * lax.rsqrt(lax.optimization_barrier(jnp.mean(rows_in * rows_in, -1, keepdims=True)) + EPSILON) * gain_vec

def attend(queries, key_rows, value_rows, positions):
    step_rows = min(512, LEN)
    score_scale = HD ** (-0.5)

    def attend_block(block_item):
        query_rows, query_pos = block_item
        scores = jnp.einsum('qhd,khd->hqk', query_rows, key_rows, precision=HIGHEST) * score_scale
        scores = low_back(scores)
        visible = positions[None, None, :] <= query_pos[None, :, None]
        scores = jnp.where(visible, scores, MASKED)
        largest = lax.optimization_barrier(jnp.max(scores, -1, keepdims=True))
        weights = jnp.where(visible, jnp.exp(scores - largest), 0.0)
        probabilities = weights / lax.optimization_barrier(jnp.sum(weights, -1, keepdims=True))
        return jnp.einsum('hqk,khd->qhd', low(probabilities), value_rows, precision=HIGHEST)
    blocks = LEN // step_rows
    attended = lax.map(jax.checkpoint(attend_block), (queries.reshape(blocks, step_rows, HEADS, HD), positions.reshape(blocks, step_rows)))
    return attended.reshape(LEN, HEADS * HD)

def reference(layer_input, block_table, attn_gain, query_weight, key_weight, value_weight, out_weight, mlp_gain, gate_weight, up_weight, down_weight, cotangent):
    inner = jnp.arange(BLK, dtype=jnp.int32)
    positions = (block_table[:, :, :, None] * BLK + inner[None, None, None, :]).reshape(SEQS, LEN).astype(jnp.int32)

    def forward(inputs, attn_gain, query_weight, key_weight, value_weight, out_weight, mlp_gain, gate_weight, up_weight, down_weight):
        outputs = []
        for sequence in range(SEQS):
            cosine, sine_tab = rope_tables(positions[sequence])
            source = inputs[sequence]
            normed = low(rms_norm(source, attn_gain))
            query_pre = low_back(matmul_high(normed, query_weight)).reshape(LEN, HEADS, HD)
            key_pre = low_back(matmul_high(normed, key_weight)).reshape(LEN, HEADS, HD)
            value_low = low(low_back(matmul_high(normed, value_weight))).reshape(LEN, HEADS, HD)
            queries = low(rotate(query_pre, cosine, sine_tab))
            keys_low = low(rotate(key_pre, cosine, sine_tab))
            attended = attend(queries, keys_low, value_low, positions[sequence])
            attn_low = low(low_back(attended))
            hidden = source + low_back(matmul_high(attn_low, out_weight))
            mlp_in = low(rms_norm(hidden, mlp_gain))
            gate_pre = low_back(matmul_high(mlp_in, gate_weight))
            up_pre = low_back(matmul_high(mlp_in, up_weight))
            activation = low(jax.nn.silu(gate_pre) * up_pre)
            outputs.append(hidden + low_back(matmul_high(activation, down_weight.T)))
        return jnp.stack(outputs)
    floats = [array_in.astype(jnp.float32) for array_in in (layer_input, attn_gain, query_weight, key_weight, value_weight, out_weight, mlp_gain, gate_weight, up_weight, down_weight)]
    result, pullback = jax.vjp(forward, *floats)
    gradients = pullback(cotangent.astype(jnp.float32))
    return (result.astype(jnp.bfloat16), gradients[0], gradients[1], gradients[2], gradients[3], gradients[4], gradients[5], gradients[6], gradients[7], gradients[8], gradients[9])
```

```python
import functools
import jax, jax.numpy as jnp
from jax import lax
from jax.experimental import pallas as pl
from jax.experimental.pallas import tpu as pltpu

MESH = pl.DeviceIdType.MESH
DMA = pltpu.SemaphoreType.DMA
BF = jnp.bfloat16
F32 = jnp.float32


class Plan:
    def __init__(self):
        self.steps = []

    def at(self, when, step):
        self.steps.append((when, len(self.steps), step))

    def run(self):
        for _, _, step in sorted(self.steps, key=lambda s: s[:2]):
            step()


class Here:
    def __init__(self):
        self.me = lax.axis_index("ctx")
        self.core = lax.axis_index("fsdp")
        self.z = self.me // 4
        self.y = lax.rem(self.me // 2, 2)
        self.x = lax.rem(self.me, 2)
        self.xy = lax.rem(self.me, 4)
        self.xn = self.me + 1 - 2 * self.x
        self.yn = self.me + 2 - 4 * self.y


def remote(src, dst, send_sem, recv_sem, **device):
    return pltpu.make_async_remote_copy(
        src_ref=src, dst_ref=dst, send_sem=send_sem, recv_sem=recv_sem, device_id=device, device_id_type=MESH
    )


def greet_all(h):
    barrier = pltpu.get_barrier_semaphore()
    for step in range(1, 16):
        pl.semaphore_signal(barrier, inc=1, device_id={"ctx": jnp.bitwise_xor(h.me, step)}, device_id_type=MESH)
    pl.semaphore_signal(barrier, inc=1, device_id={"fsdp": 1 - h.core}, device_id_type=MESH)
    pl.semaphore_wait(barrier, 16)


GATHER_SEMS = [DMA((4,))] * 12 + [DMA]


def gather16(plan, h, src, out, sems, t0, tz, tx):
    us, ur, ds, dr, xs, xr, ys, yr, xfs, xfr, yfs, yfr, own = sems
    half = src.shape[0] // 2

    def plane(zz, source=None):
        s = zz * 4 + h.xy
        source = out.at[s] if source is None else source
        return (
            remote(source, out.at[s], xs.at[zz], xr.at[zz], ctx=h.xn),
            remote(source, out.at[s], ys.at[zz], yr.at[zz], ctx=h.yn),
        )

    def across(zz):
        sx = zz * 4 + lax.rem(h.xn, 4)
        sy = zz * 4 + lax.rem(h.yn, 4)
        top, low = pl.ds(0, half), pl.ds(half, half)
        return (
            remote(out.at[sx, top], out.at[sx, top], yfs.at[zz], yfr.at[zz], ctx=h.yn),
            remote(out.at[sy, low], out.at[sy, low], xfs.at[zz], xfr.at[zz], ctx=h.xn),
        )

    def arrived(zz):
        sx = zz * 4 + lax.rem(h.xn, 4)
        sy = zz * 4 + lax.rem(h.yn, 4)
        return (
            remote(out.at[sx], out.at[sx], xs.at[zz], xr.at[zz], ctx=h.xn),
            remote(out.at[sy], out.at[sy], ys.at[zz], yr.at[zz], ctx=h.yn),
        )

    def hop(k, up, source=None):
        it = (h.z - k if up else h.z + k) * 4 + h.xy
        send, recv = (us, ur) if up else (ds, dr)
        source = out.at[it] if source is None else source
        to = h.me + 4 if up else h.me - 4
        return remote(source, out.at[it], send.at[k], recv.at[k + 1], ctx=to)

    def landed(k, up):
        it = (h.z - k if up else h.z + k) * 4 + h.xy
        send, recv = (us, ur) if up else (ds, dr)
        return remote(out.at[it], out.at[it], send.at[k - 1], recv.at[k], ctx=h.me)

    local = pltpu.make_async_copy(src, out.at[h.me], own)

    def first():
        pl.when(h.z < 3)(lambda: hop(0, True, src).start())
        pl.when(h.z > 0)(lambda: hop(0, False, src).start())
        for c in plane(h.z, src):
            c.start()
        local.start()

    plan.at(t0, first)

    def step(k, up):
        def go():
            landed(k, up).wait_recv()
            if k < 3:
                pl.when((h.z < 3) if up else (h.z > 0))(lambda: hop(k, up).start())
            for c in plane(h.z - k if up else h.z + k):
                c.start()

        pl.when((h.z >= k) if up else (h.z + k <= 3))(go)

    def forward(zz):
        got, on = arrived(zz), across(zz)
        for g, c in zip(got, on):
            g.wait_recv()
            c.start()

    def finish(zz):
        sx = zz * 4 + 3 - h.xy
        top, low = pl.ds(0, half), pl.ds(half, half)
        remote(out.at[sx, top], out.at[sx, top], yfs.at[zz], yfr.at[zz], ctx=h.yn).wait_recv()
        remote(out.at[sx, low], out.at[sx, low], xfs.at[zz], xfr.at[zz], ctx=h.xn).wait_recv()

    plan.at(t0 + 0.8 * tx, lambda: forward(h.z))
    for k in (1, 2, 3):
        for up in (True, False):
            valid = (lambda k=k, up=up: (h.z >= k) if up else (h.z + k <= 3))
            plan.at(t0 + k * tz, functools.partial(step, k, up))
            zz = (lambda k=k, up=up: h.z - k if up else h.z + k)
            plan.at(t0 + (k + 0.8) * tx, lambda v=valid, q=zz: pl.when(v())(lambda: forward(q())))

    def drain():
        for zz in range(4):
            finish(zz)
        for k in range(3):
            pl.when((h.z >= k) & (h.z < 3))(lambda: hop(k, True).wait_send())
            pl.when((h.z + k <= 3) & (h.z > 0))(lambda: hop(k, False).wait_send())
        for zz in range(4):
            for c in plane(zz) + across(zz):
                c.wait_send()
        local.wait()

    plan.at(t0 + 4.5 * tx, drain)


SCATTER_SEMS = [DMA((4,))] * 8 + [DMA((4,))] * 2


def scatter_scratch(rows, width):
    half = width // 2
    return [
        pltpu.VMEM((4, 2, rows, half), BF),
        pltpu.VMEM((4, 2, rows, half), BF),
        pltpu.VMEM((4, rows, half), BF),
        pltpu.VMEM((4, rows, half), BF),
        pltpu.VMEM((4, rows, half), BF),
        pltpu.VMEM((4, rows, half), BF),
        pltpu.VMEM((3, rows, width), BF),
        pltpu.VMEM((3, rows, width), BF),
    ] + SCATTER_SEMS


N_SCATTER = 18
AHEAD = 2


def scatter16(plan, h, part, out, scratch, t0, tx):
    ra, rb, sa, sb, qa, qb, sz, rz = scratch[:8]
    as_, ar, bs, br, cs, cr, es, er, zs, zr = scratch[8:]
    rows, width = part.shape[3:]
    half = width // 2
    lo, hi = pl.ds(0, half), pl.ds(half, half)
    xo, yo = 1 - h.x, 1 - h.y

    def place(k):
        return lax.rem(h.z + k, 4)

    def first(i, k):
        return (
            remote(part.at[place(k), :, xo, :, lo], ra.at[i], as_.at[i], ar.at[i], ctx=h.xn),
            remote(part.at[place(k), yo, :, :, hi], rb.at[i], bs.at[i], br.at[i], ctx=h.yn),
        )

    def second(i):
        return (
            remote(sa.at[i], qa.at[i], cs.at[i], cr.at[i], ctx=h.yn),
            remote(sb.at[i], qb.at[i], es.at[i], er.at[i], ctx=h.xn),
        )

    def third(k):
        return remote(sz.at[k - 1], rz.at[k - 1], zs.at[k], zr.at[k], ctx=place(k) * 4 + h.xy)

    def start(i, k):
        for c in first(i, k):
            c.start()

    def middle(i, k):
        a, b = first(i, k)
        c, e = second(i)
        a.wait_recv()
        sa[i] = (part[place(k), yo, h.x, :, lo].astype(F32) + ra[i, yo].astype(F32)).astype(BF)
        c.start()
        b.wait_recv()
        sb[i] = (part[place(k), h.y, xo, :, hi].astype(F32) + rb[i, xo].astype(F32)).astype(BF)
        e.start()

    def total(i, k):
        c, e = second(i)
        c.wait_recv()
        e.wait_recv()
        left = part[place(k), h.y, h.x, :, lo].astype(F32) + ra[i, h.y].astype(F32) + qa[i].astype(F32)
        right = part[place(k), h.y, h.x, :, hi].astype(F32) + rb[i, h.x].astype(F32) + qb[i].astype(F32)
        if k:
            sz[k - 1, :, lo] = left.astype(BF)
            sz[k - 1, :, hi] = right.astype(BF)
            third(k).start()
        else:
            out[:, lo] = left
            out[:, hi] = right

    def last():
        for k in (1, 2, 3):
            third(k).wait_recv()
        out[...] += rz[0].astype(F32) + rz[1].astype(F32) + rz[2].astype(F32)
        for k in (1, 2, 3):
            third(k).wait_send()
        for i, k in enumerate((2, 1, 3, 0)):
            for c in first(i, k) + second(i):
                c.wait_send()

    for i, k in enumerate((2, 1, 3, 0)):
        plan.at(t0 + max(0, i - AHEAD + 0.71) * tx if i >= AHEAD else t0 + 0.01 * i, functools.partial(start, i, k))
        plan.at(t0 + i * tx + 0.7 * tx, functools.partial(middle, i, k))
        plan.at(t0 + i * tx + 1.35 * tx, functools.partial(total, i, k))
    plan.at(t0 + 5 * tx, last)


DEAL_SEMS = [DMA((16,))] * 4 + [DMA]


def deal16(plan, h, piece, put, passed, sems, t0, t1, both=True):
    ss, sr, fs, fr, own = sems

    def send(step):
        to = jnp.bitwise_xor(h.me, step)
        return remote(piece(to), put(h.me), ss.at[step], sr.at[step], ctx=to)

    def got(step):
        at = jnp.bitwise_xor(h.me, step)
        return remote(put(at), put(at), ss.at[step], sr.at[step], ctx=at)

    def hand(step):
        at = jnp.bitwise_xor(h.me, step)
        return remote(put(at) if step else piece(h.me), passed(at, h.core), fs.at[step], fr.at[step], fsdp=1 - h.core)

    def taken(step):
        at = jnp.bitwise_xor(h.me, step)
        return remote(passed(at, 1 - h.core), passed(at, 1 - h.core), fs.at[step], fr.at[step], fsdp=1 - h.core)

    local = pltpu.make_async_copy(piece(h.me), put(h.me), own)

    def first():
        for step in ORDER:
            send(step).start()
        local.start()
        if both:
            hand(0).start()

    plan.at(t0, first)
    for i, step in enumerate(ORDER):

        def relay(step=step):
            got(step).wait_recv()
            if both:
                hand(step).start()

        plan.at(t0 + (t1 - t0) * (i + 1) / 15, relay)

    def drain():
        if both:
            for step in range(16):
                taken(step).wait_recv()
                hand(step).wait_send()
        for step in ORDER:
            send(step).wait_send()
        local.wait()

    plan.at(t1 + 2, drain)


ORDER = (1, 2, 3, 4, 5, 6, 7, 8, 9, 10, 11, 12, 13, 14, 15)

ROWS = 256


def _tri():
    i = lax.broadcasted_iota(jnp.int32, (ROWS, ROWS), 0)
    j = lax.broadcasted_iota(jnp.int32, (ROWS, ROWS), 1)
    return i <= j


def _heads(value):
    lane = lax.broadcasted_iota(jnp.int32, value.shape, 1)
    zero = jnp.zeros_like(value)
    return jnp.where(lane < 64, value, zero), jnp.where(lane >= 64, value, zero)


def _nt(a, b):
    return lax.dot_general(a, b, (((1,), (1,)), ((), ())), preferred_element_type=F32)


def _tn(a, b):
    return lax.dot_general(a, b, (((0,), (0,)), ((), ())), preferred_element_type=F32)


def _nn(a, b):
    return jnp.dot(a, b, preferred_element_type=F32)


def _scores(keys, query, tri):
    scores = _nt(keys, query)
    n = keys.shape[0]
    low = jnp.where(tri, scores[n - ROWS :], -1e30)
    return low if n == ROWS else jnp.concatenate([scores[: n - ROWS], low], 0)


def sort_rows(order_ref, src, dst, blk=64):
    for b in range(src.shape[0] // blk):
        at = pl.multiple_of(order_ref[b] * blk, blk)
        dst[b * blk : (b + 1) * blk, :] = src[pl.ds(at, blk), :]


def attend(qs, ks, vs, os, lse):
    tri = _tri()
    for i in range(qs.shape[0] // ROWS):
        n = (i + 1) * ROWS
        mine = slice(i * ROWS, n)
        total = None
        for head, query in enumerate(_heads(qs[mine, :] * BF(0.125))):
            scores = _scores(ks[:n, :], query, tri)
            top = jnp.max(scores, 0, keepdims=True)
            raw = jnp.exp(scores - top)
            size = jnp.sum(raw, 0, keepdims=True)
            lse[head : head + 1, mine] = top + jnp.log(size)
            probs = (raw * (1.0 / size)).astype(BF)
            part = _tn(probs, _heads(vs[:n, :])[head])
            total = part if total is None else total + part
        os[mine, :] = total.astype(BF)


def attend_back(qs, ks, vs, gs, lse, dq, dk, dv):
    tri = _tri()
    dk[...] = jnp.zeros_like(dk)
    dv[...] = jnp.zeros_like(dv)
    for i in range(qs.shape[0] // ROWS):
        n = (i + 1) * ROWS
        mine = slice(i * ROWS, n)
        total = None
        queries = _heads(qs[mine, :] * BF(0.125))
        grads = _heads(gs[mine, :])
        for head in range(2):
            scores = _scores(ks[:n, :], queries[head], tri)
            probs = jnp.exp(scores - lse[head : head + 1, mine])
            gp = _nt(vs[:n, :], grads[head])
            delta = jnp.sum(probs * gp, 0, keepdims=True)
            ds = (probs * (gp - delta)).astype(BF)
            dv[:n, :] += _nn(probs.astype(BF), grads[head])
            dk[:n, :] += _nn(ds, queries[head])
            part = _tn(ds, _heads(ks[:n, :])[head])
            total = part if total is None else total + part
        dq[mine, :] = total * 0.125


def fwd_kernel(order, table, q, k, v, o, lse, qs, ks, vs, os):
    for a, b in ((q, qs), (k, ks), (v, vs)):
        sort_rows(order, a, b)
    attend(qs, ks, vs, os, lse)
    sort_rows(table, os, o)


def bwd_kernel(order, table, qs, ks, vs, g, lse, dq, dk, dv, gs, dqs, dks, dvs):
    sort_rows(order, g, gs)
    attend_back(qs, ks, vs, gs, lse, dqs, dks, dvs)
    for a, b in ((dqs, dq), (dks, dk), (dvs, dv)):
        sort_rows(table, a, b)


def attention(order, table, q, k, v):
    n = q.shape[0]
    rows = jax.ShapeDtypeStruct((n, 128), BF)
    return pl.pallas_call(
        fwd_kernel,
        out_shape=(rows, jax.ShapeDtypeStruct((2, n), F32), rows, rows, rows),
        grid_spec=pltpu.PrefetchScalarGridSpec(
            num_scalar_prefetch=2, grid=(),
            in_specs=[pl.BlockSpec(memory_space=pltpu.VMEM)] * 3,
            out_specs=[pl.BlockSpec(memory_space=pltpu.VMEM)] * 5,
            scratch_shapes=[pltpu.VMEM((n, 128), BF)],
        ),
        compiler_params=pltpu.CompilerParams(vmem_limit_bytes=48 << 20),
        name="attention",
    )(order, table, q, k, v)


def attention_back(order, table, qs, ks, vs, g, lse):
    n = qs.shape[0]
    rows = jax.ShapeDtypeStruct((n, 128), F32)
    return pl.pallas_call(
        bwd_kernel,
        out_shape=(rows, rows, rows),
        grid_spec=pltpu.PrefetchScalarGridSpec(
            num_scalar_prefetch=2, grid=(),
            in_specs=[pl.BlockSpec(memory_space=pltpu.VMEM)] * 5,
            out_specs=[pl.BlockSpec(memory_space=pltpu.VMEM)] * 3,
            scratch_shapes=[pltpu.VMEM((n, 128), BF)] + [pltpu.VMEM((n, 128), F32)] * 3,
        ),
        compiler_params=pltpu.CompilerParams(vmem_limit_bytes=48 << 20),
        name="attention_back",
    )(order, table, qs, ks, vs, g, lse)


from jax.sharding import PartitionSpec as P

HEADS = 32
HD = 64
EPSILON = 1e-05
THETA_BASE = 130000.0
ANY = pl.BlockSpec(memory_space=pl.ANY)
INNER = pl.BlockSpec(memory_space=pltpu.VMEM)


def comm_call(kernel, outs, out_specs, in_specs, scratch, cid, name, vmem=40):
    return pl.pallas_call(
        kernel,
        out_shape=outs,
        in_specs=in_specs,
        out_specs=out_specs,
        scratch_shapes=scratch,
        compiler_params=pltpu.CompilerParams(
            collective_id=cid, has_side_effects=True, vmem_limit_bytes=vmem << 20
        ),
        name=name,
    )


def take(refs, n):
    head, refs[:] = refs[:n], refs[n:]
    return head


def columns(src, width):
    return lambda c: src.at[:, pl.ds(pl.multiple_of(c * width, 128), width)]


def deal_columns(plan, h, src, out, sems, t0, t1):
    deal16(
        plan, h, columns(src, out.shape[3]), lambda c: out.at[c, h.core], lambda c, core: out.at[c, core], sems, t0, t1
    )


def entry_kernel(x, wq, wk, wv, gains, xg, q_out, k_out, v_out, g_out, *refs):
    refs = list(refs)
    h = Here()
    greet_all(h)
    plan = Plan()
    for src, out in ((wq, q_out), (wk, k_out), (wv, v_out)):
        deal_columns(plan, h, src, out, take(refs, 5), 0, 20)
    deal16(
        plan, h, lambda c: gains, lambda c: g_out.at[c, h.core], lambda c, core: g_out.at[c, core], take(refs, 5), 0, 21
    )
    gather16(plan, h, x, xg, take(refs, 13), 0, 14, 20)
    plan.run()


def entry(x, wq, wk, wv, gains):
    rows, width = x.shape
    block = (16, 2, wq.shape[0], width // 16)
    outs = (
        jax.ShapeDtypeStruct((16, rows, width), BF),
        *[jax.ShapeDtypeStruct(block, BF)] * 3,
        jax.ShapeDtypeStruct((16, 2) + gains.shape, BF),
    )
    return comm_call(entry_kernel, outs, [ANY] * 5, [ANY] * 5, DEAL_SEMS * 4 + GATHER_SEMS, 0, "entry")(
        x, wq, wk, wv, gains
    )


def weights_kernel(wg, wu, wd, wo, cot, g_out, u_out, d_out, o_out, c_out, *refs):
    refs = list(refs)
    h = Here()
    greet_all(h)
    plan = Plan()
    for src, out in ((wg, g_out), (wu, u_out), (wd, d_out)):
        deal_columns(plan, h, src, out, take(refs, 5), 0, 100)
    gather16(plan, h, wo, o_out.at[:, h.core], take(refs, 13), 0, 14, 18)
    gather16(plan, h, cot, c_out, take(refs, 13), 10, 20, 28)
    send, recv = take(refs, 2)
    mine, other = o_out.at[:, h.core], o_out.at[:, 1 - h.core]
    across = remote(mine, mine, send, recv, fsdp=1 - h.core)
    plan.at(105, across.start)

    def end():
        remote(other, other, send, recv, fsdp=1 - h.core).wait_recv()
        across.wait_send()

    plan.at(200, end)
    plan.run()


def weights(wg, wu, wd, wo, cot):
    rows, width = cot.shape
    block = (16, 2, wg.shape[0], wg.shape[1] // 16)
    outs = (
        *[jax.ShapeDtypeStruct(block, BF)] * 3,
        jax.ShapeDtypeStruct((16, 2) + wo.shape, BF),
        jax.ShapeDtypeStruct((16, rows, width), BF),
    )
    return comm_call(
        weights_kernel, outs, [ANY] * 5, [ANY] * 5, DEAL_SEMS * 3 + GATHER_SEMS * 2 + [DMA, DMA], 1, "weights"
    )(wg, wu, wd, wo, cot)


def to_tokens_kernel(src, out, *sems):
    h = Here()
    greet_all(h)
    plan = Plan()
    deal16(plan, h, lambda c: src.at[c], columns_of(out, 128), None, sems, 0, 8, both=False)
    plan.run()


def columns_of(out, width):
    return lambda c: out.at[:, pl.ds(pl.multiple_of(c * width, 128), width)]


def to_tokens(src):
    ctx, rows, width = src.shape
    outs = jax.ShapeDtypeStruct((rows, ctx * width), BF)
    return comm_call(to_tokens_kernel, outs, ANY, [ANY], DEAL_SEMS, 2, "to_tokens")(src)


def to_heads_kernel(src, out, *sems):
    h = Here()
    greet_all(h)
    plan = Plan()
    deal16(plan, h, columns(src, out.shape[2]), lambda c: out.at[c], None, sems, 0, 8, both=False)
    plan.run()


def to_heads(src):
    rows, width = src.shape
    outs = jax.ShapeDtypeStruct((16, rows, width // 16), BF)
    return comm_call(to_heads_kernel, outs, ANY, [ANY], DEAL_SEMS, 3, "to_heads")(src)


def gather_kernel(src, out, *sems):
    h = Here()
    greet_all(h)
    plan = Plan()
    gather16(plan, h, src, out, sems, 0, 12, 17)
    plan.run()


def gather(src):
    outs = jax.ShapeDtypeStruct((16,) + src.shape, BF)
    return comm_call(gather_kernel, outs, ANY, [ANY], GATHER_SEMS, 4, "gather")(src)


def scatter_kernel(part, out, *scratch):
    h = Here()
    greet_all(h)
    plan = Plan()
    scatter16(plan, h, part, out, scratch, 0, 17)
    plan.run()


def scatter(part, cid):
    rows, width = part.shape[0] // 16, part.shape[1]
    outs = jax.ShapeDtypeStruct((rows, width), F32)
    return comm_call(
        scatter_kernel, outs, INNER, [INNER], scatter_scratch(rows, width), cid, f"scatter{cid}", 48
    )(part.reshape(4, 2, 2, rows, width))


def core_sum(plan, h, part, got, total, sems, t0, t1):
    send, recv = sems
    across = remote(part.at[:, 1 - h.core], got, send, recv, fsdp=1 - h.core)
    plan.at(t0, across.start)

    def add():
        remote(part.at[:, h.core], got, send, recv, fsdp=1 - h.core).wait_recv()
        for c in range(16):
            total[c] = (part[c, h.core].astype(F32) + got[c].astype(F32)).astype(BF)
        across.wait_send()

    plan.at(t1, add)


def home_kernel(*refs):
    refs = list(refs)
    parts, gains = take(refs, 6), take(refs, 1)[0]
    outs, gains_out = take(refs, 6), take(refs, 1)[0]
    h = Here()
    greet_all(h)
    plan = Plan()
    for i, (part, out) in enumerate(zip(parts, outs)):
        got, total = take(refs, 2)
        core_sum(plan, h, part, got, total, take(refs, 2), 0.1 * i, 2 * i + 1)
        deal16(
            plan, h, lambda c, t=total: t.at[c], columns_of(out, part.shape[3]), None, take(refs, 5), 2 * i + 1.5, 90 + i,
            both=False,
        )
    deal16(plan, h, lambda c: gains.at[c], lambda c: gains_out.at[c], None, take(refs, 5), 0, 20, both=False)
    plan.run()


def home(parts, gains):
    scratch = []
    for p in parts:
        buffer = pltpu.VMEM((p.shape[0],) + p.shape[2:], BF)
        scratch += [buffer, buffer, DMA, DMA] + DEAL_SEMS
    outs = [jax.ShapeDtypeStruct((p.shape[2], 16 * p.shape[3]), BF) for p in parts]
    outs.append(jax.ShapeDtypeStruct(gains.shape, F32))
    return comm_call(
        home_kernel, tuple(outs), [ANY] * 7, [INNER] * 7, scratch + DEAL_SEMS, 6, "home", 52
    )(*parts, gains)


def out_home_kernel(part, out, got, total, s, r, *scratch):
    h = Here()
    greet_all(h)
    plan = Plan()
    core_sum(plan, h, part, got, total, (s, r), 0, 1)
    plan.run()
    plan = Plan()
    view = total.reshape(4, 2, 2, *total.shape[1:])
    scatter16(plan, h, view, out, scratch, 2, 9)
    plan.run()


def out_home(part):
    ctx, _, rows, width = part.shape
    buffer = pltpu.VMEM((ctx, rows, width), BF)
    outs = jax.ShapeDtypeStruct((rows, width), F32)
    return comm_call(
        out_home_kernel, outs, INNER, [INNER], [buffer, buffer, DMA, DMA] + scatter_scratch(rows, width), 7, "out_home", 48
    )(part)


def rope_tables(positions):
    inv_freq = THETA_BASE ** (-(jnp.arange(HD // 2, dtype=F32) * 2.0 / HD))
    angles = positions.astype(F32)[:, None] * inv_freq[None, :]
    return jnp.tile(jnp.cos(angles), (1, 4)), jnp.tile(jnp.sin(angles), (1, 4))


def swap(values):
    a, b, c, d = jnp.split(values, 4, -1)
    return jnp.concatenate([b, a, d, c], -1)


def fast_body(x, table, attn_gain, wq, wk, wv, wo, mlp_gain, wg, wu, wd, cot):
    x, cot, table = x[0], cot[0], table[0].reshape(32)
    rows, width = x.shape
    length = rows * 16
    core = lax.axis_index("fsdp")
    gains = jnp.pad(jnp.concatenate([attn_gain, mlp_gain])[None], ((0, 15), (0, 0)))
    xg, bq, bk, bv, gains = entry(x, wq, wk, wv, gains)
    gains = gains[:, :, 0].reshape(32, 2, 64).astype(F32)
    again, mgain = gains[:, 0].reshape(width), gains[:, 1].reshape(width)
    slots = jnp.arange(32, dtype=jnp.int32)
    order = jnp.sum(jnp.where(table[None, :] == slots[:, None], slots[None, :], 0), 1)
    positions = (table[:, None] * 64 + jnp.arange(64, dtype=jnp.int32)[None]).reshape(length)
    cos, sin = rope_tables(positions)
    turn = jnp.where(jnp.arange(128) % 64 < 32, -1.0, 1.0).astype(F32)
    sin = sin * turn

    source = xg.reshape(length, width).astype(F32)
    inv_all = lax.rsqrt(jnp.mean(source * source, -1, keepdims=True) + EPSILON)
    normed = (source * inv_all * again).astype(BF)
    bq, bk, bv = (b.reshape(width, 128) for b in (bq, bk, bv))

    def dot(a, b):
        return jnp.dot(a, b, preferred_element_type=F32)

    def dot_nt(a, b):
        return lax.dot_general(a, b, (((1,), (1,)), ((), ())), preferred_element_type=F32)

    def dot_tn(a, b):
        return lax.dot_general(a, b, (((0,), (0,)), ((), ())), preferred_element_type=F32)

    qkv = dot(normed, jnp.concatenate([bq, bk, bv], 1))
    q, k, v = qkv[:, :128], qkv[:, 128:256], qkv[:, 256:].astype(BF)
    q = (q * cos + swap(q) * sin).astype(BF)
    k = (k * cos + swap(k) * sin).astype(BF)
    o, lse, qs, ks, vs = attention(order, table, q, k, v)
    bg, bu, bd, full_out, cot_all = weights(wg, wu, wd, wo, cot)
    full_out = full_out.reshape(width, width)
    bg, bu, bd = (b.reshape(width, b.shape[3]) for b in (bg, bu, bd))
    cot_all = cot_all.reshape(length, width)
    attn_low = to_tokens(o.reshape(16, rows, 128))
    own = x.astype(F32)
    inv_in = lax.rsqrt(jnp.mean(own * own, -1, keepdims=True) + EPSILON)
    hidden = own + dot(attn_low, full_out)
    inv_mid = lax.rsqrt(jnp.mean(hidden * hidden, -1, keepdims=True) + EPSILON)
    mlp_in = gather((hidden * inv_mid * mgain).astype(BF)).reshape(length, width)
    gate, up = dot(mlp_in, bg), dot(mlp_in, bu)
    sig = jax.nn.sigmoid(gate)
    act = (gate * sig * up).astype(BF)
    out_part = dot_nt(act, bd).astype(BF)
    grad_act = dot(cot_all, bd)
    grad_gate = (grad_act * up * sig * (1.0 + gate * (1.0 - sig))).astype(BF)
    grad_up = (grad_act * gate * sig).astype(BF)
    gmi_part = (dot_nt(grad_gate, bg) + dot_nt(grad_up, bu)).astype(BF)
    gmi = scatter(gmi_part, 5)
    layer_output = (hidden + scatter(out_part, 8)).astype(BF)

    def norm_back(grad, source, inv, gain):
        scaled = grad * gain
        inner = jnp.sum(scaled * source, -1, keepdims=True)
        return inv * scaled - inv * inv * inv / width * source * inner

    mgain_part = jnp.sum(gmi * hidden * inv_mid, 0)
    grad_hidden = cot.astype(F32) + norm_back(gmi, hidden, inv_mid, mgain)
    grad_branch = grad_hidden.astype(BF)
    grad_att = to_heads(dot_nt(grad_branch, full_out).astype(BF)).reshape(length, 128)
    dq, dk, dv = attention_back(order, table, qs, ks, vs, grad_att, lse)
    dq = (dq * cos - swap(dq) * sin).astype(BF)
    dk = (dk * cos - swap(dk) * sin).astype(BF)
    grad_qkv = jnp.concatenate([dq, dk, dv.astype(BF)], 1)
    gn_part = dot_nt(grad_qkv, jnp.concatenate([bq, bk, bv], 1)).astype(BF)
    gn = scatter(gn_part, 9)
    input_grad = grad_hidden + norm_back(gn, own, inv_in, again)
    again_part = jnp.sum(gn * own * inv_in, 0)
    gains = jnp.stack([again_part, mgain_part]).reshape(2, 16, 128).transpose(1, 0, 2)
    gains = jnp.pad(gains, ((0, 0), (0, 6), (0, 0)))

    def pieces(grad):
        return grad.astype(BF).reshape(16, 2, 64, grad.shape[1])

    wo_grad = out_home(pieces(dot_tn(attn_low, grad_branch)))
    parts = [
        pieces(dot_tn(normed, dq)),
        pieces(dot_tn(normed, dk)),
        pieces(dot_tn(normed, dv.astype(BF))),
        pieces(dot_tn(mlp_in, grad_gate)),
        pieces(dot_tn(mlp_in, grad_up)),
        pieces(dot_tn(cot_all, act)),
    ]
    *grads, gains = home(parts, gains)
    gq, gk, gv, gg, gu, gd = (g.astype(F32) for g in grads)
    gains = lax.psum(jnp.sum(gains, 0), "fsdp")
    gains = lax.dynamic_slice_in_dim(gains, core * 64, 64, 1)
    return (layer_output[None], input_grad[None], gains[0], gq, gk, gv, wo_grad, gains[1], gg, gu, gd)


MASKED = -1e30


def general_tables(positions):
    inv_freq = THETA_BASE ** (-(jnp.arange(HD // 2, dtype=jnp.float32) * 2.0 / HD))
    angles = positions.astype(jnp.float32)[:, None] * inv_freq[None, :]
    cosine = jnp.cos(angles)
    sine_tab = jnp.sin(angles)
    return (jnp.concatenate([cosine, cosine], -1), jnp.concatenate([sine_tab, sine_tab], -1))


def rotate(values, cosine, sine_tab):
    middle = values.shape[-1] // 2
    turned = jnp.concatenate([-values[..., middle:], values[..., :middle]], -1)
    return values * cosine[:, None, :] + turned * sine_tab[:, None, :]


def rotate_back(grads_in, cosine, sine_tab):
    middle = grads_in.shape[-1] // 2
    shifted = grads_in * sine_tab[:, None, :]
    turned = jnp.concatenate([shifted[..., middle:], -shifted[..., :middle]], -1)
    return grads_in * cosine[:, None, :] + turned


def inverse_rms(rows_in):
    return lax.rsqrt(jnp.mean(rows_in * rows_in, -1, keepdims=True) + EPSILON)


def general_norm_back(grad_normed, rows_in, inverse, gain_vec):
    scaled = grad_normed * gain_vec
    inner_sum = jnp.sum(scaled * rows_in, -1, keepdims=True)
    return inverse * scaled - inverse * inverse * inverse / rows_in.shape[-1] * rows_in * inner_sum


def score_rows(query_rows, key_rows, query_pos, key_pos):
    scores = jnp.einsum(
        "qhd,khd->hqk", query_rows, key_rows, preferred_element_type=jnp.float32
    ) * HD ** (-0.5)
    visible = key_pos[None, None, :] <= query_pos[None, :, None]
    return (scores, visible)


def softmax_rows(scores, visible, log_total):
    return jnp.where(
        visible, jnp.exp(jnp.where(visible, scores - log_total[..., None], MASKED)), 0.0
    )


def walk_keys(kv_steps, top_pos, width, step_fn, initial):
    step_rows = kv_steps.shape[1]
    offsets = jnp.arange(step_rows, dtype=jnp.int32)

    def advance(carried, step_item):
        step_index, kv_block = step_item
        first_key = step_index * step_rows
        key_rows = kv_block[:, :width].reshape(step_rows, HEADS, HD)
        value_rows = kv_block[:, width:].reshape(step_rows, HEADS, HD)
        key_pos = first_key + offsets
        updated = lax.cond(
            first_key <= top_pos,
            lambda state: step_fn(state, key_rows, value_rows, key_pos),
            lambda state: state,
            carried,
        )
        return (updated, None)

    indices = jnp.arange(kv_steps.shape[0], dtype=jnp.int32)
    final_state, ignored = lax.scan(advance, initial, (indices, kv_steps))
    return final_state


def general_body(
    layer_input,
    block_table,
    attn_gain,
    query_weight,
    key_weight,
    value_weight,
    out_weight,
    mlp_gain,
    gate_weight,
    up_weight,
    down_weight,
    cotangent,
):
    tokens = layer_input.shape[1]
    width = layer_input.shape[2]
    half_rows = tokens // 2
    ranks = lax.axis_size("ctx")
    length = tokens * ranks
    score_scale = HD ** (-0.5)
    block_ids = block_table[0].reshape(2 * ranks)
    own_blocks = lax.dynamic_slice_in_dim(block_ids, lax.axis_index("ctx") * 2, 2)
    inner = jnp.arange(half_rows, dtype=jnp.int32)
    query_pos = (own_blocks[:, None] * half_rows + inner[None, :]).reshape(tokens)
    cosine, sine_tab = general_tables(query_pos)
    full_query, full_key, full_value, full_out, full_attn_gain = (
        lax.all_gather(query_weight, ("ctx", "fsdp"), axis=0, tiled=True),
        lax.all_gather(key_weight, ("ctx", "fsdp"), axis=0, tiled=True),
        lax.all_gather(value_weight, ("ctx", "fsdp"), axis=0, tiled=True),
        lax.all_gather(out_weight, ("ctx", "fsdp"), axis=0, tiled=True),
        lax.all_gather(attn_gain, ("ctx", "fsdp"), axis=0, tiled=True),
    )
    source = layer_input[0].astype(jnp.float32)
    inverse_in = inverse_rms(source)
    normed = (source * inverse_in * full_attn_gain.astype(jnp.float32)).astype(jnp.bfloat16)
    query_pre = jnp.dot(normed, full_query, preferred_element_type=jnp.float32).reshape(
        tokens, HEADS, HD
    )
    key_pre = jnp.dot(normed, full_key, preferred_element_type=jnp.float32).reshape(
        tokens, HEADS, HD
    )
    value_low = jnp.dot(normed, full_value, preferred_element_type=jnp.float32).astype(jnp.bfloat16)
    queries = rotate(query_pre, cosine, sine_tab).astype(jnp.bfloat16)
    keys_low = rotate(key_pre, cosine, sine_tab).astype(jnp.bfloat16).reshape(tokens, width)
    kv_dev = lax.all_gather(jnp.concatenate([keys_low, value_low], 1), "ctx", axis=0, tiled=True)
    slot_ids = jnp.arange(2 * ranks, dtype=jnp.int32)
    holder = jnp.sum(jnp.where(block_ids[None, :] == slot_ids[:, None], slot_ids[None, :], 0), 1)
    chosen = (holder[:, None] == slot_ids[None, :]).astype(jnp.bfloat16)
    kv_seq = jnp.einsum(
        "ab,bn->an", chosen, kv_dev.reshape(2 * ranks, half_rows * 2 * width)
    ).reshape(length, 2 * width)
    step_rows = min(512, length)
    kv_steps = kv_seq.reshape(length // step_rows, step_rows, 2 * width)
    log_totals = []
    attended_parts = []
    top_list = []
    for slot_index in range(2):
        slot_queries = queries[slot_index * half_rows : (slot_index + 1) * half_rows]
        slot_pos = query_pos[slot_index * half_rows : (slot_index + 1) * half_rows]
        top_pos = own_blocks[slot_index] * half_rows + half_rows - 1
        top_list.append(top_pos)

        def stat_step(state, key_rows, value_rows, key_pos):
            running, running_sum = state
            scores, visible = score_rows(slot_queries, key_rows, slot_pos, key_pos)
            scores = jnp.where(visible, scores, MASKED)
            newest = jnp.maximum(running, jnp.max(scores, -1))
            running_sum = running_sum * jnp.exp(running - newest) + jnp.sum(
                jnp.where(visible, jnp.exp(scores - newest[..., None]), 0.0), -1
            )
            return (newest, running_sum)

        start_state = (
            jnp.full((HEADS, half_rows), MASKED, jnp.float32),
            jnp.zeros((HEADS, half_rows), jnp.float32),
        )
        running, running_sum = walk_keys(kv_steps, top_pos, width, stat_step, start_state)
        log_total = running + jnp.log(running_sum)

        def value_step(accumulated, key_rows, value_rows, key_pos):
            scores, visible = score_rows(slot_queries, key_rows, slot_pos, key_pos)
            weights_low = softmax_rows(scores, visible, log_total).astype(jnp.bfloat16)
            return accumulated + jnp.einsum(
                "hqk,khd->qhd", weights_low, value_rows, preferred_element_type=jnp.float32
            )

        attended_parts.append(
            walk_keys(
                kv_steps, top_pos, width, value_step, jnp.zeros((half_rows, HEADS, HD), jnp.float32)
            )
        )
        log_totals.append(log_total)
    attended = jnp.concatenate(attended_parts, 0)
    log_all = jnp.concatenate(log_totals, 1)
    attn_low = attended.reshape(tokens, width).astype(jnp.bfloat16)
    hidden = source + jnp.dot(attn_low, full_out, preferred_element_type=jnp.float32)
    full_gate, full_up, full_down, full_mlp_gain = (
        lax.all_gather(gate_weight, ("ctx", "fsdp"), axis=0, tiled=True),
        lax.all_gather(up_weight, ("ctx", "fsdp"), axis=0, tiled=True),
        lax.all_gather(down_weight, ("ctx", "fsdp"), axis=0, tiled=True),
        lax.all_gather(mlp_gain, ("ctx", "fsdp"), axis=0, tiled=True),
    )
    inverse_mid = inverse_rms(hidden)
    mlp_in = (hidden * inverse_mid * full_mlp_gain.astype(jnp.float32)).astype(jnp.bfloat16)
    gate_pre = jnp.dot(mlp_in, full_gate, preferred_element_type=jnp.float32)
    up_pre = jnp.dot(mlp_in, full_up, preferred_element_type=jnp.float32)
    activation = (jax.nn.silu(gate_pre) * up_pre).astype(jnp.bfloat16)
    branch_mlp = jnp.einsum("tf,df->td", activation, full_down, preferred_element_type=jnp.float32)
    layer_output = (hidden + branch_mlp).astype(jnp.bfloat16)
    back_gate, back_up, back_down, back_mlp_gain = (
        lax.all_gather(gate_weight, ("ctx", "fsdp"), axis=0, tiled=True),
        lax.all_gather(up_weight, ("ctx", "fsdp"), axis=0, tiled=True),
        lax.all_gather(down_weight, ("ctx", "fsdp"), axis=0, tiled=True),
        lax.all_gather(mlp_gain, ("ctx", "fsdp"), axis=0, tiled=True),
    )
    grad_out_low = cotangent[0]
    grad_act = jnp.dot(grad_out_low, back_down, preferred_element_type=jnp.float32)
    sigmoid_gate = jax.nn.sigmoid(gate_pre)
    grad_gate = (grad_act * up_pre * sigmoid_gate * (1.0 + gate_pre * (1.0 - sigmoid_gate))).astype(
        jnp.bfloat16
    )
    grad_up = (grad_act * gate_pre * sigmoid_gate).astype(jnp.bfloat16)
    grad_mlp_in = jnp.einsum(
        "tf,df->td", grad_gate, back_gate, preferred_element_type=jnp.float32
    ) + jnp.einsum("tf,df->td", grad_up, back_up, preferred_element_type=jnp.float32)
    mlp_gain_term = jnp.sum(grad_mlp_in * hidden * inverse_mid, 0)
    grad_hidden = grad_out_low.astype(jnp.float32) + general_norm_back(
        grad_mlp_in, hidden, inverse_mid, back_mlp_gain.astype(jnp.float32)
    )
    grad_branch = grad_hidden.astype(jnp.bfloat16)
    back_query, back_key, back_value, back_out, back_attn_gain = (
        lax.all_gather(query_weight, ("ctx", "fsdp"), axis=0, tiled=True),
        lax.all_gather(key_weight, ("ctx", "fsdp"), axis=0, tiled=True),
        lax.all_gather(value_weight, ("ctx", "fsdp"), axis=0, tiled=True),
        lax.all_gather(out_weight, ("ctx", "fsdp"), axis=0, tiled=True),
        lax.all_gather(attn_gain, ("ctx", "fsdp"), axis=0, tiled=True),
    )
    grad_attended = (
        jnp.einsum("te,de->td", grad_branch, back_out, preferred_element_type=jnp.float32)
        .astype(jnp.bfloat16)
        .reshape(tokens, HEADS, HD)
    )
    delta_all = jnp.sum(grad_attended.astype(jnp.float32) * attended, -1).T
    grad_query_parts = []
    for slot_index in range(2):
        slot_queries = queries[slot_index * half_rows : (slot_index + 1) * half_rows]
        slot_pos = query_pos[slot_index * half_rows : (slot_index + 1) * half_rows]
        slot_grad_out = grad_attended[slot_index * half_rows : (slot_index + 1) * half_rows]
        slot_delta = delta_all[:, slot_index * half_rows : (slot_index + 1) * half_rows]
        slot_log = log_totals[slot_index]

        def query_step(accumulated, key_rows, value_rows, key_pos):
            scores, visible = score_rows(slot_queries, key_rows, slot_pos, key_pos)
            weights_full = softmax_rows(scores, visible, slot_log)
            grad_weights = jnp.einsum(
                "qhd,khd->hqk", slot_grad_out, value_rows, preferred_element_type=jnp.float32
            )
            grad_scores = (weights_full * (grad_weights - slot_delta[..., None])).astype(
                jnp.bfloat16
            )
            return accumulated + jnp.einsum(
                "hqk,khd->qhd", grad_scores, key_rows, preferred_element_type=jnp.float32
            )

        grad_query_parts.append(
            walk_keys(
                kv_steps,
                top_list[slot_index],
                width,
                query_step,
                jnp.zeros((half_rows, HEADS, HD), jnp.float32),
            )
        )
    grad_queries = jnp.concatenate(grad_query_parts, 0) * score_scale
    grad_query_low = (
        rotate_back(grad_queries, cosine, sine_tab).reshape(tokens, width).astype(jnp.bfloat16)
    )
    bottom_key = jnp.min(query_pos)
    query_both = lax.all_gather(
        jnp.concatenate([queries.reshape(tokens, width), grad_attended.reshape(tokens, width)], 1),
        "ctx",
        axis=0,
        tiled=True,
    )
    stats_both = lax.all_gather(
        jnp.stack([log_all.T, delta_all.T], 1).astype(jnp.bfloat16), "ctx", axis=0, tiled=True
    ).astype(jnp.float32)
    all_pos = (block_ids[:, None] * half_rows + inner[None, :]).reshape(length)
    own_keys = keys_low.reshape(tokens, HEADS, HD)
    own_values = value_low.reshape(tokens, HEADS, HD)

    def gather_step(carried, piece_index):
        first = piece_index * step_rows
        piece_pos = lax.dynamic_slice_in_dim(all_pos, first, step_rows)

        def live_piece(state):
            rows_here = lax.dynamic_slice_in_dim(query_both, first, step_rows, 0)
            stats_here = lax.dynamic_slice_in_dim(stats_both, first, step_rows, 0)
            piece_queries = rows_here[:, :width].reshape(step_rows, HEADS, HD)
            piece_grads = rows_here[:, width:].reshape(step_rows, HEADS, HD)
            piece_log = stats_here[:, 0, :].T
            piece_delta = stats_here[:, 1, :].T
            scores, visible = score_rows(piece_queries, own_keys, piece_pos, query_pos)
            weights_full = softmax_rows(scores, visible, piece_log)
            grad_weights = jnp.einsum(
                "qhd,khd->hqk", piece_grads, own_values, preferred_element_type=jnp.float32
            )
            grad_scores = (weights_full * (grad_weights - piece_delta[..., None])).astype(
                jnp.bfloat16
            )
            grad_keys = (
                jnp.einsum(
                    "hqk,qhd->khd", grad_scores, piece_queries, preferred_element_type=jnp.float32
                )
                * score_scale
            )
            grad_values = jnp.einsum(
                "hqk,qhd->khd",
                weights_full.astype(jnp.bfloat16),
                piece_grads,
                preferred_element_type=jnp.float32,
            )
            return (state[0] + grad_keys, state[1] + grad_values)

        updated = lax.cond(
            jnp.max(piece_pos) >= bottom_key, live_piece, lambda state: state, carried
        )
        return (updated, None)

    start_grads = (
        jnp.zeros((tokens, HEADS, HD), jnp.float32),
        jnp.zeros((tokens, HEADS, HD), jnp.float32),
    )
    summed, ignored = lax.scan(
        gather_step, start_grads, jnp.arange(length // step_rows, dtype=jnp.int32)
    )
    kv_grads = jnp.concatenate(
        [summed[0].reshape(tokens, width), summed[1].reshape(tokens, width)], 1
    )
    grad_key_low = (
        rotate_back(kv_grads[:, :width].reshape(tokens, HEADS, HD), cosine, sine_tab)
        .reshape(tokens, width)
        .astype(jnp.bfloat16)
    )
    grad_value_low = kv_grads[:, width:].astype(jnp.bfloat16)
    grad_normed = jnp.einsum(
        "te,de->td", grad_query_low, back_query, preferred_element_type=jnp.float32
    )
    grad_normed = grad_normed + jnp.einsum(
        "te,de->td", grad_key_low, back_key, preferred_element_type=jnp.float32
    )
    grad_normed = grad_normed + jnp.einsum(
        "te,de->td", grad_value_low, back_value, preferred_element_type=jnp.float32
    )
    attn_gain_term = jnp.sum(grad_normed * source * inverse_in, 0)
    input_grad = grad_hidden + general_norm_back(
        grad_normed, source, inverse_in, back_attn_gain.astype(jnp.float32)
    )

    def outer_sum(left_side, right_side):
        return jnp.einsum("tc,te->ce", left_side, right_side, preferred_element_type=jnp.float32)

    weight_grads = lax.psum_scatter(
        jnp.concatenate(
            [
                outer_sum(normed, grad_query_low),
                outer_sum(normed, grad_key_low),
                outer_sum(normed, grad_value_low),
                outer_sum(attn_low, grad_branch),
                outer_sum(mlp_in, grad_gate),
                outer_sum(mlp_in, grad_up),
                outer_sum(grad_out_low, activation),
            ],
            1,
        ),
        ("ctx", "fsdp"),
        scatter_dimension=0,
        tiled=True,
    )
    gain_grads = lax.psum_scatter(
        jnp.stack([attn_gain_term, mlp_gain_term], 1),
        ("ctx", "fsdp"),
        scatter_dimension=0,
        tiled=True,
    )
    hidden_units = gate_weight.shape[1]
    edge_attn = 4 * width
    return (
        layer_output[None],
        input_grad[None],
        gain_grads[:, 0],
        weight_grads[:, 0:width],
        weight_grads[:, width : 2 * width],
        weight_grads[:, 2 * width : 3 * width],
        weight_grads[:, 3 * width : edge_attn],
        gain_grads[:, 1],
        weight_grads[:, edge_attn : edge_attn + hidden_units],
        weight_grads[:, edge_attn + hidden_units : edge_attn + 2 * hidden_units],
        weight_grads[:, edge_attn + 2 * hidden_units : edge_attn + 3 * hidden_units],
    )


def solution(mesh):
    both = ("ctx", "fsdp")
    rows = P(both, None)
    tokens = P("fsdp", "ctx", None)
    return jax.shard_map(
        fast_body if mesh.shape["ctx"] == 16 and mesh.shape["fsdp"] == 2 else general_body,
        mesh=mesh,
        in_specs=(tokens, P("fsdp", None, None), P(both), rows, rows, rows, rows, P(both), rows, rows, rows, tokens),
        out_specs=(tokens, tokens, P(both), rows, rows, rows, rows, P(both), rows, rows, rows),
        check_vma=False,
    )
```

```python
import functools
import jax, jax.numpy as jnp
from jax import lax
from jax.experimental import pallas as pl
from jax.experimental.pallas import tpu as pltpu

MESH = pl.DeviceIdType.MESH
DMA = pltpu.SemaphoreType.DMA
BF = jnp.bfloat16
F32 = jnp.float32


class Plan:
    def __init__(self):
        self.steps = []

    def at(self, when, step):
        self.steps.append((when, len(self.steps), step))

    def run(self):
        for _, _, step in sorted(self.steps, key=lambda s: s[:2]):
            step()


class Here:
    def __init__(self):
        self.me = lax.axis_index("ctx")
        self.core = lax.axis_index("fsdp")
        self.z = self.me // 4
        self.y = lax.rem(self.me // 2, 2)
        self.x = lax.rem(self.me, 2)
        self.xy = lax.rem(self.me, 4)
        self.xn = self.me + 1 - 2 * self.x
        self.yn = self.me + 2 - 4 * self.y


def remote(src, dst, send_sem, recv_sem, **device):
    return pltpu.make_async_remote_copy(
        src_ref=src, dst_ref=dst, send_sem=send_sem, recv_sem=recv_sem, device_id=device, device_id_type=MESH
    )


def greet_all(h):
    barrier = pltpu.get_barrier_semaphore()
    for step in range(1, 16):
        pl.semaphore_signal(barrier, inc=1, device_id={"ctx": jnp.bitwise_xor(h.me, step)}, device_id_type=MESH)
    pl.semaphore_signal(barrier, inc=1, device_id={"fsdp": 1 - h.core}, device_id_type=MESH)
    pl.semaphore_wait(barrier, 16)


GATHER_SEMS = [DMA((4,))] * 12 + [DMA]


def gather16(plan, h, src, out, sems, t0, tz, tx, by_plane=False):
    us, ur, ds, dr, xs, xr, ys, yr, xfs, xfr, yfs, yfr, own = sems
    half = src.shape[0] // 2

    def plane(zz, source=None):
        s = zz * 4 + h.xy
        source = out.at[s] if source is None else source
        return (
            remote(source, out.at[s], xs.at[zz], xr.at[zz], ctx=h.xn),
            remote(source, out.at[s], ys.at[zz], yr.at[zz], ctx=h.yn),
        )

    def across(zz):
        sx = zz * 4 + lax.rem(h.xn, 4)
        sy = zz * 4 + lax.rem(h.yn, 4)
        top, low = pl.ds(0, half), pl.ds(half, half)
        return (
            remote(out.at[sx, top], out.at[sx, top], yfs.at[zz], yfr.at[zz], ctx=h.yn),
            remote(out.at[sy, low], out.at[sy, low], xfs.at[zz], xfr.at[zz], ctx=h.xn),
        )

    def arrived(zz):
        sx = zz * 4 + lax.rem(h.xn, 4)
        sy = zz * 4 + lax.rem(h.yn, 4)
        return (
            remote(out.at[sx], out.at[sx], xs.at[zz], xr.at[zz], ctx=h.xn),
            remote(out.at[sy], out.at[sy], ys.at[zz], yr.at[zz], ctx=h.yn),
        )

    def hop(k, up, source=None):
        it = (h.z - k if up else h.z + k) * 4 + h.xy
        send, recv = (us, ur) if up else (ds, dr)
        source = out.at[it] if source is None else source
        to = h.me + 4 if up else h.me - 4
        return remote(source, out.at[it], send.at[k], recv.at[k + 1], ctx=to)

    def landed(k, up):
        it = (h.z - k if up else h.z + k) * 4 + h.xy
        send, recv = (us, ur) if up else (ds, dr)
        return remote(out.at[it], out.at[it], send.at[k - 1], recv.at[k], ctx=h.me)

    local = pltpu.make_async_copy(src, out.at[h.me], own)

    def first():
        pl.when(h.z < 3)(lambda: hop(0, True, src).start())
        pl.when(h.z > 0)(lambda: hop(0, False, src).start())
        for c in plane(h.z, src):
            c.start()
        local.start()

    plan.at(t0, first)

    def step(k, up):
        def go():
            landed(k, up).wait_recv()
            if k < 3:
                pl.when((h.z < 3) if up else (h.z > 0))(lambda: hop(k, up).start())
            for c in plane(h.z - k if up else h.z + k):
                c.start()

        pl.when((h.z >= k) if up else (h.z + k <= 3))(go)

    def forward(zz):
        got, on = arrived(zz), across(zz)
        for g, c in zip(got, on):
            g.wait_recv()
            c.start()

    def finish(zz):
        sx = zz * 4 + 3 - h.xy
        top, low = pl.ds(0, half), pl.ds(half, half)
        remote(out.at[sx, top], out.at[sx, top], yfs.at[zz], yfr.at[zz], ctx=h.yn).wait_recv()
        remote(out.at[sx, low], out.at[sx, low], xfs.at[zz], xfr.at[zz], ctx=h.xn).wait_recv()

    plan.at(t0 + 0.8 * tx, lambda: forward(h.z))
    for k in (1, 2, 3):
        for up in (True, False):
            valid = (lambda k=k, up=up: (h.z >= k) if up else (h.z + k <= 3))
            plan.at(t0 + k * tz, functools.partial(step, k, up))
            zz = (lambda k=k, up=up: h.z - k if up else h.z + k)
            plan.at(t0 + (k + 0.8) * tx, lambda v=valid, q=zz: pl.when(v())(lambda: forward(q())))

    def drain():
        if not by_plane:
            for zz in range(4):
                finish(zz)
        for k in range(3):
            pl.when((h.z >= k) & (h.z < 3))(lambda: hop(k, True).wait_send())
            pl.when((h.z + k <= 3) & (h.z > 0))(lambda: hop(k, False).wait_send())
        for zz in range(4):
            for c in plane(zz) + across(zz):
                c.wait_send()

    plan.at(t0 + 0.85 * tx, local.wait)
    plan.at(t0 + 4.5 * tx, drain)
    return finish


SCATTER_SEMS = [DMA((4,))] * 8 + [DMA((4,))] * 2


def scatter_scratch(rows, width):
    half = width // 2
    return [
        pltpu.VMEM((4, 2, rows, half), BF),
        pltpu.VMEM((4, 2, rows, half), BF),
        pltpu.VMEM((4, rows, half), BF),
        pltpu.VMEM((4, rows, half), BF),
        pltpu.VMEM((4, rows, half), BF),
        pltpu.VMEM((4, rows, half), BF),
        pltpu.VMEM((3, rows, width), BF),
        pltpu.VMEM((3, rows, width), BF),
    ] + SCATTER_SEMS


N_SCATTER = 18
AHEAD = 1


def scatter16(plan, h, part, out, scratch, t0, tx):
    ra, rb, sa, sb, qa, qb, sz, rz = scratch[:8]
    as_, ar, bs, br, cs, cr, es, er, zs, zr = scratch[8:]
    rows, width = part.shape[3:]
    half = width // 2
    lo, hi = pl.ds(0, half), pl.ds(half, half)
    xo, yo = 1 - h.x, 1 - h.y

    def place(k):
        return jnp.bitwise_xor(h.z, k)

    def first(i, k):
        return (
            remote(part.at[place(k), :, xo, :, lo], ra.at[i], as_.at[i], ar.at[i], ctx=h.xn),
            remote(part.at[place(k), yo, :, :, hi], rb.at[i], bs.at[i], br.at[i], ctx=h.yn),
        )

    def second(i):
        return (
            remote(sa.at[i], qa.at[i], cs.at[i], cr.at[i], ctx=h.yn),
            remote(sb.at[i], qb.at[i], es.at[i], er.at[i], ctx=h.xn),
        )

    def third(k):
        return remote(sz.at[k - 1], rz.at[k - 1], zs.at[k], zr.at[k], ctx=place(k) * 4 + h.xy)

    def start(i, k):
        for c in first(i, k):
            c.start()

    def middle(i, k):
        a, b = first(i, k)
        c, e = second(i)
        a.wait_recv()
        sa[i] = (part[place(k), yo, h.x, :, lo].astype(F32) + ra[i, yo].astype(F32)).astype(BF)
        c.start()
        b.wait_recv()
        sb[i] = (part[place(k), h.y, xo, :, hi].astype(F32) + rb[i, xo].astype(F32)).astype(BF)
        e.start()

    def total(i, k):
        c, e = second(i)
        c.wait_recv()
        e.wait_recv()
        left = part[place(k), h.y, h.x, :, lo].astype(F32) + ra[i, h.y].astype(F32) + qa[i].astype(F32)
        right = part[place(k), h.y, h.x, :, hi].astype(F32) + rb[i, h.x].astype(F32) + qb[i].astype(F32)
        if k:
            sz[k - 1, :, lo] = left.astype(BF)
            sz[k - 1, :, hi] = right.astype(BF)
            third(k).start()
        else:
            out[:, lo] = left
            out[:, hi] = right

    def last():
        for k in (1, 2, 3):
            third(k).wait_recv()
        out[...] += rz[0].astype(F32) + rz[1].astype(F32) + rz[2].astype(F32)
        for k in (1, 2, 3):
            third(k).wait_send()
        for i, k in enumerate((1, 2, 3, 0)):
            for c in first(i, k) + second(i):
                c.wait_send()

    for i, k in enumerate((1, 2, 3, 0)):
        plan.at(t0 + max(0, i - AHEAD + 0.71) * tx if i >= AHEAD else t0 + 0.01 * i, functools.partial(start, i, k))
        plan.at(t0 + i * tx + 0.7 * tx, functools.partial(middle, i, k))
        plan.at(t0 + i * tx + 1.35 * tx, functools.partial(total, i, k))
    plan.at(t0 + 5 * tx, last)


DEAL_SEMS = [DMA((16,))] * 4 + [DMA]


def deal16(plan, h, piece, put, passed, sems, t0, t1, both=True, pace=0.0, relay_from=None):
    ss, sr, fs, fr, own = sems

    def send(step):
        to = jnp.bitwise_xor(h.me, step)
        return remote(piece(to), put(h.me), ss.at[step], sr.at[step], ctx=to)

    def got(step):
        at = jnp.bitwise_xor(h.me, step)
        return remote(put(at), put(at), ss.at[step], sr.at[step], ctx=at)

    def hand(step):
        at = jnp.bitwise_xor(h.me, step)
        return remote(put(at) if step else piece(h.me), passed(at, h.core), fs.at[step], fr.at[step], fsdp=1 - h.core)

    def taken(step):
        at = jnp.bitwise_xor(h.me, step)
        return remote(passed(at, 1 - h.core), passed(at, 1 - h.core), fs.at[step], fr.at[step], fsdp=1 - h.core)

    local = pltpu.make_async_copy(piece(h.me), put(h.me), own)

    def first():
        local.start()
        if both:
            hand(0).start()

    plan.at(t0, first)
    for i, step in enumerate(ORDER):
        plan.at(t0 + pace * i, lambda step=step: send(step).start())

        def relay(step=step):
            got(step).wait_recv()
            if both:
                hand(step).start()

        since = t0 if relay_from is None else relay_from
        plan.at(since + (t1 - since) * (i + 1) / 15 if both else t1, relay)

    def drain():
        if both:
            for step in range(16):
                taken(step).wait_recv()
                hand(step).wait_send()
        for step in ORDER:
            send(step).wait_send()

    plan.at(t1, local.wait)
    plan.at(t1 + 2, drain)


ORDER = (12, 8, 13, 9, 14, 10, 15, 11, 4, 5, 6, 7, 3, 1, 2)

ROWS = 256


def _tri():
    i = lax.broadcasted_iota(jnp.int32, (ROWS, ROWS), 0)
    j = lax.broadcasted_iota(jnp.int32, (ROWS, ROWS), 1)
    return i <= j


def _heads(value):
    lane = lax.broadcasted_iota(jnp.int32, value.shape, 1)
    zero = jnp.zeros_like(value)
    return jnp.where(lane < 64, value, zero), jnp.where(lane >= 64, value, zero)


def _nt(a, b):
    return lax.dot_general(a, b, (((1,), (1,)), ((), ())), preferred_element_type=F32)


def _tn(a, b):
    return lax.dot_general(a, b, (((0,), (0,)), ((), ())), preferred_element_type=F32)


def _nn(a, b):
    return jnp.dot(a, b, preferred_element_type=F32)


def _scores(keys, query, tri):
    scores = _nt(keys, query)
    n = keys.shape[0]
    low = jnp.where(tri, scores[n - ROWS :], -1e30)
    return low if n == ROWS else jnp.concatenate([scores[: n - ROWS], low], 0)


def sort_rows(order_ref, src, dst):
    for b in range(src.shape[0]):
        dst[b * 64 : (b + 1) * 64, :] = src[order_ref[b]]


def attend_step(i, qs, ks, vs, os, lse):
    tri = _tri()
    n = (i + 1) * ROWS
    mine = slice(i * ROWS, n)
    total = None
    for head, query in enumerate(_heads(qs[mine, :] * BF(0.125))):
        scores = _scores(ks[:n, :], query, tri)
        top = jnp.max(scores, 0, keepdims=True)
        raw = jnp.exp(scores - top)
        size = jnp.sum(raw, 0, keepdims=True)
        lse[head : head + 1, mine] = top + jnp.log(size)
        probs = (raw * (1.0 / size)).astype(BF)
        part = _tn(probs, _heads(vs[:n, :])[head])
        total = part if total is None else total + part
    os[mine, :] = total.astype(BF)


def back_step(i, qs, ks, vs, gs, lse, dq, dk, dv):
    tri = _tri()
    n = (i + 1) * ROWS
    mine = slice(i * ROWS, n)
    total = None
    queries = _heads(qs[mine, :] * BF(0.125))
    grads = _heads(gs[mine, :])
    for head in range(2):
        scores = _scores(ks[:n, :], queries[head], tri)
        probs = jnp.exp(scores - lse[head : head + 1, mine])
        gp = _nt(vs[:n, :], grads[head])
        delta = jnp.sum(probs * gp, 0, keepdims=True)
        ds = (probs * (gp - delta)).astype(BF)
        dv[:n, :] += _nn(probs.astype(BF), grads[head])
        dk[:n, :] += _nn(ds, queries[head])
        part = _tn(ds, _heads(ks[:n, :])[head])
        total = part if total is None else total + part
    dq[mine, :] = total * 0.125


def swap_halves(values):
    lane = lax.broadcasted_iota(jnp.int32, values.shape, 1)
    return jnp.where(lax.rem(lane, 64) < 32, pltpu.roll(values, 96, 1), pltpu.roll(values, 32, 1))


from jax.sharding import PartitionSpec as P

HEADS = 32
HD = 64
EPSILON = 1e-05
THETA_BASE = 130000.0
ANY = pl.BlockSpec(memory_space=pl.ANY)
INNER = pl.BlockSpec(memory_space=pltpu.VMEM)


def comm_call(kernel, outs, out_specs, in_specs, scratch, cid, name, vmem=40):
    return pl.pallas_call(
        kernel,
        out_shape=outs,
        in_specs=in_specs,
        out_specs=out_specs,
        scratch_shapes=scratch,
        compiler_params=pltpu.CompilerParams(
            collective_id=cid, has_side_effects=True, vmem_limit_bytes=vmem << 20
        ),
        name=name,
    )


def take(refs, n):
    head, refs[:] = refs[:n], refs[n:]
    return head


def columns(src, width):
    return lambda c: src.at[:, pl.ds(pl.multiple_of(c * width, 128), width)]


def columns_of(out, width):
    return lambda c: out.at[:, pl.ds(pl.multiple_of(c * width, 128), width)]


def deal_columns(plan, h, src, out, sems, t0, t1, relay_from, lanes=None):
    lanes = pl.ds(0, out.shape[3]) if lanes is None else lanes
    deal16(
        plan, h, columns(src, lanes.size), lambda c: out.at[c, h.core, :, lanes], lambda c, core: out.at[c, core, :, lanes],
        sems, t0, t1, relay_from=relay_from,
    )


def front_kernel(
    order, table, x, wq, wk, wv, wg, wu, wd, wo, cot, tile, cos, sin,
    normed, w_out, gains, qs, ks, vs, lse, low, g_out, u_out, d_out, o_out, c_out, *refs
):
    refs = list(refs)
    xg, wqkv, tiles, stage, q, k_rows, v, o, o_rows = take(refs, 9)
    stage_sem, send, recv = take(refs, 3)
    rows, width = x.shape
    h = Here()
    greet_all(h)
    plan = Plan()
    for i, src in enumerate((wq, wk, wv)):
        deal_columns(plan, h, src, wqkv, take(refs, 5), 0, 16, 10, pl.ds(i * 128, 128))
    deal16(
        plan, h, lambda c: tile, lambda c: tiles.at[c, h.core], lambda c, core: tiles.at[c, core], take(refs, 5), 0, 17,
        relay_from=11,
    )
    done = gather16(plan, h, x, xg, take(refs, 13), 0, 14, 20, by_plane=True)
    for i, (src, out) in enumerate(((wg, g_out), (wu, u_out), (wd, d_out))):
        deal_columns(plan, h, src, out, take(refs, 5), 20 + i, 190 + i, 170)
    gather16(plan, h, wo, o_out.at[:, h.core], take(refs, 13), 75, 10, 14)
    gather16(plan, h, cot, c_out, take(refs, 13), 105, 18, 26)
    to_sems = take(refs, 5)
    mine, other = o_out.at[:, h.core], o_out.at[:, 1 - h.core]
    across = remote(mine, mine, send, recv, fsdp=1 - h.core)
    plan.at(160, across.start)

    def plane(k):
        return jnp.bitwise_xor(h.z, k)

    def put_normed(k):
        at = pl.ds(pl.multiple_of(plane(k) * 4 * rows, 4 * rows), 4 * rows)
        return pltpu.make_async_copy(stage, normed.at[at], stage_sem)

    def spread_gains():
        gains[...] = jnp.zeros_like(gains)
        for c in range(16):
            both = tiles[c, 0].astype(F32) + tiles[c, 1].astype(F32)
            gains[:, c * 128 : (c + 1) * 128] = both[0:8]

    def work(k):
        zz = plane(k)
        done(zz)
        if k:
            put_normed(k - 1).wait()
        else:
            spread_gains()
        for p in range(2):
            at = pl.ds(pl.multiple_of((zz * 4 + p * 2) * rows, 2 * rows), 2 * rows)
            blocks = pl.ds(zz * 8 + p * 4, 4)
            value = xg[pl.ds(zz * 4 + p * 2, 2)].reshape(2 * rows, width).astype(F32)
            inverse = lax.rsqrt(jnp.mean(value * value, -1, keepdims=True) + EPSILON)
            value = (value * inverse * gains[0:1, :]).astype(BF)
            stage[p * 2 * rows : (p + 1) * 2 * rows, :] = value
            pre = _nn(value, wqkv[...].reshape(width, 384))
            for i, out in enumerate((q, k_rows)):
                part = pre[:, i * 128 : (i + 1) * 128]
                turned = part * cos[at, :] + swap_halves(part) * sin[at, :]
                out[blocks] = turned.astype(BF).reshape(4, 64, 128)
            v[blocks] = pre[:, 256:].astype(BF).reshape(4, 64, 128)
        put_normed(k).start()

    for k in range(4):
        plan.at((24, 42, 62, 82)[k], functools.partial(work, k))

    def sort():
        put_normed(3).wait()
        for a, b in ((q, qs), (k_rows, ks), (v, vs)):
            sort_rows(order, a, b)
        w_out[...] = wqkv[...].reshape(width, 384)

    plan.at(83, sort)
    for i in range(16 * rows // ROWS):
        plan.at(84 + 1.3 * i, functools.partial(attend_step, i, qs, ks, vs, o.reshape(16 * rows, 128), lse))

    def unsort():
        for b in range(32):
            o_rows[b // 2, (b % 2) * 64 : (b % 2 + 1) * 64, :] = o[table[b]]

    plan.at(96, unsort)
    deal16(plan, h, lambda c: o_rows.at[c], columns_of(low, 128), None, to_sems, 96.1, 200, both=False)

    def end():
        remote(other, other, send, recv, fsdp=1 - h.core).wait_recv()
        across.wait_send()

    plan.at(210, end)
    plan.run()


def front(order, table, x, wq, wk, wv, wg, wu, wd, wo, cot, tile, cos, sin):
    rows, width = x.shape
    length = 16 * rows
    block = jax.ShapeDtypeStruct((16, 2, wg.shape[0], wg.shape[1] // 16), BF)
    heads = jax.ShapeDtypeStruct((length, 128), BF)
    outs = (
        jax.ShapeDtypeStruct((length, width), BF), jax.ShapeDtypeStruct((width, 384), BF),
        jax.ShapeDtypeStruct((8, width), F32), heads, heads, heads, jax.ShapeDtypeStruct((2, length), F32),
        jax.ShapeDtypeStruct((rows, width), BF), block, block, block,
        jax.ShapeDtypeStruct((16, 2) + wo.shape, BF), jax.ShapeDtypeStruct((16, rows, width), BF),
    )
    smem = pl.BlockSpec(memory_space=pltpu.SMEM)
    scratch = [
        pltpu.VMEM((16, rows, width), BF), pltpu.VMEM((16, 2, wq.shape[0], 384), BF), pltpu.VMEM((16, 2) + tile.shape, BF),
        pltpu.VMEM((4 * rows, width), BF), *[pltpu.VMEM((32, 64, 128), BF)] * 4, pltpu.VMEM((16, rows, 128), BF),
        DMA, DMA, DMA,
    ]
    scratch += DEAL_SEMS * 4 + GATHER_SEMS + DEAL_SEMS * 3 + GATHER_SEMS * 2 + DEAL_SEMS
    return comm_call(
        front_kernel, outs, [ANY] + [INNER] * 6 + [ANY] * 6, [smem] * 2 + [INNER] + [ANY] * 8 + [INNER] * 3, scratch, 0,
        "front", 58,
    )(order, table, x, wq, wk, wv, wg, wu, wd, wo, cot, tile, cos, sin)


def mlp_kernel(src, cot, bg, bu, bd, gmi, out_part, own_gu, d_home, *refs):
    refs = list(refs)
    xm, ct, wg, wu, wd, grads, act, part, stage, cols = take(refs, 10)
    other_gu, got_gu, own_d, other_d, got_d = take(refs, 5)
    w_sem, ct_sem, cols_sem, stage_sem, ex_sems = take(refs, 5)
    rows, width = src.shape
    hidden = wg.shape[1]
    block = own_d.shape[1]
    h = Here()
    loads = [pltpu.make_async_copy(a, b, w_sem.at[i]) for i, (a, b) in enumerate(((bg, wg), (bu, wu), (bd, wd)))]

    def plane(k):
        return jnp.bitwise_xor(h.z, k)

    def load_cot(k):
        return pltpu.make_async_copy(cot.at[pl.ds(plane(k) * 4, 4)], ct.at[k % 2], ct_sem.at[k % 2])

    def put_out(k):
        return pltpu.make_async_copy(stage, out_part.at[pl.ds(plane(k) * 4, 4)], stage_sem)

    for c in loads + [load_cot(0), load_cot(1)]:
        c.start()
    greet_all(h)
    plan = Plan()
    done = gather16(plan, h, src, xm, take(refs, 13), 0, 12, 17, by_plane=True)

    def work(k):
        zz = plane(k)
        done(zz)
        if k == 0:
            for c in loads:
                c.wait()
        load_cot(k).wait()
        if k:
            put_out(k - 1).wait()

        def pair(p, carry):
            two = pl.ds(p * 2, 2)
            at = pl.ds(pl.multiple_of((zz * 4 + p * 2) * rows, 2 * rows), 2 * rows)
            x = xm[pl.ds(zz * 4 + p * 2, 2)].reshape(2 * rows, width)
            gate, up = _nn(x, wg[...]), _nn(x, wu[...])
            sig = jax.nn.sigmoid(gate)
            silu = gate * sig
            low = (silu * up).astype(BF)
            act[at, :] = low
            stage[two] = _nt(low, wd[...]).astype(BF).reshape(2, rows, width)
            grad = _nn(ct[k % 2, two].reshape(2 * rows, width), wd[...])
            grad_gate = (grad * up * sig * (1.0 + gate * (1.0 - sig))).astype(BF)
            grad_up = (grad * silu).astype(BF)
            grads[at, pl.ds(0, hidden)] = grad_gate
            grads[at, pl.ds(hidden, hidden)] = grad_up
            back = _nt(grad_gate, wg[...]) + _nt(grad_up, wu[...])
            part[zz, pl.ds(p, 1)] = back.astype(BF).reshape(1, 2, rows, width)
            return carry

        lax.fori_loop(0, 2, pair, 0)
        put_out(k).start()
        if k + 2 < 4:
            load_cot(k + 2).start()

    for k in range(4):
        plan.at((22, 38, 55, 72)[k], functools.partial(work, k))
    plan.at(76, lambda: put_out(3).wait())
    scatter16(plan, h, part, gmi, take(refs, N_SCATTER), 44, 18)

    def split(c, both, own, other):
        both = both.astype(BF).reshape(2, block, both.shape[1])
        own[c] = jnp.where(h.core == 0, both[0], both[1])
        other[c] = jnp.where(h.core == 0, both[1], both[0])

    def exchange(i, other, got):
        return remote(other, got, ex_sems.at[i], ex_sems.at[2 + i], fsdp=1 - h.core)

    def load_cols(c):
        slot = lax.rem(c, 2)
        at = pl.ds(pl.multiple_of(c * 2 * block, 128), 2 * block)
        return pltpu.make_async_copy(cot.at[:, :, at], cols.at[slot], cols_sem.at[slot])

    def grads_gu(first):
        def one(c, carry):
            at = pl.ds(pl.multiple_of(c * 2 * block, 128), 2 * block)
            lhs = xm[:, :, at].reshape(16 * rows, 2 * block)
            split(c, _tn(lhs, grads[...]), own_gu, other_gu)
            return carry

        lax.fori_loop(first, first + 4, one, 0)

    def grads_d(first):
        def one(c, carry):
            pl.when(c < 15)(lambda: load_cols(c + 1).start())
            load_cols(c).wait()
            lhs = cols[lax.rem(c, 2)].reshape(16 * rows, 2 * block)
            split(c, _tn(lhs, act[...]), own_d, other_d)
            return carry

        lax.fori_loop(first, first + 4, one, 0)

    def join(i, own, other, got):
        exchange(i, other, got).wait_recv()
        for c in range(16):
            own[c] = (own[c].astype(F32) + got[c].astype(F32)).astype(BF)
        exchange(i, other, got).wait_send()

    plan.at(74, lambda: load_cols(0).start())
    for i in range(4):
        plan.at(76.5 + 2 * i, functools.partial(grads_d, 4 * i))
        plan.at(88 + 3 * i, functools.partial(grads_gu, 4 * i))
    plan.at(85, lambda: exchange(1, other_d, got_d).start())
    plan.at(89, lambda: join(1, own_d, other_d, got_d))
    plan.at(100, lambda: exchange(0, other_gu, got_gu).start())
    plan.at(110, lambda: join(0, own_gu, other_gu, got_gu))
    deal16(plan, h, lambda c: own_d.at[c], columns_of(d_home, hidden), None, take(refs, 5), 89.1, 182, both=False)
    plan.run()


def mlp(src, cot, bg, bu, bd):
    rows, width = src.shape
    block, hidden = bg.shape[2:]
    full = pltpu.VMEM((width, hidden), BF)
    gu, d = pltpu.VMEM((16, block, 2 * hidden), BF), pltpu.VMEM((16, block, hidden), BF)
    scratch = [
        pltpu.VMEM((16, rows, width), BF), pltpu.VMEM((2, 4, rows, width), BF), full, full, full,
        pltpu.VMEM((16 * rows, 2 * hidden), BF), pltpu.VMEM((16 * rows, hidden), BF),
        pltpu.VMEM((4, 2, 2, rows, width), BF), pltpu.VMEM((4, rows, width), BF),
        pltpu.VMEM((2, 16, rows, 2 * block), BF), gu, gu, d, d, d,
        DMA((3,)), DMA((2,)), DMA((2,)), DMA, DMA((4,)),
    ]
    scratch += GATHER_SEMS + scatter_scratch(rows, width) + DEAL_SEMS
    home = jax.ShapeDtypeStruct((block, 16 * hidden), BF)
    outs = (jax.ShapeDtypeStruct((rows, width), F32), jax.ShapeDtypeStruct((16, rows, width), BF), jax.ShapeDtypeStruct((16, block, 2 * hidden), BF), home)
    return comm_call(mlp_kernel, outs, [INNER, ANY, INNER, ANY], [ANY] * 5, scratch, 5, "mlp", 61)(
        src, cot, *(b.reshape(width, hidden) for b in (bg, bu, bd))
    )


def outer_home(plan, h, left, right, own, other, got, send, recv, t0, t1):
    rows = own.shape[1]
    over = remote(other, got, send, recv, fsdp=1 - h.core)

    def compute():
        mine, theirs = pl.multiple_of(h.core * rows, rows), pl.multiple_of((1 - h.core) * rows, rows)
        for c in range(16):
            lhs = left[:, c * 2 * rows : (c + 1) * 2 * rows]
            both = _tn(lhs, right[...]).astype(BF).reshape(2, rows, right.shape[1])
            own[c] = jnp.where(h.core == 0, both[0], both[1])
            other[c] = jnp.where(h.core == 0, both[1], both[0])
        over.start()

    def add():
        over.wait_recv()
        for c in range(16):
            own[c] = (own[c].astype(F32) + got[c].astype(F32)).astype(BF)
        over.wait_send()

    plan.at(t0, compute)
    plan.at(t1, add)


def back_kernel(order, table, ga, qs, ks, vs, lse, cos, sin, out_part, low, branch, gu, dqkv, out_sum, wo_sum, g_home, *refs):
    refs = list(refs)
    gh, gs, dq, dk, dv, own, other, got = take(refs, 8)
    send, recv = take(refs, 2)
    gh_rows = gh.reshape(16, ga.shape[0], 128)
    flat = [g.reshape(qs.shape) for g in (dq, dk, dv)]
    h = Here()
    greet_all(h)
    plan = Plan()
    deal16(plan, h, columns(ga, 128), lambda c: gh_rows.at[c], None, take(refs, 5), 0, 14, both=False)
    gu_sems = take(refs, 5)
    scatter16(plan, h, out_part, out_sum, take(refs, N_SCATTER), 1, 20)
    outer_home(plan, h, low, branch, own, other, got, send, recv, 2, 8)
    first = pl.ds(0, gu.shape[2] // 2)
    deal16(
        plan, h, lambda c: gu.at[c, :, first], columns_of(g_home, gu.shape[2] // 2), None, gu_sems, 3, 198, both=False
    )
    scatter16(plan, h, own.reshape(4, 2, 2, *own.shape[1:]), wo_sum, take(refs, N_SCATTER), 8.1, 18)

    def begin():
        sort_rows(order, gh, gs)
        dk[...] = jnp.zeros_like(dk)
        dv[...] = jnp.zeros_like(dv)

    plan.at(15, begin)
    for i in range(qs.shape[0] // ROWS):
        plan.at(16 + 2.2 * i, functools.partial(back_step, i, qs, ks, vs, gs, lse, *flat))

    def end():
        for b in range(32):
            rows = slice(b * 64, (b + 1) * 64)
            for i, grad in enumerate((dq, dk)):
                value = grad[table[b]]
                turned = swap_halves(value)
                dqkv[rows, i * 128 : (i + 1) * 128] = (value * cos[rows, :] - turned * sin[rows, :]).astype(BF)
            dqkv[rows, 256:] = dv[table[b]].astype(BF)

    plan.at(34.5, end)
    plan.run()


def back(order, table, ga, qs, ks, vs, lse, cos, sin, out_part, low, branch, gu):
    rows, width = ga.shape
    length = qs.shape[0]
    smem = pl.BlockSpec(memory_space=pltpu.SMEM)
    half = pltpu.VMEM((16, width // 32, width), BF)
    outs = (
        jax.ShapeDtypeStruct((length, 384), BF),
        jax.ShapeDtypeStruct((rows, width), F32),
        jax.ShapeDtypeStruct((width // 32, width), F32),
        jax.ShapeDtypeStruct((gu.shape[1], 8 * gu.shape[2]), BF),
    )
    scratch = [pltpu.VMEM((32, 64, 128), BF), pltpu.VMEM((length, 128), BF)]
    scratch += [pltpu.VMEM((32, 64, 128), F32)] * 3 + [half] * 3 + [DMA] * 2 + DEAL_SEMS * 2
    scratch += scatter_scratch(rows, width) + scatter_scratch(width // 32, width)
    return comm_call(back_kernel, outs, [INNER] * 3 + [ANY], [smem] * 2 + [INNER] * 10 + [ANY], scratch, 6, "back", 60)(
        order, table, ga, qs, ks, vs, lse, cos, sin, out_part.reshape(4, 2, 2, rows, width), low, branch, gu
    )


def core_sum(plan, h, part, got, total, sems, t0, t1):
    send, recv, mine = sems
    across = remote(part.at[:, 1 - h.core], got, send, recv, fsdp=1 - h.core)
    local = pltpu.make_async_copy(part.at[:, h.core], total, mine)

    def start():
        across.start()
        local.start()

    def add():
        across.wait_recv()
        local.wait()
        for c in range(16):
            total[c] = (total[c].astype(F32) + got[c].astype(F32)).astype(BF)
        across.wait_send()

    plan.at(t0, start)
    plan.at(t1, add)


def home_kernel(n, *refs):
    refs = list(refs)
    gn, parts, (scaled, other_gain, gu) = take(refs, 1)[0], take(refs, n), take(refs, 3)
    gn_out, outs, gains_out, u_home = take(refs, 1)[0], take(refs, n), *take(refs, 2)
    h = Here()
    greet_all(h)
    plan = Plan()
    for i, (part, out) in enumerate(zip(parts, outs)):
        got, total = take(refs, 2)
        core_sum(plan, h, part, got, total, take(refs, 3), 0.1 * i, 2 * i + 1)
        deal16(
            plan, h, lambda c, t=total: t.at[c], columns_of(out, part.shape[3]), None, take(refs, 5), 2 * i + 1.5, 198 + i,
            both=False,
        )
    last = pl.ds(gu.shape[2] // 2, gu.shape[2] // 2)
    deal16(
        plan, h, lambda c: gu.at[c, :, last], columns_of(u_home, gu.shape[2] // 2), None, take(refs, 5), 0.5, 197, both=False
    )
    gains, got, landed, send, recv = take(refs, 5)
    gain_sems = take(refs, 5)
    scatter16(plan, h, gn, gn_out, refs, 0.5, 20)
    over = remote(gains, got, send, recv, fsdp=1 - h.core)

    def sums():
        gains[...] = jnp.zeros_like(gains)
        total = jnp.sum(gn_out[...] * scaled[...], 0, keepdims=True)
        for c in range(16):
            at = slice(c * 128, (c + 1) * 128)
            gains[c, 0:1] = total[:, at]
            gains[c, 1:2] = other_gain[:, at]
        over.start()
        over.wait_recv()
        over.wait_send()
        gains[...] += got[...]

    plan.at(200, sums)
    deal16(plan, h, lambda c: gains.at[c], lambda c: landed.at[c], None, gain_sems, 201, 204, both=False)

    def add():
        total = landed[0]
        for c in range(1, 16):
            total = total + landed[c]
        gains_out[...] = total

    plan.at(300, add)
    plan.run()


def home(gn, parts, scaled, other_gain, gu):
    scratch = []
    rows, width = gn.shape[0] // 16, gn.shape[1]
    for p in parts:
        buffer = pltpu.VMEM((p.shape[0],) + p.shape[2:], BF)
        scratch += [buffer, buffer, DMA, DMA, DMA] + DEAL_SEMS
    outs = [jax.ShapeDtypeStruct((rows, width), F32)]
    outs += [jax.ShapeDtypeStruct((p.shape[2], 16 * p.shape[3]), BF) for p in parts]
    outs.append(jax.ShapeDtypeStruct((8, 128), F32))
    outs.append(jax.ShapeDtypeStruct((gu.shape[1], 8 * gu.shape[2]), BF))
    n = len(parts)
    tile = pltpu.VMEM((16, 8, 128), F32)
    scratch += DEAL_SEMS + [tile, tile, tile, DMA, DMA] + DEAL_SEMS + scatter_scratch(rows, width)
    return comm_call(
        functools.partial(home_kernel, n), tuple(outs), [INNER] + [ANY] * n + [INNER, ANY], [INNER] + [ANY] * n + [INNER] * 2 + [ANY],
        scratch, 7, "home", 58,
    )(gn.reshape(4, 2, 2, rows, width), *parts, scaled, other_gain, gu)


def rope_tables(positions):
    inv_freq = THETA_BASE ** (-(jnp.arange(HD // 2, dtype=F32) * 2.0 / HD))
    angles = positions.astype(F32)[:, None] * inv_freq[None, :]
    return jnp.tile(jnp.cos(angles), (1, 4)), jnp.tile(jnp.sin(angles), (1, 4))


def swap(values):
    a, b, c, d = jnp.split(values, 4, -1)
    return jnp.concatenate([b, a, d, c], -1)


def fast_body(x, table, attn_gain, wq, wk, wv, wo, mlp_gain, wg, wu, wd, cot):
    x, cot, table = x[0], cot[0], table[0].reshape(32)
    rows, width = x.shape
    length = rows * 16
    core = lax.axis_index("fsdp")
    slots = jnp.arange(32, dtype=jnp.int32)
    order = jnp.sum(jnp.where(table[None, :] == slots[:, None], slots[None, :], 0), 1)
    positions = (table[:, None] * 64 + jnp.arange(64, dtype=jnp.int32)[None]).reshape(length)
    cos, sin = rope_tables(positions)
    turn = jnp.where(jnp.arange(128) % 64 < 32, -1.0, 1.0).astype(F32)
    sin = sin * turn

    def dot(a, b):
        return jnp.dot(a, b, preferred_element_type=F32)

    def dot_nt(a, b):
        return lax.dot_general(a, b, (((1,), (1,)), ((), ())), preferred_element_type=F32)

    def dot_tn(a, b):
        return lax.dot_general(a, b, (((0,), (0,)), ((), ())), preferred_element_type=F32)

    lane = jnp.arange(128) // 64
    tile = jnp.where(lane[None] == core, jnp.tile(jnp.stack([attn_gain, mlp_gain]), (1, 2)), 0)
    tile = jnp.pad(tile, ((0, 14), (0, 0)))
    normed, wqkv, gains, qs, ks, vs, lse, attn_low, bg, bu, bd, full_out, cot_all = front(
        order, table, x, wq, wk, wv, wg, wu, wd, wo, cot, tile, cos, sin
    )
    again, mgain = gains[0], gains[1]
    full_out = full_out.reshape(width, width)
    own = x.astype(F32)
    inv_in = lax.rsqrt(jnp.mean(own * own, -1, keepdims=True) + EPSILON)
    hidden = own + dot(attn_low, full_out)
    inv_mid = lax.rsqrt(jnp.mean(hidden * hidden, -1, keepdims=True) + EPSILON)
    gmi, out_part, part_gu, gd = mlp((hidden * inv_mid * mgain).astype(BF), cot_all, bg, bu, bd)

    def norm_back(grad, source, inv, gain):
        scaled = grad * gain
        inner = jnp.sum(scaled * source, -1, keepdims=True)
        return inv * scaled - inv * inv * inv / width * source * inner

    mgain_part = jnp.sum(gmi * hidden * inv_mid, 0)
    grad_hidden = cot.astype(F32) + norm_back(gmi, hidden, inv_mid, mgain)
    grad_branch = grad_hidden.astype(BF)
    grad_att = dot_nt(grad_branch, full_out).astype(BF)
    grad_qkv, out_sum, wo_grad, gg = back(
        order, table, grad_att, qs, ks, vs, lse, cos, sin, out_part, attn_low, grad_branch, part_gu
    )
    layer_output = (hidden + out_sum).astype(BF)
    gn_part = dot_nt(grad_qkv, wqkv).astype(BF)

    def pieces(grad):
        return grad.astype(BF).reshape(16, 2, 64, grad.shape[1])

    parts = [pieces(dot_tn(normed, grad_qkv))]
    gn, gqkv, gains, gu = home(gn_part, parts, own * inv_in, mgain_part[None], part_gu)
    input_grad = grad_hidden + norm_back(gn, own, inv_in, again)
    gg, gu, gd, gqkv = (g.astype(F32) for g in (gg, gu, gd, gqkv))
    gq, gk, gv = (gqkv.reshape(64, 16, 3, 128)[:, :, i].reshape(64, width) for i in range(3))
    gains = lax.dynamic_slice_in_dim(gains, core * 64, 64, 1)
    return (layer_output[None], input_grad[None], gains[0], gq, gk, gv, wo_grad, gains[1], gg, gu, gd)


MASKED = -1e30


def general_tables(positions):
    inv_freq = THETA_BASE ** (-(jnp.arange(HD // 2, dtype=jnp.float32) * 2.0 / HD))
    angles = positions.astype(jnp.float32)[:, None] * inv_freq[None, :]
    cosine = jnp.cos(angles)
    sine_tab = jnp.sin(angles)
    return (jnp.concatenate([cosine, cosine], -1), jnp.concatenate([sine_tab, sine_tab], -1))


def rotate(values, cosine, sine_tab):
    middle = values.shape[-1] // 2
    turned = jnp.concatenate([-values[..., middle:], values[..., :middle]], -1)
    return values * cosine[:, None, :] + turned * sine_tab[:, None, :]


def rotate_back(grads_in, cosine, sine_tab):
    middle = grads_in.shape[-1] // 2
    shifted = grads_in * sine_tab[:, None, :]
    turned = jnp.concatenate([shifted[..., middle:], -shifted[..., :middle]], -1)
    return grads_in * cosine[:, None, :] + turned


def inverse_rms(rows_in):
    return lax.rsqrt(jnp.mean(rows_in * rows_in, -1, keepdims=True) + EPSILON)


def general_norm_back(grad_normed, rows_in, inverse, gain_vec):
    scaled = grad_normed * gain_vec
    inner_sum = jnp.sum(scaled * rows_in, -1, keepdims=True)
    return inverse * scaled - inverse * inverse * inverse / rows_in.shape[-1] * rows_in * inner_sum


def score_rows(query_rows, key_rows, query_pos, key_pos):
    scores = jnp.einsum(
        "qhd,khd->hqk", query_rows, key_rows, preferred_element_type=jnp.float32
    ) * HD ** (-0.5)
    visible = key_pos[None, None, :] <= query_pos[None, :, None]
    return (scores, visible)


def softmax_rows(scores, visible, log_total):
    return jnp.where(
        visible, jnp.exp(jnp.where(visible, scores - log_total[..., None], MASKED)), 0.0
    )


def walk_keys(kv_steps, top_pos, width, step_fn, initial):
    step_rows = kv_steps.shape[1]
    offsets = jnp.arange(step_rows, dtype=jnp.int32)

    def advance(carried, step_item):
        step_index, kv_block = step_item
        first_key = step_index * step_rows
        key_rows = kv_block[:, :width].reshape(step_rows, HEADS, HD)
        value_rows = kv_block[:, width:].reshape(step_rows, HEADS, HD)
        key_pos = first_key + offsets
        updated = lax.cond(
            first_key <= top_pos,
            lambda state: step_fn(state, key_rows, value_rows, key_pos),
            lambda state: state,
            carried,
        )
        return (updated, None)

    indices = jnp.arange(kv_steps.shape[0], dtype=jnp.int32)
    final_state, ignored = lax.scan(advance, initial, (indices, kv_steps))
    return final_state


def general_body(
    layer_input,
    block_table,
    attn_gain,
    query_weight,
    key_weight,
    value_weight,
    out_weight,
    mlp_gain,
    gate_weight,
    up_weight,
    down_weight,
    cotangent,
):
    tokens = layer_input.shape[1]
    width = layer_input.shape[2]
    half_rows = tokens // 2
    ranks = lax.axis_size("ctx")
    length = tokens * ranks
    score_scale = HD ** (-0.5)
    block_ids = block_table[0].reshape(2 * ranks)
    own_blocks = lax.dynamic_slice_in_dim(block_ids, lax.axis_index("ctx") * 2, 2)
    inner = jnp.arange(half_rows, dtype=jnp.int32)
    query_pos = (own_blocks[:, None] * half_rows + inner[None, :]).reshape(tokens)
    cosine, sine_tab = general_tables(query_pos)
    full_query, full_key, full_value, full_out, full_attn_gain = (
        lax.all_gather(query_weight, ("ctx", "fsdp"), axis=0, tiled=True),
        lax.all_gather(key_weight, ("ctx", "fsdp"), axis=0, tiled=True),
        lax.all_gather(value_weight, ("ctx", "fsdp"), axis=0, tiled=True),
        lax.all_gather(out_weight, ("ctx", "fsdp"), axis=0, tiled=True),
        lax.all_gather(attn_gain, ("ctx", "fsdp"), axis=0, tiled=True),
    )
    source = layer_input[0].astype(jnp.float32)
    inverse_in = inverse_rms(source)
    normed = (source * inverse_in * full_attn_gain.astype(jnp.float32)).astype(jnp.bfloat16)
    query_pre = jnp.dot(normed, full_query, preferred_element_type=jnp.float32).reshape(
        tokens, HEADS, HD
    )
    key_pre = jnp.dot(normed, full_key, preferred_element_type=jnp.float32).reshape(
        tokens, HEADS, HD
    )
    value_low = jnp.dot(normed, full_value, preferred_element_type=jnp.float32).astype(jnp.bfloat16)
    queries = rotate(query_pre, cosine, sine_tab).astype(jnp.bfloat16)
    keys_low = rotate(key_pre, cosine, sine_tab).astype(jnp.bfloat16).reshape(tokens, width)
    kv_dev = lax.all_gather(jnp.concatenate([keys_low, value_low], 1), "ctx", axis=0, tiled=True)
    slot_ids = jnp.arange(2 * ranks, dtype=jnp.int32)
    holder = jnp.sum(jnp.where(block_ids[None, :] == slot_ids[:, None], slot_ids[None, :], 0), 1)
    chosen = (holder[:, None] == slot_ids[None, :]).astype(jnp.bfloat16)
    kv_seq = jnp.einsum(
        "ab,bn->an", chosen, kv_dev.reshape(2 * ranks, half_rows * 2 * width)
    ).reshape(length, 2 * width)
    step_rows = min(512, length)
    kv_steps = kv_seq.reshape(length // step_rows, step_rows, 2 * width)
    log_totals = []
    attended_parts = []
    top_list = []
    for slot_index in range(2):
        slot_queries = queries[slot_index * half_rows : (slot_index + 1) * half_rows]
        slot_pos = query_pos[slot_index * half_rows : (slot_index + 1) * half_rows]
        top_pos = own_blocks[slot_index] * half_rows + half_rows - 1
        top_list.append(top_pos)

        def stat_step(state, key_rows, value_rows, key_pos):
            running, running_sum = state
            scores, visible = score_rows(slot_queries, key_rows, slot_pos, key_pos)
            scores = jnp.where(visible, scores, MASKED)
            newest = jnp.maximum(running, jnp.max(scores, -1))
            running_sum = running_sum * jnp.exp(running - newest) + jnp.sum(
                jnp.where(visible, jnp.exp(scores - newest[..., None]), 0.0), -1
            )
            return (newest, running_sum)

        start_state = (
            jnp.full((HEADS, half_rows), MASKED, jnp.float32),
            jnp.zeros((HEADS, half_rows), jnp.float32),
        )
        running, running_sum = walk_keys(kv_steps, top_pos, width, stat_step, start_state)
        log_total = running + jnp.log(running_sum)

        def value_step(accumulated, key_rows, value_rows, key_pos):
            scores, visible = score_rows(slot_queries, key_rows, slot_pos, key_pos)
            weights_low = softmax_rows(scores, visible, log_total).astype(jnp.bfloat16)
            return accumulated + jnp.einsum(
                "hqk,khd->qhd", weights_low, value_rows, preferred_element_type=jnp.float32
            )

        attended_parts.append(
            walk_keys(
                kv_steps, top_pos, width, value_step, jnp.zeros((half_rows, HEADS, HD), jnp.float32)
            )
        )
        log_totals.append(log_total)
    attended = jnp.concatenate(attended_parts, 0)
    log_all = jnp.concatenate(log_totals, 1)
    attn_low = attended.reshape(tokens, width).astype(jnp.bfloat16)
    hidden = source + jnp.dot(attn_low, full_out, preferred_element_type=jnp.float32)
    full_gate, full_up, full_down, full_mlp_gain = (
        lax.all_gather(gate_weight, ("ctx", "fsdp"), axis=0, tiled=True),
        lax.all_gather(up_weight, ("ctx", "fsdp"), axis=0, tiled=True),
        lax.all_gather(down_weight, ("ctx", "fsdp"), axis=0, tiled=True),
        lax.all_gather(mlp_gain, ("ctx", "fsdp"), axis=0, tiled=True),
    )
    inverse_mid = inverse_rms(hidden)
    mlp_in = (hidden * inverse_mid * full_mlp_gain.astype(jnp.float32)).astype(jnp.bfloat16)
    gate_pre = jnp.dot(mlp_in, full_gate, preferred_element_type=jnp.float32)
    up_pre = jnp.dot(mlp_in, full_up, preferred_element_type=jnp.float32)
    activation = (jax.nn.silu(gate_pre) * up_pre).astype(jnp.bfloat16)
    branch_mlp = jnp.einsum("tf,df->td", activation, full_down, preferred_element_type=jnp.float32)
    layer_output = (hidden + branch_mlp).astype(jnp.bfloat16)
    back_gate, back_up, back_down, back_mlp_gain = (
        lax.all_gather(gate_weight, ("ctx", "fsdp"), axis=0, tiled=True),
        lax.all_gather(up_weight, ("ctx", "fsdp"), axis=0, tiled=True),
        lax.all_gather(down_weight, ("ctx", "fsdp"), axis=0, tiled=True),
        lax.all_gather(mlp_gain, ("ctx", "fsdp"), axis=0, tiled=True),
    )
    grad_out_low = cotangent[0]
    grad_act = jnp.dot(grad_out_low, back_down, preferred_element_type=jnp.float32)
    sigmoid_gate = jax.nn.sigmoid(gate_pre)
    grad_gate = (grad_act * up_pre * sigmoid_gate * (1.0 + gate_pre * (1.0 - sigmoid_gate))).astype(
        jnp.bfloat16
    )
    grad_up = (grad_act * gate_pre * sigmoid_gate).astype(jnp.bfloat16)
    grad_mlp_in = jnp.einsum(
        "tf,df->td", grad_gate, back_gate, preferred_element_type=jnp.float32
    ) + jnp.einsum("tf,df->td", grad_up, back_up, preferred_element_type=jnp.float32)
    mlp_gain_term = jnp.sum(grad_mlp_in * hidden * inverse_mid, 0)
    grad_hidden = grad_out_low.astype(jnp.float32) + general_norm_back(
        grad_mlp_in, hidden, inverse_mid, back_mlp_gain.astype(jnp.float32)
    )
    grad_branch = grad_hidden.astype(jnp.bfloat16)
    back_query, back_key, back_value, back_out, back_attn_gain = (
        lax.all_gather(query_weight, ("ctx", "fsdp"), axis=0, tiled=True),
        lax.all_gather(key_weight, ("ctx", "fsdp"), axis=0, tiled=True),
        lax.all_gather(value_weight, ("ctx", "fsdp"), axis=0, tiled=True),
        lax.all_gather(out_weight, ("ctx", "fsdp"), axis=0, tiled=True),
        lax.all_gather(attn_gain, ("ctx", "fsdp"), axis=0, tiled=True),
    )
    grad_attended = (
        jnp.einsum("te,de->td", grad_branch, back_out, preferred_element_type=jnp.float32)
        .astype(jnp.bfloat16)
        .reshape(tokens, HEADS, HD)
    )
    delta_all = jnp.sum(grad_attended.astype(jnp.float32) * attended, -1).T
    grad_query_parts = []
    for slot_index in range(2):
        slot_queries = queries[slot_index * half_rows : (slot_index + 1) * half_rows]
        slot_pos = query_pos[slot_index * half_rows : (slot_index + 1) * half_rows]
        slot_grad_out = grad_attended[slot_index * half_rows : (slot_index + 1) * half_rows]
        slot_delta = delta_all[:, slot_index * half_rows : (slot_index + 1) * half_rows]
        slot_log = log_totals[slot_index]

        def query_step(accumulated, key_rows, value_rows, key_pos):
            scores, visible = score_rows(slot_queries, key_rows, slot_pos, key_pos)
            weights_full = softmax_rows(scores, visible, slot_log)
            grad_weights = jnp.einsum(
                "qhd,khd->hqk", slot_grad_out, value_rows, preferred_element_type=jnp.float32
            )
            grad_scores = (weights_full * (grad_weights - slot_delta[..., None])).astype(
                jnp.bfloat16
            )
            return accumulated + jnp.einsum(
                "hqk,khd->qhd", grad_scores, key_rows, preferred_element_type=jnp.float32
            )

        grad_query_parts.append(
            walk_keys(
                kv_steps,
                top_list[slot_index],
                width,
                query_step,
                jnp.zeros((half_rows, HEADS, HD), jnp.float32),
            )
        )
    grad_queries = jnp.concatenate(grad_query_parts, 0) * score_scale
    grad_query_low = (
        rotate_back(grad_queries, cosine, sine_tab).reshape(tokens, width).astype(jnp.bfloat16)
    )
    bottom_key = jnp.min(query_pos)
    query_both = lax.all_gather(
        jnp.concatenate([queries.reshape(tokens, width), grad_attended.reshape(tokens, width)], 1),
        "ctx",
        axis=0,
        tiled=True,
    )
    stats_both = lax.all_gather(
        jnp.stack([log_all.T, delta_all.T], 1).astype(jnp.bfloat16), "ctx", axis=0, tiled=True
    ).astype(jnp.float32)
    all_pos = (block_ids[:, None] * half_rows + inner[None, :]).reshape(length)
    own_keys = keys_low.reshape(tokens, HEADS, HD)
    own_values = value_low.reshape(tokens, HEADS, HD)

    def gather_step(carried, piece_index):
        first = piece_index * step_rows
        piece_pos = lax.dynamic_slice_in_dim(all_pos, first, step_rows)

        def live_piece(state):
            rows_here = lax.dynamic_slice_in_dim(query_both, first, step_rows, 0)
            stats_here = lax.dynamic_slice_in_dim(stats_both, first, step_rows, 0)
            piece_queries = rows_here[:, :width].reshape(step_rows, HEADS, HD)
            piece_grads = rows_here[:, width:].reshape(step_rows, HEADS, HD)
            piece_log = stats_here[:, 0, :].T
            piece_delta = stats_here[:, 1, :].T
            scores, visible = score_rows(piece_queries, own_keys, piece_pos, query_pos)
            weights_full = softmax_rows(scores, visible, piece_log)
            grad_weights = jnp.einsum(
                "qhd,khd->hqk", piece_grads, own_values, preferred_element_type=jnp.float32
            )
            grad_scores = (weights_full * (grad_weights - piece_delta[..., None])).astype(
                jnp.bfloat16
            )
            grad_keys = (
                jnp.einsum(
                    "hqk,qhd->khd", grad_scores, piece_queries, preferred_element_type=jnp.float32
                )
                * score_scale
            )
            grad_values = jnp.einsum(
                "hqk,qhd->khd",
                weights_full.astype(jnp.bfloat16),
                piece_grads,
                preferred_element_type=jnp.float32,
            )
            return (state[0] + grad_keys, state[1] + grad_values)

        updated = lax.cond(
            jnp.max(piece_pos) >= bottom_key, live_piece, lambda state: state, carried
        )
        return (updated, None)

    start_grads = (
        jnp.zeros((tokens, HEADS, HD), jnp.float32),
        jnp.zeros((tokens, HEADS, HD), jnp.float32),
    )
    summed, ignored = lax.scan(
        gather_step, start_grads, jnp.arange(length // step_rows, dtype=jnp.int32)
    )
    kv_grads = jnp.concatenate(
        [summed[0].reshape(tokens, width), summed[1].reshape(tokens, width)], 1
    )
    grad_key_low = (
        rotate_back(kv_grads[:, :width].reshape(tokens, HEADS, HD), cosine, sine_tab)
        .reshape(tokens, width)
        .astype(jnp.bfloat16)
    )
    grad_value_low = kv_grads[:, width:].astype(jnp.bfloat16)
    grad_normed = jnp.einsum(
        "te,de->td", grad_query_low, back_query, preferred_element_type=jnp.float32
    )
    grad_normed = grad_normed + jnp.einsum(
        "te,de->td", grad_key_low, back_key, preferred_element_type=jnp.float32
    )
    grad_normed = grad_normed + jnp.einsum(
        "te,de->td", grad_value_low, back_value, preferred_element_type=jnp.float32
    )
    attn_gain_term = jnp.sum(grad_normed * source * inverse_in, 0)
    input_grad = grad_hidden + general_norm_back(
        grad_normed, source, inverse_in, back_attn_gain.astype(jnp.float32)
    )

    def outer_sum(left_side, right_side):
        return jnp.einsum("tc,te->ce", left_side, right_side, preferred_element_type=jnp.float32)

    weight_grads = lax.psum_scatter(
        jnp.concatenate(
            [
                outer_sum(normed, grad_query_low),
                outer_sum(normed, grad_key_low),
                outer_sum(normed, grad_value_low),
                outer_sum(attn_low, grad_branch),
                outer_sum(mlp_in, grad_gate),
                outer_sum(mlp_in, grad_up),
                outer_sum(grad_out_low, activation),
            ],
            1,
        ),
        ("ctx", "fsdp"),
        scatter_dimension=0,
        tiled=True,
    )
    gain_grads = lax.psum_scatter(
        jnp.stack([attn_gain_term, mlp_gain_term], 1),
        ("ctx", "fsdp"),
        scatter_dimension=0,
        tiled=True,
    )
    hidden_units = gate_weight.shape[1]
    edge_attn = 4 * width
    return (
        layer_output[None],
        input_grad[None],
        gain_grads[:, 0],
        weight_grads[:, 0:width],
        weight_grads[:, width : 2 * width],
        weight_grads[:, 2 * width : 3 * width],
        weight_grads[:, 3 * width : edge_attn],
        gain_grads[:, 1],
        weight_grads[:, edge_attn : edge_attn + hidden_units],
        weight_grads[:, edge_attn + hidden_units : edge_attn + 2 * hidden_units],
        weight_grads[:, edge_attn + 2 * hidden_units : edge_attn + 3 * hidden_units],
    )


def solution(mesh):
    both = ("ctx", "fsdp")
    rows = P(both, None)
    tokens = P("fsdp", "ctx", None)
    return jax.shard_map(
        fast_body if mesh.shape["ctx"] == 16 and mesh.shape["fsdp"] == 2 else general_body,
        mesh=mesh,
        in_specs=(tokens, P("fsdp", None, None), P(both), rows, rows, rows, rows, P(both), rows, rows, rows, tokens),
        out_specs=(tokens, tokens, P(both), rows, rows, rows, rows, P(both), rows, rows, rows),
        check_vma=False,
    )
```

```python
import functools
import jax, jax.numpy as jnp
from jax import lax
from jax.experimental import pallas as pl
from jax.experimental.pallas import tpu as pltpu

MESH = pl.DeviceIdType.MESH
DMA = pltpu.SemaphoreType.DMA
BF = jnp.bfloat16
F32 = jnp.float32


class Plan:
    def __init__(self):
        self.steps = []

    def at(self, when, step):
        self.steps.append((when, len(self.steps), step))

    def run(self):
        for _, _, step in sorted(self.steps, key=lambda s: s[:2]):
            step()


class Here:
    def __init__(self):
        self.me = lax.axis_index("ctx")
        self.core = lax.axis_index("fsdp")
        self.z = self.me // 4
        self.y = lax.rem(self.me // 2, 2)
        self.x = lax.rem(self.me, 2)
        self.xy = lax.rem(self.me, 4)
        self.xn = self.me + 1 - 2 * self.x
        self.yn = self.me + 2 - 4 * self.y


def remote(src, dst, send_sem, recv_sem, **device):
    return pltpu.make_async_remote_copy(
        src_ref=src, dst_ref=dst, send_sem=send_sem, recv_sem=recv_sem, device_id=device, device_id_type=MESH
    )


def greet_all(h):
    barrier = pltpu.get_barrier_semaphore()
    for step in range(1, 16):
        pl.semaphore_signal(barrier, inc=1, device_id={"ctx": jnp.bitwise_xor(h.me, step)}, device_id_type=MESH)
    pl.semaphore_signal(barrier, inc=1, device_id={"fsdp": 1 - h.core}, device_id_type=MESH)
    pl.semaphore_wait(barrier, 16)


GATHER_SEMS = [DMA((4,))] * 12 + [DMA]


def gather16(plan, h, src, out, sems, t0, tz, tx, by_plane=False):
    us, ur, ds, dr, xs, xr, ys, yr, xfs, xfr, yfs, yfr, own = sems
    half = src.shape[0] // 2

    def plane(zz, source=None):
        s = zz * 4 + h.xy
        source = out.at[s] if source is None else source
        return (
            remote(source, out.at[s], xs.at[zz], xr.at[zz], ctx=h.xn),
            remote(source, out.at[s], ys.at[zz], yr.at[zz], ctx=h.yn),
        )

    def across(zz):
        sx = zz * 4 + lax.rem(h.xn, 4)
        sy = zz * 4 + lax.rem(h.yn, 4)
        top, low = pl.ds(0, half), pl.ds(half, half)
        return (
            remote(out.at[sx, top], out.at[sx, top], yfs.at[zz], yfr.at[zz], ctx=h.yn),
            remote(out.at[sy, low], out.at[sy, low], xfs.at[zz], xfr.at[zz], ctx=h.xn),
        )

    def arrived(zz):
        sx = zz * 4 + lax.rem(h.xn, 4)
        sy = zz * 4 + lax.rem(h.yn, 4)
        return (
            remote(out.at[sx], out.at[sx], xs.at[zz], xr.at[zz], ctx=h.xn),
            remote(out.at[sy], out.at[sy], ys.at[zz], yr.at[zz], ctx=h.yn),
        )

    def hop(k, up, source=None):
        it = (h.z - k if up else h.z + k) * 4 + h.xy
        send, recv = (us, ur) if up else (ds, dr)
        source = out.at[it] if source is None else source
        to = h.me + 4 if up else h.me - 4
        return remote(source, out.at[it], send.at[k], recv.at[k + 1], ctx=to)

    def landed(k, up):
        it = (h.z - k if up else h.z + k) * 4 + h.xy
        send, recv = (us, ur) if up else (ds, dr)
        return remote(out.at[it], out.at[it], send.at[k - 1], recv.at[k], ctx=h.me)

    local = pltpu.make_async_copy(src, out.at[h.me], own)

    def first():
        pl.when(h.z < 3)(lambda: hop(0, True, src).start())
        pl.when(h.z > 0)(lambda: hop(0, False, src).start())
        for c in plane(h.z, src):
            c.start()
        local.start()

    plan.at(t0, first)

    def step(k, up):
        def go():
            landed(k, up).wait_recv()
            if k < 3:
                pl.when((h.z < 3) if up else (h.z > 0))(lambda: hop(k, up).start())
            for c in plane(h.z - k if up else h.z + k):
                c.start()

        pl.when((h.z >= k) if up else (h.z + k <= 3))(go)

    def forward(zz):
        got, on = arrived(zz), across(zz)
        for g, c in zip(got, on):
            g.wait_recv()
            c.start()

    def finish(zz):
        sx = zz * 4 + 3 - h.xy
        top, low = pl.ds(0, half), pl.ds(half, half)
        remote(out.at[sx, top], out.at[sx, top], yfs.at[zz], yfr.at[zz], ctx=h.yn).wait_recv()
        remote(out.at[sx, low], out.at[sx, low], xfs.at[zz], xfr.at[zz], ctx=h.xn).wait_recv()

    plan.at(t0 + 0.8 * tx, lambda: forward(h.z))
    for k in (1, 2, 3):
        for up in (True, False):
            valid = (lambda k=k, up=up: (h.z >= k) if up else (h.z + k <= 3))
            plan.at(t0 + k * tz, functools.partial(step, k, up))
            zz = (lambda k=k, up=up: h.z - k if up else h.z + k)
            plan.at(t0 + (k + 0.8) * tx, lambda v=valid, q=zz: pl.when(v())(lambda: forward(q())))

    def drain():
        if not by_plane:
            for zz in range(4):
                finish(zz)
        for k in range(3):
            pl.when((h.z >= k) & (h.z < 3))(lambda: hop(k, True).wait_send())
            pl.when((h.z + k <= 3) & (h.z > 0))(lambda: hop(k, False).wait_send())
        for zz in range(4):
            for c in plane(zz) + across(zz):
                c.wait_send()

    plan.at(t0 + 0.85 * tx, local.wait)
    plan.at(t0 + 4.5 * tx, drain)
    return finish


SCATTER_SEMS = [DMA((4,))] * 8 + [DMA((4,))] * 2


def scatter_scratch(rows, width):
    half = width // 2
    return [
        pltpu.VMEM((4, 2, rows, half), BF),
        pltpu.VMEM((4, 2, rows, half), BF),
        pltpu.VMEM((4, rows, half), BF),
        pltpu.VMEM((4, rows, half), BF),
        pltpu.VMEM((4, rows, half), BF),
        pltpu.VMEM((4, rows, half), BF),
        pltpu.VMEM((3, rows, width), BF),
        pltpu.VMEM((3, rows, width), BF),
    ] + SCATTER_SEMS


N_SCATTER = 18
AHEAD = 1


def scatter16(plan, h, part, out, scratch, t0, tx):
    ra, rb, sa, sb, qa, qb, sz, rz = scratch[:8]
    as_, ar, bs, br, cs, cr, es, er, zs, zr = scratch[8:]
    rows, width = part.shape[3:]
    half = width // 2
    lo, hi = pl.ds(0, half), pl.ds(half, half)
    xo, yo = 1 - h.x, 1 - h.y

    def place(k):
        return jnp.bitwise_xor(h.z, k)

    def first(i, k):
        return (
            remote(part.at[place(k), :, xo, :, lo], ra.at[i], as_.at[i], ar.at[i], ctx=h.xn),
            remote(part.at[place(k), yo, :, :, hi], rb.at[i], bs.at[i], br.at[i], ctx=h.yn),
        )

    def second(i):
        return (
            remote(sa.at[i], qa.at[i], cs.at[i], cr.at[i], ctx=h.yn),
            remote(sb.at[i], qb.at[i], es.at[i], er.at[i], ctx=h.xn),
        )

    def third(k):
        return remote(sz.at[k - 1], rz.at[k - 1], zs.at[k], zr.at[k], ctx=place(k) * 4 + h.xy)

    def start(i, k):
        for c in first(i, k):
            c.start()

    def middle(i, k):
        a, b = first(i, k)
        c, e = second(i)
        a.wait_recv()
        sa[i] = (part[place(k), yo, h.x, :, lo].astype(F32) + ra[i, yo].astype(F32)).astype(BF)
        c.start()
        b.wait_recv()
        sb[i] = (part[place(k), h.y, xo, :, hi].astype(F32) + rb[i, xo].astype(F32)).astype(BF)
        e.start()

    def total(i, k):
        c, e = second(i)
        c.wait_recv()
        e.wait_recv()
        left = part[place(k), h.y, h.x, :, lo].astype(F32) + ra[i, h.y].astype(F32) + qa[i].astype(F32)
        right = part[place(k), h.y, h.x, :, hi].astype(F32) + rb[i, h.x].astype(F32) + qb[i].astype(F32)
        if k:
            sz[k - 1, :, lo] = left.astype(BF)
            sz[k - 1, :, hi] = right.astype(BF)
            third(k).start()
        else:
            out[:, lo] = left
            out[:, hi] = right

    def last():
        for k in (1, 2, 3):
            third(k).wait_recv()
        out[...] += rz[0].astype(F32) + rz[1].astype(F32) + rz[2].astype(F32)
        for k in (1, 2, 3):
            third(k).wait_send()
        for i, k in enumerate((1, 2, 3, 0)):
            for c in first(i, k) + second(i):
                c.wait_send()

    for i, k in enumerate((1, 2, 3, 0)):
        plan.at(t0 + max(0, i - AHEAD + 0.71) * tx if i >= AHEAD else t0 + 0.01 * i, functools.partial(start, i, k))
        plan.at(t0 + i * tx + 0.7 * tx, functools.partial(middle, i, k))
        plan.at(t0 + i * tx + 1.35 * tx, functools.partial(total, i, k))
    plan.at(t0 + 5 * tx, last)


DEAL_SEMS = [DMA((16,))] * 4 + [DMA]


def deal16(plan, h, piece, put, passed, sems, t0, t1, both=True, pace=0.0, relay_from=None):
    ss, sr, fs, fr, own = sems

    def send(step):
        to = jnp.bitwise_xor(h.me, step)
        return remote(piece(to), put(h.me), ss.at[step], sr.at[step], ctx=to)

    def got(step):
        at = jnp.bitwise_xor(h.me, step)
        return remote(put(at), put(at), ss.at[step], sr.at[step], ctx=at)

    def hand(step):
        at = jnp.bitwise_xor(h.me, step)
        return remote(put(at) if step else piece(h.me), passed(at, h.core), fs.at[step], fr.at[step], fsdp=1 - h.core)

    def taken(step):
        at = jnp.bitwise_xor(h.me, step)
        return remote(passed(at, 1 - h.core), passed(at, 1 - h.core), fs.at[step], fr.at[step], fsdp=1 - h.core)

    local = pltpu.make_async_copy(piece(h.me), put(h.me), own)

    def first():
        local.start()
        if both:
            hand(0).start()

    plan.at(t0, first)
    for i, step in enumerate(ORDER):
        plan.at(t0 + pace * i, lambda step=step: send(step).start())

        def relay(step=step):
            got(step).wait_recv()
            if both:
                hand(step).start()

        since = t0 if relay_from is None else relay_from
        plan.at(since + (t1 - since) * (i + 1) / 15 if both else t1, relay)

    def drain():
        if both:
            for step in range(16):
                taken(step).wait_recv()
                hand(step).wait_send()
        for step in ORDER:
            send(step).wait_send()

    plan.at(t1, local.wait)
    plan.at(t1 + 2, drain)


ORDER = (12, 8, 13, 9, 14, 10, 15, 11, 4, 5, 6, 7, 3, 1, 2)


GATHER8_SEMS = [DMA((4,))] * 6 + [DMA]


def gather8(plan, h, src, out, sems, t0, tz, tx):
    us, ur, ds, dr, xs, xr, own = sems

    def level(zz, source=None):
        s = zz * 2 + h.x
        return remote(out.at[s] if source is None else source, out.at[s], xs.at[zz], xr.at[zz], ctx=h.xn)

    def hop(k, up, source=None):
        it = (h.z - k if up else h.z + k) * 2 + h.x
        send, recv = (us, ur) if up else (ds, dr)
        to = h.me + 4 if up else h.me - 4
        return remote(out.at[it] if source is None else source, out.at[it], send.at[k], recv.at[k + 1], ctx=to)

    def landed(k, up):
        it = (h.z - k if up else h.z + k) * 2 + h.x
        send, recv = (us, ur) if up else (ds, dr)
        return remote(out.at[it], out.at[it], send.at[k - 1], recv.at[k], ctx=h.me)

    local = pltpu.make_async_copy(src, out.at[h.z * 2 + h.x], own)

    def first():
        pl.when(h.z < 3)(lambda: hop(0, True, src).start())
        pl.when(h.z > 0)(lambda: hop(0, False, src).start())
        level(h.z, src).start()
        local.start()

    plan.at(t0, first)

    def step(k, up):
        def go():
            landed(k, up).wait_recv()
            if k < 3:
                pl.when((h.z < 3) if up else (h.z > 0))(lambda: hop(k, up).start())
            level(h.z - k if up else h.z + k).start()

        pl.when((h.z >= k) if up else (h.z + k <= 3))(go)

    for k in (1, 2, 3):
        for up in (True, False):
            plan.at(t0 + k * tz, functools.partial(step, k, up))

    def finish(zz):
        s = zz * 2 + 1 - h.x
        remote(out.at[s], out.at[s], xs.at[zz], xr.at[zz], ctx=h.xn).wait_recv()

    def drain():
        for k in range(3):
            pl.when((h.z >= k) & (h.z < 3))(lambda: hop(k, True).wait_send())
            pl.when((h.z + k <= 3) & (h.z > 0))(lambda: hop(k, False).wait_send())
        for zz in range(4):
            level(zz).wait_send()

    plan.at(t0 + 0.85 * tx, local.wait)
    plan.at(t0 + 4.5 * tx, drain)
    return finish


def scatter8_scratch(rows, width):
    few = pltpu.VMEM((3, rows, width), BF)
    return [pltpu.VMEM((4, rows, width), BF), few, few] + [DMA((4,))] * 4


N_SCATTER8 = 7


def scatter8(plan, h, part, out, scratch, starts, totals, end):
    ra, sz, rz, as_, ar, zs, zr = scratch

    def place(k):
        return jnp.bitwise_xor(h.z, k)

    def first(i, k):
        return remote(part.at[place(k), 1 - h.x], ra.at[i], as_.at[i], ar.at[i], ctx=h.xn)

    def second(k):
        return remote(sz.at[k - 1], rz.at[k - 1], zs.at[k], zr.at[k], ctx=place(k) * 4 + h.xy)

    def total(i, k):
        first(i, k).wait_recv()
        value = part[place(k), h.x].astype(F32) + ra[i].astype(F32)
        if k:
            sz[k - 1] = value.astype(BF)
            second(k).start()
        else:
            out[...] = value

    def last():
        for k in (1, 2, 3):
            second(k).wait_recv()
        out[...] += rz[0].astype(F32) + rz[1].astype(F32) + rz[2].astype(F32)
        for k in (1, 2, 3):
            second(k).wait_send()
        for i, k in enumerate((1, 2, 3, 0)):
            first(i, k).wait_send()

    for i, k in enumerate((1, 2, 3, 0)):
        plan.at(starts[i], lambda i=i, k=k: first(i, k).start())
        plan.at(totals[i], functools.partial(total, i, k))
    plan.at(end, last)


DEAL8_SEMS = [DMA((8,))] * 2 + [DMA]


def deal8(plan, h, piece, put, sems, t0, t1):
    ss, sr, own = sems
    row = h.z * 2 + h.x

    def place(r):
        return (r // 2) * 4 + h.y * 2 + lax.rem(r, 2)

    def send(step):
        to = jnp.bitwise_xor(row, step)
        return remote(piece(to), put(row), ss.at[step], sr.at[step], ctx=place(to))

    def got(step):
        at = jnp.bitwise_xor(row, step)
        return remote(put(at), put(at), ss.at[step], sr.at[step], ctx=place(at))

    local = pltpu.make_async_copy(piece(row), put(row), own)

    def start():
        for step in (7, 5, 6, 4, 3, 2, 1):
            send(step).start()
        local.start()

    def end():
        for step in (7, 5, 6, 4, 3, 2, 1):
            got(step).wait_recv()
        local.wait()

    def drain():
        for step in (7, 5, 6, 4, 3, 2, 1):
            send(step).wait_send()

    plan.at(t0, start)
    plan.at(t1, end)
    plan.at(t1 + 40, drain)

ROWS = 256


def _tri():
    i = lax.broadcasted_iota(jnp.int32, (ROWS, ROWS), 0)
    j = lax.broadcasted_iota(jnp.int32, (ROWS, ROWS), 1)
    return i <= j


def _heads(value):
    lane = lax.broadcasted_iota(jnp.int32, value.shape, 1)
    zero = jnp.zeros_like(value)
    return jnp.where(lane < 64, value, zero), jnp.where(lane >= 64, value, zero)


def _nt(a, b):
    return lax.dot_general(a, b, (((1,), (1,)), ((), ())), preferred_element_type=F32)


def _tn(a, b):
    return lax.dot_general(a, b, (((0,), (0,)), ((), ())), preferred_element_type=F32)


def _nn(a, b):
    return jnp.dot(a, b, preferred_element_type=F32)


def _scores(keys, query, tri):
    scores = _nt(keys, query)
    n = keys.shape[0]
    low = jnp.where(tri, scores[n - ROWS :], -1e30)
    return low if n == ROWS else jnp.concatenate([scores[: n - ROWS], low], 0)


def sort_rows(order_ref, src, dst):
    for b in range(src.shape[0]):
        dst[b * 64 : (b + 1) * 64, :] = src[order_ref[b]]


def attend_step(i, qs, ks, vs, os, lse):
    tri = _tri()
    n = (i + 1) * ROWS
    mine = slice(i * ROWS, n)
    total = None
    for head, query in enumerate(_heads(qs[mine, :] * BF(0.125))):
        scores = _scores(ks[:n, :], query, tri)
        top = jnp.max(scores, 0, keepdims=True)
        raw = jnp.exp(scores - top)
        size = jnp.sum(raw, 0, keepdims=True)
        lse[head : head + 1, mine] = top + jnp.log(size)
        probs = (raw * (1.0 / size)).astype(BF)
        part = _tn(probs, _heads(vs[:n, :])[head])
        total = part if total is None else total + part
    os[mine, :] = total.astype(BF)


def back_step(i, qs, ks, vs, gs, lse, dq, dk, dv):
    tri = _tri()
    n = (i + 1) * ROWS
    mine = slice(i * ROWS, n)
    total = None
    queries = _heads(qs[mine, :] * BF(0.125))
    grads = _heads(gs[mine, :])
    for head in range(2):
        scores = _scores(ks[:n, :], queries[head], tri)
        probs = jnp.exp(scores - lse[head : head + 1, mine])
        gp = _nt(vs[:n, :], grads[head])
        delta = jnp.sum(probs * gp, 0, keepdims=True)
        ds = (probs * (gp - delta)).astype(BF)
        dv[:n, :] += _nn(probs.astype(BF), grads[head])
        dk[:n, :] += _nn(ds, queries[head])
        part = _tn(ds, _heads(ks[:n, :])[head])
        total = part if total is None else total + part
    dq[mine, :] = total * 0.125


def swap_halves(values):
    lane = lax.broadcasted_iota(jnp.int32, values.shape, 1)
    return jnp.where(lax.rem(lane, 64) < 32, pltpu.roll(values, 96, 1), pltpu.roll(values, 32, 1))


from jax.sharding import PartitionSpec as P

HEADS = 32
HD = 64
EPSILON = 1e-05
THETA_BASE = 130000.0
ANY = pl.BlockSpec(memory_space=pl.ANY)
INNER = pl.BlockSpec(memory_space=pltpu.VMEM)


def comm_call(kernel, outs, out_specs, in_specs, scratch, cid, name, vmem=40):
    return pl.pallas_call(
        kernel,
        out_shape=outs,
        in_specs=in_specs,
        out_specs=out_specs,
        scratch_shapes=scratch,
        compiler_params=pltpu.CompilerParams(
            collective_id=cid, has_side_effects=True, vmem_limit_bytes=vmem << 20
        ),
        name=name,
    )


def take(refs, n):
    head, refs[:] = refs[:n], refs[n:]
    return head


def columns(src, width):
    return lambda c: src.at[:, pl.ds(pl.multiple_of(c * width, 128), width)]


def columns_of(out, width):
    return lambda c: out.at[:, pl.ds(pl.multiple_of(c * width, 128), width)]


def deal_columns(plan, h, src, out, sems, t0, t1, relay_from, lanes=None):
    lanes = pl.ds(0, out.shape[3]) if lanes is None else lanes
    deal16(
        plan, h, columns(src, lanes.size), lambda c: out.at[c, h.core, :, lanes], lambda c, core: out.at[c, core, :, lanes],
        sems, t0, t1, relay_from=relay_from,
    )


SPREAD = ((22, 83, 140, 200), (60, 97, 160, 201), (84, 125, 190, 202))


def spread_columns(plan, h, src, out, sems, t0, t1, t2, t3):
    ys, yr, cs, cr = sems[3].at[0], sems[3].at[1], sems[3].at[2], sems[3].at[3]
    w = out.shape[5]
    deal8(
        plan, h, lambda r: src.at[:, pl.ds(pl.multiple_of(r * w, 128), w)],
        lambda r: out.at[r // 2, h.y, lax.rem(r, 2), h.core], sems[:3], t0, t1,
    )
    mine, theirs = out.at[:, h.y, :, h.core], out.at[:, 1 - h.y, :, h.core]
    over_y = remote(mine, mine, ys, yr, ctx=h.yn)
    all_mine, all_other = out.at[:, :, :, h.core], out.at[:, :, :, 1 - h.core]
    over_core = remote(all_mine, all_mine, cs, cr, fsdp=1 - h.core)
    plan.at(t1 + 0.5, over_y.start)

    def pass_on():
        remote(theirs, theirs, ys, yr, ctx=h.yn).wait_recv()
        over_core.start()

    def end():
        remote(all_other, all_other, cs, cr, fsdp=1 - h.core).wait_recv()
        over_y.wait_send()
        over_core.wait_send()

    plan.at(t2, pass_on)
    plan.at(t3, end)


def front_kernel(
    order, table, x, wq, wk, wv, wg, wu, wd, wo, cot, tile, cos, sin,
    normed, w_out, gains, qs, ks, vs, lse, low, g_out, u_out, d_out, o_out, c_out, *refs
):
    refs = list(refs)
    xg, wqkv, tiles, stage, q, k_rows, v, o, o_rows = take(refs, 9)
    stage_sem, send, recv = take(refs, 3)
    rows, width = x.shape
    h = Here()
    greet_all(h)
    plan = Plan()
    for i, src in enumerate((wq, wk, wv)):
        deal_columns(plan, h, src, wqkv, take(refs, 5), 0, 16, 10, pl.ds(i * 128, 128))
    deal16(
        plan, h, lambda c: tile, lambda c: tiles.at[c, h.core], lambda c, core: tiles.at[c, core], take(refs, 5), 0, 17,
        relay_from=11,
    )
    done = gather16(plan, h, x, xg, take(refs, 13), 0, 14, 20, by_plane=True)
    for i, (src, out) in enumerate(((wg, g_out), (wu, u_out), (wd, d_out))):
        spread_columns(plan, h, src, out, take(refs, 4), *SPREAD[i])
    gather16(plan, h, wo, o_out.at[:, h.core], take(refs, 13), 98, 10, 14)
    seen = gather8(plan, h, cot, c_out, take(refs, 7), 82.5, 18, 20)
    plan.at(185, lambda: [seen(zz) for zz in range(4)])
    to_sems = take(refs, 5)
    mine, other = o_out.at[:, h.core], o_out.at[:, 1 - h.core]
    across = remote(mine, mine, send, recv, fsdp=1 - h.core)
    plan.at(165, across.start)

    def plane(k):
        return jnp.bitwise_xor(h.z, k)

    def put_normed(k):
        at = pl.ds(pl.multiple_of(plane(k) * 4 * rows, 4 * rows), 4 * rows)
        return pltpu.make_async_copy(stage, normed.at[at], stage_sem)

    def spread_gains():
        gains[...] = jnp.zeros_like(gains)
        for c in range(16):
            both = tiles[c, 0].astype(F32) + tiles[c, 1].astype(F32)
            gains[:, c * 128 : (c + 1) * 128] = both[0:8]

    def work(k):
        zz = plane(k)
        done(zz)
        if k:
            put_normed(k - 1).wait()
        else:
            spread_gains()
        for p in range(2):
            at = pl.ds(pl.multiple_of((zz * 4 + p * 2) * rows, 2 * rows), 2 * rows)
            blocks = pl.ds(zz * 8 + p * 4, 4)
            value = xg[pl.ds(zz * 4 + p * 2, 2)].reshape(2 * rows, width).astype(F32)
            inverse = lax.rsqrt(jnp.mean(value * value, -1, keepdims=True) + EPSILON)
            value = (value * inverse * gains[0:1, :]).astype(BF)
            stage[p * 2 * rows : (p + 1) * 2 * rows, :] = value
            pre = _nn(value, wqkv[...].reshape(width, 384))
            for i, out in enumerate((q, k_rows)):
                part = pre[:, i * 128 : (i + 1) * 128]
                turned = part * cos[at, :] + swap_halves(part) * sin[at, :]
                out[blocks] = turned.astype(BF).reshape(4, 64, 128)
            v[blocks] = pre[:, 256:].astype(BF).reshape(4, 64, 128)
        put_normed(k).start()

    for k in range(4):
        plan.at((24, 42, 62, 82)[k], functools.partial(work, k))

    def sort():
        put_normed(3).wait()
        for a, b in ((q, qs), (k_rows, ks), (v, vs)):
            sort_rows(order, a, b)
        w_out[...] = wqkv[...].reshape(width, 384)

    plan.at(83, sort)
    for i in range(16 * rows // ROWS):
        plan.at(84 + 1.3 * i, functools.partial(attend_step, i, qs, ks, vs, o.reshape(16 * rows, 128), lse))

    def unsort():
        for b in range(32):
            o_rows[b // 2, (b % 2) * 64 : (b % 2 + 1) * 64, :] = o[table[b]]

    plan.at(96, unsort)
    deal16(plan, h, lambda c: o_rows.at[c], columns_of(low, 128), None, to_sems, 96.1, 200, both=False)

    def end():
        remote(other, other, send, recv, fsdp=1 - h.core).wait_recv()
        across.wait_send()

    plan.at(210, end)
    plan.run()


def front(order, table, x, wq, wk, wv, wg, wu, wd, wo, cot, tile, cos, sin):
    rows, width = x.shape
    length = 16 * rows
    block = jax.ShapeDtypeStruct((4, 2, 2, 2, wg.shape[0], wg.shape[1] // 8), BF)
    heads = jax.ShapeDtypeStruct((length, 128), BF)
    outs = (
        jax.ShapeDtypeStruct((length, width), BF), jax.ShapeDtypeStruct((width, 384), BF),
        jax.ShapeDtypeStruct((8, width), F32), heads, heads, heads, jax.ShapeDtypeStruct((2, length), F32),
        jax.ShapeDtypeStruct((rows, width), BF), block, block, block,
        jax.ShapeDtypeStruct((16, 2) + wo.shape, BF), jax.ShapeDtypeStruct((8, rows, width), BF),
    )
    smem = pl.BlockSpec(memory_space=pltpu.SMEM)
    scratch = [
        pltpu.VMEM((16, rows, width), BF), pltpu.VMEM((16, 2, wq.shape[0], 384), BF), pltpu.VMEM((16, 2) + tile.shape, BF),
        pltpu.VMEM((4 * rows, width), BF), *[pltpu.VMEM((32, 64, 128), BF)] * 4, pltpu.VMEM((16, rows, 128), BF),
        DMA, DMA, DMA,
    ]
    scratch += DEAL_SEMS * 4 + GATHER_SEMS + (DEAL8_SEMS + [DMA((4,))]) * 3 + GATHER_SEMS + GATHER8_SEMS + DEAL_SEMS
    return comm_call(
        front_kernel, outs, [ANY] + [INNER] * 6 + [ANY] * 6, [smem] * 2 + [INNER] + [ANY] * 8 + [INNER] * 3, scratch, 0,
        "front", 58,
    )(order, table, x, wq, wk, wv, wg, wu, wd, wo, cot, tile, cos, sin)


def mlp_kernel(src, cot, bg, bu, bd, gmi, out_part, sum_g, own_u, d_home, *refs):
    refs = list(refs)
    xm, ct, wg, wu, wd, grads, act, part, stage, cols = take(refs, 10)
    own_g, other_gu, got_gu, own_d, other_d, got_d, sum_d = take(refs, 7)
    w_sem, ct_sem, cols_sem, stage_sem, ex_sems = take(refs, 5)
    rows, width = src.shape
    hidden = wg.shape[1]
    block = own_d.shape[1]
    h = Here()
    loads = [pltpu.make_async_copy(a, b, w_sem.at[i]) for i, (a, b) in enumerate(((bg, wg), (bu, wu), (bd, wd)))]

    def plane(k):
        return jnp.bitwise_xor(h.z, k)

    def load_cot(k):
        return pltpu.make_async_copy(cot.at[pl.ds(plane(k) * 2, 2)], ct.at[k % 2], ct_sem.at[k % 2])

    def put_out(k):
        return pltpu.make_async_copy(stage, out_part.at[pl.ds(plane(k) * 2, 2)], stage_sem)

    for c in loads + [load_cot(0), load_cot(1)]:
        c.start()
    greet_all(h)
    plan = Plan()
    done = gather8(plan, h, src, xm, take(refs, 7), 0, 12, 12)

    def work(k):
        zz = plane(k)
        done(zz)
        if k == 0:
            for c in loads:
                c.wait()
        load_cot(k).wait()
        if k:
            put_out(k - 1).wait()
        at = pl.ds(pl.multiple_of(zz * 2 * rows, 2 * rows), 2 * rows)
        x = xm[pl.ds(zz * 2, 2)].reshape(2 * rows, width)
        gate, up = _nn(x, wg[...]), _nn(x, wu[...])
        sig = jax.nn.sigmoid(gate)
        silu = gate * sig
        low = (silu * up).astype(BF)
        act[at, :] = low
        stage[...] = _nt(low, wd[...]).astype(BF).reshape(2, rows, width)
        grad = _nn(ct[k % 2].reshape(2 * rows, width), wd[...])
        grad_gate = (grad * up * sig * (1.0 + gate * (1.0 - sig))).astype(BF)
        grad_up = (grad * silu).astype(BF)
        grads[at, pl.ds(0, hidden)] = grad_gate
        grads[at, pl.ds(hidden, hidden)] = grad_up
        back = _nt(grad_gate, wg[...]) + _nt(grad_up, wu[...])
        part[zz] = back.astype(BF).reshape(2, rows, width)
        put_out(k).start()
        if k + 2 < 4:
            load_cot(k + 2).start()

    for k in range(4):
        plan.at((15, 26, 38, 50)[k], functools.partial(work, k))
    plan.at(55, lambda: put_out(3).wait())
    scatter8(plan, h, part, gmi, take(refs, N_SCATTER8), (27, 39, 50.2, 50.3), (50.4, 58.5, 66.5, 75), 110)

    def split(c, both, own, other, lanes):
        both = both.astype(BF).reshape(2, block, both.shape[1])
        own[c] = jnp.where(h.core == 0, both[0], both[1])
        other[c, :, lanes] = jnp.where(h.core == 0, both[1], both[0])

    def exchange(i, other, got):
        return remote(other, got, ex_sems.at[i], ex_sems.at[2 + i], fsdp=1 - h.core)

    def load_cols(c):
        slot = lax.rem(c, 2)
        at = pl.ds(pl.multiple_of(c * 2 * block, 128), 2 * block)
        return pltpu.make_async_copy(cot.at[:, :, at], cols.at[slot], cols_sem.at[slot])

    def grads_gu(first):
        def one(c, carry):
            at = pl.ds(pl.multiple_of(c * 2 * block, 128), 2 * block)
            lhs = xm[:, :, at].reshape(8 * rows, 2 * block)
            split(c, _tn(lhs, grads[:, :hidden]), own_g, other_gu, pl.ds(0, hidden))
            split(c, _tn(lhs, grads[:, hidden:]), own_u, other_gu, pl.ds(hidden, hidden))
            return carry

        lax.fori_loop(first, first + 4, one, 0)

    def grads_d(first):
        def one(c, carry):
            pl.when(c < 15)(lambda: load_cols(c + 1).start())
            load_cols(c).wait()
            lhs = cols[lax.rem(c, 2)].reshape(8 * rows, 2 * block)
            split(c, _tn(lhs, act[...]), own_d, other_d, pl.ds(0, hidden))
            return carry

        lax.fori_loop(first, first + 4, one, 0)

    def over_y(i, own, result):
        own, result = own.reshape(4, 2, 2, *own.shape[1:]), result.reshape(4, 2, *own.shape[1:])
        return remote(own.at[:, 1 - h.y], result, ex_sems.at[4 + i], ex_sems.at[6 + i], ctx=h.yn)

    def join(i, own, other, got, result):
        exchange(i, other, got).wait_recv()
        for c in range(16):
            own[c] = (own[c].astype(F32) + got[c, :, 0:hidden].astype(F32)).astype(BF)
        over_y(i, own, result).start()

    def join_u():
        for c in range(16):
            own_u[c] = (own_u[c].astype(F32) + got_gu[c, :, hidden:].astype(F32)).astype(BF)

    def add_y(i, own, other, got, result):
        over_y(i, own, result).wait_recv()
        for r in range(8):
            z, x = r // 2, r % 2
            mine = jnp.where(h.y == 0, own[z * 4 + x], own[z * 4 + 2 + x])
            result[r] = (mine.astype(F32) + result[r].astype(F32)).astype(BF)

    def sent(i, own, other, got, result):
        exchange(i, other, got).wait_send()
        over_y(i, own, result).wait_send()

    d, g = (own_d, other_d, got_d, sum_d), (own_g, other_gu, got_gu, sum_g)
    plan.at(50.5, lambda: load_cols(0).start())
    for i in range(4):
        plan.at(56 + 2 * i, functools.partial(grads_d, 4 * i))
        plan.at(68 + 3 * i, functools.partial(grads_gu, 4 * i))
    plan.at(64, lambda: exchange(1, other_d, got_d).start())
    plan.at(68.5, lambda: join(1, *d))
    plan.at(82, lambda: exchange(0, other_gu, got_gu).start())
    plan.at(86, lambda: join(0, *g))
    plan.at(86.5, join_u)
    plan.at(90, lambda: add_y(1, *d))
    deal8(plan, h, lambda r: sum_d.at[r], columns_of(d_home, hidden), take(refs, 3), 90.1, 200)
    plan.at(112, lambda: add_y(0, *g))
    plan.at(201, lambda: [sent(1, *d), sent(0, *g)])
    plan.run()


def mlp(src, cot, bg, bu, bd):
    rows, width = src.shape
    block, hidden = bg.shape[4:]
    full = pltpu.VMEM((width, hidden), BF)
    gu, d = pltpu.VMEM((16, block, 2 * hidden), BF), pltpu.VMEM((16, block, hidden), BF)
    scratch = [
        pltpu.VMEM((8, rows, width), BF), pltpu.VMEM((2, 2, rows, width), BF), full, full, full,
        pltpu.VMEM((8 * rows, 2 * hidden), BF), pltpu.VMEM((8 * rows, hidden), BF),
        pltpu.VMEM((4, 2, rows, width), BF), pltpu.VMEM((2, rows, width), BF),
        pltpu.VMEM((2, 8, rows, 2 * block), BF), d, gu, gu, d, d, d,
        pltpu.VMEM((8, block, hidden), BF),
        DMA((3,)), DMA((2,)), DMA((2,)), DMA, DMA((8,)),
    ]
    scratch += GATHER8_SEMS + scatter8_scratch(rows, width) + DEAL8_SEMS
    outs = (
        jax.ShapeDtypeStruct((rows, width), F32), jax.ShapeDtypeStruct((8, rows, width), BF),
        jax.ShapeDtypeStruct((8, block, hidden), BF), jax.ShapeDtypeStruct((16, block, hidden), BF),
        jax.ShapeDtypeStruct((block, 8 * hidden), BF),
    )
    return comm_call(mlp_kernel, outs, [INNER, ANY, INNER, INNER, ANY], [ANY] * 5, scratch, 5, "mlp", 62)(
        src, cot, *(b.reshape(width, hidden) for b in (bg, bu, bd))
    )


def outer_home(plan, h, left, right, own, other, got, send, recv, t0, t1):
    rows = own.shape[1]
    over = remote(other, got, send, recv, fsdp=1 - h.core)

    def compute():
        mine, theirs = pl.multiple_of(h.core * rows, rows), pl.multiple_of((1 - h.core) * rows, rows)
        for c in range(16):
            lhs = left[:, c * 2 * rows : (c + 1) * 2 * rows]
            both = _tn(lhs, right[...]).astype(BF).reshape(2, rows, right.shape[1])
            own[c] = jnp.where(h.core == 0, both[0], both[1])
            other[c] = jnp.where(h.core == 0, both[1], both[0])
        over.start()

    def add():
        over.wait_recv()
        for c in range(16):
            own[c] = (own[c].astype(F32) + got[c].astype(F32)).astype(BF)
        over.wait_send()

    plan.at(t0, compute)
    plan.at(t1, add)


def back_kernel(order, table, ga, qs, ks, vs, lse, cos, sin, out_part, low, branch, sum_g, own_u, dqkv, out_sum, wo_sum, sum_u, g_home, *refs):
    refs = list(refs)
    gh, gs, dq, dk, dv, own, other, got = take(refs, 8)
    send, recv = take(refs, 2)
    gh_rows = gh.reshape(16, ga.shape[0], 128)
    flat = [g.reshape(qs.shape) for g in (dq, dk, dv)]
    h = Here()
    greet_all(h)
    plan = Plan()
    deal16(plan, h, columns(ga, 128), lambda c: gh_rows.at[c], None, take(refs, 5), 0, 14, both=False)
    gu_sems = take(refs, 3)
    scatter8(plan, h, out_part, out_sum, take(refs, N_SCATTER8), (1, 18, 35, 52), (18.8, 35.8, 52.8, 69.8), 94)
    outer_home(plan, h, low, branch, own, other, got, send, recv, 2, 8)
    deal8(plan, h, lambda r: sum_g.at[r], columns_of(g_home, sum_g.shape[2]), gu_sems, 3, 198)
    half_u, u_sems = take(refs, 2)
    split_u = own_u.reshape(4, 2, 2, *own_u.shape[1:])
    over_u = remote(split_u.at[:, 1 - h.y], sum_u, u_sems.at[0], u_sems.at[1], ctx=h.yn)
    keep_u = pltpu.make_async_copy(split_u.at[:, h.y], half_u, u_sems.at[2])

    def start_u():
        over_u.start()
        keep_u.start()

    def end_u():
        over_u.wait_recv()
        keep_u.wait()
        for z in range(4):
            sum_u[z] = (sum_u[z].astype(F32) + half_u[z].astype(F32)).astype(BF)
        over_u.wait_send()

    plan.at(2.5, start_u)
    plan.at(90, end_u)
    scatter16(plan, h, own.reshape(4, 2, 2, *own.shape[1:]), wo_sum, take(refs, N_SCATTER), 8.1, 18)

    def begin():
        sort_rows(order, gh, gs)
        dk[...] = jnp.zeros_like(dk)
        dv[...] = jnp.zeros_like(dv)

    plan.at(15, begin)
    for i in range(qs.shape[0] // ROWS):
        plan.at(16 + 2.2 * i, functools.partial(back_step, i, qs, ks, vs, gs, lse, *flat))

    def end():
        for b in range(32):
            rows = slice(b * 64, (b + 1) * 64)
            for i, grad in enumerate((dq, dk)):
                value = grad[table[b]]
                turned = swap_halves(value)
                dqkv[rows, i * 128 : (i + 1) * 128] = (value * cos[rows, :] - turned * sin[rows, :]).astype(BF)
            dqkv[rows, 256:] = dv[table[b]].astype(BF)

    plan.at(34.5, end)
    plan.run()


def back(order, table, ga, qs, ks, vs, lse, cos, sin, out_part, low, branch, sum_g, own_u):
    rows, width = ga.shape
    length = qs.shape[0]
    smem = pl.BlockSpec(memory_space=pltpu.SMEM)
    half = pltpu.VMEM((16, width // 32, width), BF)
    outs = (
        jax.ShapeDtypeStruct((length, 384), BF),
        jax.ShapeDtypeStruct((rows, width), F32),
        jax.ShapeDtypeStruct((width // 32, width), F32),
        jax.ShapeDtypeStruct((4, 2) + sum_g.shape[1:], BF),
        jax.ShapeDtypeStruct((sum_g.shape[1], 8 * sum_g.shape[2]), BF),
    )
    scratch = [pltpu.VMEM((32, 64, 128), BF), pltpu.VMEM((length, 128), BF)]
    scratch += [pltpu.VMEM((32, 64, 128), F32)] * 3 + [half] * 3 + [DMA] * 2 + DEAL_SEMS + DEAL8_SEMS
    scratch += scatter8_scratch(rows, width) + [pltpu.VMEM((4, 2) + sum_g.shape[1:], BF), DMA((3,))]
    scratch += scatter_scratch(width // 32, width)
    return comm_call(back_kernel, outs, [INNER] * 4 + [ANY], [smem] * 2 + [INNER] * 10 + [ANY] * 2, scratch, 6, "back", 60)(
        order, table, ga, qs, ks, vs, lse, cos, sin, out_part.reshape(4, 2, rows, width), low, branch, sum_g, own_u
    )


def home_kernel(
    dqkv, wqkv, normed, gd, gg, gu, x, grad_hidden, gain, other_gain,
    input_grad, q_out, k_out, v_out, gains_out, d_out, g_out, u_out, *refs
):
    refs = list(refs)
    part, nm, own, other, got, landed, d32, g32, u16, u32, gn, gains, gains_got, gains_landed = take(refs, 14)
    nm_sem, ex_sems, out_sems, gain_sems = take(refs, 4)
    rows, width = x.shape
    block = own.shape[1]
    h = Here()
    load = pltpu.make_async_copy(normed, nm, nm_sem)
    load.start()
    greet_all(h)
    plan = Plan()
    deal8(plan, h, lambda r: gu.at[r], columns_of(u16, gu.shape[2]), take(refs, 3), 0.4, 150)

    def plane(k):
        zz = jnp.bitwise_xor(h.z, k)
        for p in range(2):
            at = pl.ds(pl.multiple_of((zz * 4 + p * 2) * rows, 2 * rows), 2 * rows)
            part[zz, pl.ds(p, 1)] = _nt(dqkv[at, :], wqkv[...]).astype(BF).reshape(1, 2, rows, width)

    for i, k in enumerate((1, 2, 3, 0)):
        plan.at((0.1, 1, 2, 3)[i], functools.partial(plane, k))
    scatter16(plan, h, part, gn, take(refs, N_SCATTER), 0.2, 20)
    plan.at(4, load.wait)

    def grads(first):
        def one(c, carry):
            at = pl.ds(pl.multiple_of(c * 2 * block, 128), 2 * block)
            both = _tn(nm[:, at], dqkv[...]).astype(BF).reshape(2, block, 384)
            own[c] = jnp.where(h.core == 0, both[0], both[1])
            other[c] = jnp.where(h.core == 0, both[1], both[0])
            return carry

        lax.fori_loop(first, first + 4, one, 0)

    for i in range(4):
        plan.at(4.1 + i, functools.partial(grads, 4 * i))
    over = remote(other, got, ex_sems.at[0], ex_sems.at[1], fsdp=1 - h.core)
    plan.at(8, over.start)

    def join():
        over.wait_recv()
        for c in range(16):
            own[c] = (own[c].astype(F32) + got[c].astype(F32)).astype(BF)
        over.wait_send()

    plan.at(10, join)
    deal16(plan, h, lambda c: own.at[c], lambda c: landed.at[c], None, take(refs, 5), 10.1, 151, both=False)
    writes = [
        pltpu.make_async_copy(a, b, out_sems.at[i]) for i, (a, b) in enumerate(((d32, d_out), (g32, g_out), (u32, u_out)))
    ]

    def widen(i, source, target):
        target[...] = source[...].astype(F32)
        writes[i].start()

    plan.at(15, functools.partial(widen, 0, gd, d32))
    plan.at(25, functools.partial(widen, 1, gg, g32))
    plan.at(152, functools.partial(widen, 2, u16, u32))

    def finish_qkv():
        for c in range(16):
            for i, out in enumerate((q_out, k_out, v_out)):
                out[:, c * 128 : (c + 1) * 128] = landed[c, :, i * 128 : (i + 1) * 128].astype(F32)

    plan.at(203, finish_qkv)
    gain_over = remote(gains, gains_got, ex_sems.at[2], ex_sems.at[3], fsdp=1 - h.core)

    def source():
        value = x[...].astype(F32)
        return value, lax.rsqrt(jnp.mean(value * value, -1, keepdims=True) + EPSILON)

    def sums():
        value, inverse = source()
        gains[...] = jnp.zeros_like(gains)
        total = jnp.sum(gn[...] * value * inverse, 0, keepdims=True)
        for c in range(16):
            at = slice(c * 128, (c + 1) * 128)
            gains[c, 0:1] = total[:, at]
            gains[c, 1:2] = other_gain[:, at]
        gain_over.start()

    def pass_on():
        gain_over.wait_recv()
        gain_over.wait_send()
        gains[...] += gains_got[...]

    def result():
        value, inverse = source()
        scaled = gn[...] * gain[0:1, :]
        inner = jnp.sum(scaled * value, -1, keepdims=True)
        input_grad[...] = (
            grad_hidden[...] + inverse * scaled - inverse * inverse * inverse / width * value * inner
        )

    plan.at(200, sums)
    plan.at(201, pass_on)
    deal16(plan, h, lambda c: gains.at[c], lambda c: gains_landed.at[c], None, take(refs, 5), 201.5, 204, both=False)
    plan.at(202, result)

    def add():
        total = gains_landed[0]
        for c in range(1, 16):
            total = total + gains_landed[c]
        gains_out[...] = total
        for w in writes:
            w.wait()

    plan.at(300, add)
    plan.run()


def home(dqkv, wqkv, normed, gd, gg, gu, x, grad_hidden, gain, other_gain):
    rows, width = x.shape
    block, wide = gd.shape
    third = pltpu.VMEM((16, block, 384), BF)
    tile = pltpu.VMEM((16, 8, 128), F32)
    wide32 = pltpu.VMEM((block, wide), F32)
    small = jax.ShapeDtypeStruct((block, width), F32)
    large = jax.ShapeDtypeStruct((block, wide), F32)
    outs = (
        jax.ShapeDtypeStruct((rows, width), F32), small, small, small, jax.ShapeDtypeStruct((8, 128), F32), large, large, large
    )
    scratch = [
        pltpu.VMEM((4, 2, 2, rows, width), BF), pltpu.VMEM(normed.shape, BF), third, third, third, third, wide32, wide32,
        pltpu.VMEM((block, wide), BF), wide32, pltpu.VMEM((rows, width), F32), tile, tile, tile,
        DMA, DMA((4,)), DMA((3,)), DMA,
    ]
    scratch += DEAL8_SEMS + scatter_scratch(rows, width) + DEAL_SEMS * 2
    return comm_call(
        home_kernel, outs, [INNER] * 5 + [ANY] * 3, [INNER, INNER, ANY, INNER, INNER, ANY] + [INNER] * 4, scratch, 7, "home", 60
    )(dqkv, wqkv, normed, gd, gg, gu, x, grad_hidden, gain, other_gain)


def rope_tables(positions):
    inv_freq = THETA_BASE ** (-(jnp.arange(HD // 2, dtype=F32) * 2.0 / HD))
    angles = positions.astype(F32)[:, None] * inv_freq[None, :]
    return jnp.tile(jnp.cos(angles), (1, 4)), jnp.tile(jnp.sin(angles), (1, 4))


def swap(values):
    a, b, c, d = jnp.split(values, 4, -1)
    return jnp.concatenate([b, a, d, c], -1)


def fast_body(x, table, attn_gain, wq, wk, wv, wo, mlp_gain, wg, wu, wd, cot):
    x, cot, table = x[0], cot[0], table[0].reshape(32)
    rows, width = x.shape
    length = rows * 16
    core = lax.axis_index("fsdp")
    slots = jnp.arange(32, dtype=jnp.int32)
    order = jnp.sum(jnp.where(table[None, :] == slots[:, None], slots[None, :], 0), 1)
    positions = (table[:, None] * 64 + jnp.arange(64, dtype=jnp.int32)[None]).reshape(length)
    cos, sin = rope_tables(positions)
    turn = jnp.where(jnp.arange(128) % 64 < 32, -1.0, 1.0).astype(F32)
    sin = sin * turn

    def dot(a, b):
        return jnp.dot(a, b, preferred_element_type=F32)

    def dot_nt(a, b):
        return lax.dot_general(a, b, (((1,), (1,)), ((), ())), preferred_element_type=F32)

    def dot_tn(a, b):
        return lax.dot_general(a, b, (((0,), (0,)), ((), ())), preferred_element_type=F32)

    lane = jnp.arange(128) // 64
    tile = jnp.where(lane[None] == core, jnp.tile(jnp.stack([attn_gain, mlp_gain]), (1, 2)), 0)
    tile = jnp.pad(tile, ((0, 14), (0, 0)))
    normed, wqkv, gains, qs, ks, vs, lse, attn_low, bg, bu, bd, full_out, cot_all = front(
        order, table, x, wq, wk, wv, wg, wu, wd, wo, cot, tile, cos, sin
    )
    again, mgain = gains[0], gains[1]
    full_out = full_out.reshape(width, width)
    own = x.astype(F32)
    inv_in = lax.rsqrt(jnp.mean(own * own, -1, keepdims=True) + EPSILON)
    hidden = own + dot(attn_low, full_out)
    inv_mid = lax.rsqrt(jnp.mean(hidden * hidden, -1, keepdims=True) + EPSILON)
    gmi, out_part, sum_g, own_u, gd = mlp((hidden * inv_mid * mgain).astype(BF), cot_all, bg, bu, bd)

    def norm_back(grad, source, inv, gain):
        scaled = grad * gain
        inner = jnp.sum(scaled * source, -1, keepdims=True)
        return inv * scaled - inv * inv * inv / width * source * inner

    mgain_part = jnp.sum(gmi * hidden * inv_mid, 0)
    grad_hidden = cot.astype(F32) + norm_back(gmi, hidden, inv_mid, mgain)
    grad_branch = grad_hidden.astype(BF)
    grad_att = dot_nt(grad_branch, full_out).astype(BF)
    grad_qkv, out_sum, wo_grad, sum_u, gg = back(
        order, table, grad_att, qs, ks, vs, lse, cos, sin, out_part, attn_low, grad_branch, sum_g, own_u
    )
    layer_output = (hidden + out_sum).astype(BF)
    input_grad, gq, gk, gv, both, gd, gg, gu = home(
        grad_qkv, wqkv, normed, gd, gg, sum_u.reshape(sum_g.shape), x, grad_hidden, gains, mgain_part[None]
    )
    gains = lax.dynamic_slice_in_dim(both, core * 64, 64, 1)
    return (layer_output[None], input_grad[None], gains[0], gq, gk, gv, wo_grad, gains[1], gg, gu, gd)


MASKED = -1e30


def general_tables(positions):
    inv_freq = THETA_BASE ** (-(jnp.arange(HD // 2, dtype=jnp.float32) * 2.0 / HD))
    angles = positions.astype(jnp.float32)[:, None] * inv_freq[None, :]
    cosine = jnp.cos(angles)
    sine_tab = jnp.sin(angles)
    return (jnp.concatenate([cosine, cosine], -1), jnp.concatenate([sine_tab, sine_tab], -1))


def rotate(values, cosine, sine_tab):
    middle = values.shape[-1] // 2
    turned = jnp.concatenate([-values[..., middle:], values[..., :middle]], -1)
    return values * cosine[:, None, :] + turned * sine_tab[:, None, :]


def rotate_back(grads_in, cosine, sine_tab):
    middle = grads_in.shape[-1] // 2
    shifted = grads_in * sine_tab[:, None, :]
    turned = jnp.concatenate([shifted[..., middle:], -shifted[..., :middle]], -1)
    return grads_in * cosine[:, None, :] + turned


def inverse_rms(rows_in):
    return lax.rsqrt(jnp.mean(rows_in * rows_in, -1, keepdims=True) + EPSILON)


def general_norm_back(grad_normed, rows_in, inverse, gain_vec):
    scaled = grad_normed * gain_vec
    inner_sum = jnp.sum(scaled * rows_in, -1, keepdims=True)
    return inverse * scaled - inverse * inverse * inverse / rows_in.shape[-1] * rows_in * inner_sum


def score_rows(query_rows, key_rows, query_pos, key_pos):
    scores = jnp.einsum(
        "qhd,khd->hqk", query_rows, key_rows, preferred_element_type=jnp.float32
    ) * HD ** (-0.5)
    visible = key_pos[None, None, :] <= query_pos[None, :, None]
    return (scores, visible)


def softmax_rows(scores, visible, log_total):
    return jnp.where(
        visible, jnp.exp(jnp.where(visible, scores - log_total[..., None], MASKED)), 0.0
    )


def walk_keys(kv_steps, top_pos, width, step_fn, initial):
    step_rows = kv_steps.shape[1]
    offsets = jnp.arange(step_rows, dtype=jnp.int32)

    def advance(carried, step_item):
        step_index, kv_block = step_item
        first_key = step_index * step_rows
        key_rows = kv_block[:, :width].reshape(step_rows, HEADS, HD)
        value_rows = kv_block[:, width:].reshape(step_rows, HEADS, HD)
        key_pos = first_key + offsets
        updated = lax.cond(
            first_key <= top_pos,
            lambda state: step_fn(state, key_rows, value_rows, key_pos),
            lambda state: state,
            carried,
        )
        return (updated, None)

    indices = jnp.arange(kv_steps.shape[0], dtype=jnp.int32)
    final_state, ignored = lax.scan(advance, initial, (indices, kv_steps))
    return final_state


def general_body(
    layer_input,
    block_table,
    attn_gain,
    query_weight,
    key_weight,
    value_weight,
    out_weight,
    mlp_gain,
    gate_weight,
    up_weight,
    down_weight,
    cotangent,
):
    tokens = layer_input.shape[1]
    width = layer_input.shape[2]
    half_rows = tokens // 2
    ranks = lax.axis_size("ctx")
    length = tokens * ranks
    score_scale = HD ** (-0.5)
    block_ids = block_table[0].reshape(2 * ranks)
    own_blocks = lax.dynamic_slice_in_dim(block_ids, lax.axis_index("ctx") * 2, 2)
    inner = jnp.arange(half_rows, dtype=jnp.int32)
    query_pos = (own_blocks[:, None] * half_rows + inner[None, :]).reshape(tokens)
    cosine, sine_tab = general_tables(query_pos)
    full_query, full_key, full_value, full_out, full_attn_gain = (
        lax.all_gather(query_weight, ("ctx", "fsdp"), axis=0, tiled=True),
        lax.all_gather(key_weight, ("ctx", "fsdp"), axis=0, tiled=True),
        lax.all_gather(value_weight, ("ctx", "fsdp"), axis=0, tiled=True),
        lax.all_gather(out_weight, ("ctx", "fsdp"), axis=0, tiled=True),
        lax.all_gather(attn_gain, ("ctx", "fsdp"), axis=0, tiled=True),
    )
    source = layer_input[0].astype(jnp.float32)
    inverse_in = inverse_rms(source)
    normed = (source * inverse_in * full_attn_gain.astype(jnp.float32)).astype(jnp.bfloat16)
    query_pre = jnp.dot(normed, full_query, preferred_element_type=jnp.float32).reshape(
        tokens, HEADS, HD
    )
    key_pre = jnp.dot(normed, full_key, preferred_element_type=jnp.float32).reshape(
        tokens, HEADS, HD
    )
    value_low = jnp.dot(normed, full_value, preferred_element_type=jnp.float32).astype(jnp.bfloat16)
    queries = rotate(query_pre, cosine, sine_tab).astype(jnp.bfloat16)
    keys_low = rotate(key_pre, cosine, sine_tab).astype(jnp.bfloat16).reshape(tokens, width)
    kv_dev = lax.all_gather(jnp.concatenate([keys_low, value_low], 1), "ctx", axis=0, tiled=True)
    slot_ids = jnp.arange(2 * ranks, dtype=jnp.int32)
    holder = jnp.sum(jnp.where(block_ids[None, :] == slot_ids[:, None], slot_ids[None, :], 0), 1)
    chosen = (holder[:, None] == slot_ids[None, :]).astype(jnp.bfloat16)
    kv_seq = jnp.einsum(
        "ab,bn->an", chosen, kv_dev.reshape(2 * ranks, half_rows * 2 * width)
    ).reshape(length, 2 * width)
    step_rows = min(512, length)
    kv_steps = kv_seq.reshape(length // step_rows, step_rows, 2 * width)
    log_totals = []
    attended_parts = []
    top_list = []
    for slot_index in range(2):
        slot_queries = queries[slot_index * half_rows : (slot_index + 1) * half_rows]
        slot_pos = query_pos[slot_index * half_rows : (slot_index + 1) * half_rows]
        top_pos = own_blocks[slot_index] * half_rows + half_rows - 1
        top_list.append(top_pos)

        def stat_step(state, key_rows, value_rows, key_pos):
            running, running_sum = state
            scores, visible = score_rows(slot_queries, key_rows, slot_pos, key_pos)
            scores = jnp.where(visible, scores, MASKED)
            newest = jnp.maximum(running, jnp.max(scores, -1))
            running_sum = running_sum * jnp.exp(running - newest) + jnp.sum(
                jnp.where(visible, jnp.exp(scores - newest[..., None]), 0.0), -1
            )
            return (newest, running_sum)

        start_state = (
            jnp.full((HEADS, half_rows), MASKED, jnp.float32),
            jnp.zeros((HEADS, half_rows), jnp.float32),
        )
        running, running_sum = walk_keys(kv_steps, top_pos, width, stat_step, start_state)
        log_total = running + jnp.log(running_sum)

        def value_step(accumulated, key_rows, value_rows, key_pos):
            scores, visible = score_rows(slot_queries, key_rows, slot_pos, key_pos)
            weights_low = softmax_rows(scores, visible, log_total).astype(jnp.bfloat16)
            return accumulated + jnp.einsum(
                "hqk,khd->qhd", weights_low, value_rows, preferred_element_type=jnp.float32
            )

        attended_parts.append(
            walk_keys(
                kv_steps, top_pos, width, value_step, jnp.zeros((half_rows, HEADS, HD), jnp.float32)
            )
        )
        log_totals.append(log_total)
    attended = jnp.concatenate(attended_parts, 0)
    log_all = jnp.concatenate(log_totals, 1)
    attn_low = attended.reshape(tokens, width).astype(jnp.bfloat16)
    hidden = source + jnp.dot(attn_low, full_out, preferred_element_type=jnp.float32)
    full_gate, full_up, full_down, full_mlp_gain = (
        lax.all_gather(gate_weight, ("ctx", "fsdp"), axis=0, tiled=True),
        lax.all_gather(up_weight, ("ctx", "fsdp"), axis=0, tiled=True),
        lax.all_gather(down_weight, ("ctx", "fsdp"), axis=0, tiled=True),
        lax.all_gather(mlp_gain, ("ctx", "fsdp"), axis=0, tiled=True),
    )
    inverse_mid = inverse_rms(hidden)
    mlp_in = (hidden * inverse_mid * full_mlp_gain.astype(jnp.float32)).astype(jnp.bfloat16)
    gate_pre = jnp.dot(mlp_in, full_gate, preferred_element_type=jnp.float32)
    up_pre = jnp.dot(mlp_in, full_up, preferred_element_type=jnp.float32)
    activation = (jax.nn.silu(gate_pre) * up_pre).astype(jnp.bfloat16)
    branch_mlp = jnp.einsum("tf,df->td", activation, full_down, preferred_element_type=jnp.float32)
    layer_output = (hidden + branch_mlp).astype(jnp.bfloat16)
    back_gate, back_up, back_down, back_mlp_gain = (
        lax.all_gather(gate_weight, ("ctx", "fsdp"), axis=0, tiled=True),
        lax.all_gather(up_weight, ("ctx", "fsdp"), axis=0, tiled=True),
        lax.all_gather(down_weight, ("ctx", "fsdp"), axis=0, tiled=True),
        lax.all_gather(mlp_gain, ("ctx", "fsdp"), axis=0, tiled=True),
    )
    grad_out_low = cotangent[0]
    grad_act = jnp.dot(grad_out_low, back_down, preferred_element_type=jnp.float32)
    sigmoid_gate = jax.nn.sigmoid(gate_pre)
    grad_gate = (grad_act * up_pre * sigmoid_gate * (1.0 + gate_pre * (1.0 - sigmoid_gate))).astype(
        jnp.bfloat16
    )
    grad_up = (grad_act * gate_pre * sigmoid_gate).astype(jnp.bfloat16)
    grad_mlp_in = jnp.einsum(
        "tf,df->td", grad_gate, back_gate, preferred_element_type=jnp.float32
    ) + jnp.einsum("tf,df->td", grad_up, back_up, preferred_element_type=jnp.float32)
    mlp_gain_term = jnp.sum(grad_mlp_in * hidden * inverse_mid, 0)
    grad_hidden = grad_out_low.astype(jnp.float32) + general_norm_back(
        grad_mlp_in, hidden, inverse_mid, back_mlp_gain.astype(jnp.float32)
    )
    grad_branch = grad_hidden.astype(jnp.bfloat16)
    back_query, back_key, back_value, back_out, back_attn_gain = (
        lax.all_gather(query_weight, ("ctx", "fsdp"), axis=0, tiled=True),
        lax.all_gather(key_weight, ("ctx", "fsdp"), axis=0, tiled=True),
        lax.all_gather(value_weight, ("ctx", "fsdp"), axis=0, tiled=True),
        lax.all_gather(out_weight, ("ctx", "fsdp"), axis=0, tiled=True),
        lax.all_gather(attn_gain, ("ctx", "fsdp"), axis=0, tiled=True),
    )
    grad_attended = (
        jnp.einsum("te,de->td", grad_branch, back_out, preferred_element_type=jnp.float32)
        .astype(jnp.bfloat16)
        .reshape(tokens, HEADS, HD)
    )
    delta_all = jnp.sum(grad_attended.astype(jnp.float32) * attended, -1).T
    grad_query_parts = []
    for slot_index in range(2):
        slot_queries = queries[slot_index * half_rows : (slot_index + 1) * half_rows]
        slot_pos = query_pos[slot_index * half_rows : (slot_index + 1) * half_rows]
        slot_grad_out = grad_attended[slot_index * half_rows : (slot_index + 1) * half_rows]
        slot_delta = delta_all[:, slot_index * half_rows : (slot_index + 1) * half_rows]
        slot_log = log_totals[slot_index]

        def query_step(accumulated, key_rows, value_rows, key_pos):
            scores, visible = score_rows(slot_queries, key_rows, slot_pos, key_pos)
            weights_full = softmax_rows(scores, visible, slot_log)
            grad_weights = jnp.einsum(
                "qhd,khd->hqk", slot_grad_out, value_rows, preferred_element_type=jnp.float32
            )
            grad_scores = (weights_full * (grad_weights - slot_delta[..., None])).astype(
                jnp.bfloat16
            )
            return accumulated + jnp.einsum(
                "hqk,khd->qhd", grad_scores, key_rows, preferred_element_type=jnp.float32
            )

        grad_query_parts.append(
            walk_keys(
                kv_steps,
                top_list[slot_index],
                width,
                query_step,
                jnp.zeros((half_rows, HEADS, HD), jnp.float32),
            )
        )
    grad_queries = jnp.concatenate(grad_query_parts, 0) * score_scale
    grad_query_low = (
        rotate_back(grad_queries, cosine, sine_tab).reshape(tokens, width).astype(jnp.bfloat16)
    )
    bottom_key = jnp.min(query_pos)
    query_both = lax.all_gather(
        jnp.concatenate([queries.reshape(tokens, width), grad_attended.reshape(tokens, width)], 1),
        "ctx",
        axis=0,
        tiled=True,
    )
    stats_both = lax.all_gather(
        jnp.stack([log_all.T, delta_all.T], 1).astype(jnp.bfloat16), "ctx", axis=0, tiled=True
    ).astype(jnp.float32)
    all_pos = (block_ids[:, None] * half_rows + inner[None, :]).reshape(length)
    own_keys = keys_low.reshape(tokens, HEADS, HD)
    own_values = value_low.reshape(tokens, HEADS, HD)

    def gather_step(carried, piece_index):
        first = piece_index * step_rows
        piece_pos = lax.dynamic_slice_in_dim(all_pos, first, step_rows)

        def live_piece(state):
            rows_here = lax.dynamic_slice_in_dim(query_both, first, step_rows, 0)
            stats_here = lax.dynamic_slice_in_dim(stats_both, first, step_rows, 0)
            piece_queries = rows_here[:, :width].reshape(step_rows, HEADS, HD)
            piece_grads = rows_here[:, width:].reshape(step_rows, HEADS, HD)
            piece_log = stats_here[:, 0, :].T
            piece_delta = stats_here[:, 1, :].T
            scores, visible = score_rows(piece_queries, own_keys, piece_pos, query_pos)
            weights_full = softmax_rows(scores, visible, piece_log)
            grad_weights = jnp.einsum(
                "qhd,khd->hqk", piece_grads, own_values, preferred_element_type=jnp.float32
            )
            grad_scores = (weights_full * (grad_weights - piece_delta[..., None])).astype(
                jnp.bfloat16
            )
            grad_keys = (
                jnp.einsum(
                    "hqk,qhd->khd", grad_scores, piece_queries, preferred_element_type=jnp.float32
                )
                * score_scale
            )
            grad_values = jnp.einsum(
                "hqk,qhd->khd",
                weights_full.astype(jnp.bfloat16),
                piece_grads,
                preferred_element_type=jnp.float32,
            )
            return (state[0] + grad_keys, state[1] + grad_values)

        updated = lax.cond(
            jnp.max(piece_pos) >= bottom_key, live_piece, lambda state: state, carried
        )
        return (updated, None)

    start_grads = (
        jnp.zeros((tokens, HEADS, HD), jnp.float32),
        jnp.zeros((tokens, HEADS, HD), jnp.float32),
    )
    summed, ignored = lax.scan(
        gather_step, start_grads, jnp.arange(length // step_rows, dtype=jnp.int32)
    )
    kv_grads = jnp.concatenate(
        [summed[0].reshape(tokens, width), summed[1].reshape(tokens, width)], 1
    )
    grad_key_low = (
        rotate_back(kv_grads[:, :width].reshape(tokens, HEADS, HD), cosine, sine_tab)
        .reshape(tokens, width)
        .astype(jnp.bfloat16)
    )
    grad_value_low = kv_grads[:, width:].astype(jnp.bfloat16)
    grad_normed = jnp.einsum(
        "te,de->td", grad_query_low, back_query, preferred_element_type=jnp.float32
    )
    grad_normed = grad_normed + jnp.einsum(
        "te,de->td", grad_key_low, back_key, preferred_element_type=jnp.float32
    )
    grad_normed = grad_normed + jnp.einsum(
        "te,de->td", grad_value_low, back_value, preferred_element_type=jnp.float32
    )
    attn_gain_term = jnp.sum(grad_normed * source * inverse_in, 0)
    input_grad = grad_hidden + general_norm_back(
        grad_normed, source, inverse_in, back_attn_gain.astype(jnp.float32)
    )

    def outer_sum(left_side, right_side):
        return jnp.einsum("tc,te->ce", left_side, right_side, preferred_element_type=jnp.float32)

    weight_grads = lax.psum_scatter(
        jnp.concatenate(
            [
                outer_sum(normed, grad_query_low),
                outer_sum(normed, grad_key_low),
                outer_sum(normed, grad_value_low),
                outer_sum(attn_low, grad_branch),
                outer_sum(mlp_in, grad_gate),
                outer_sum(mlp_in, grad_up),
                outer_sum(grad_out_low, activation),
            ],
            1,
        ),
        ("ctx", "fsdp"),
        scatter_dimension=0,
        tiled=True,
    )
    gain_grads = lax.psum_scatter(
        jnp.stack([attn_gain_term, mlp_gain_term], 1),
        ("ctx", "fsdp"),
        scatter_dimension=0,
        tiled=True,
    )
    hidden_units = gate_weight.shape[1]
    edge_attn = 4 * width
    return (
        layer_output[None],
        input_grad[None],
        gain_grads[:, 0],
        weight_grads[:, 0:width],
        weight_grads[:, width : 2 * width],
        weight_grads[:, 2 * width : 3 * width],
        weight_grads[:, 3 * width : edge_attn],
        gain_grads[:, 1],
        weight_grads[:, edge_attn : edge_attn + hidden_units],
        weight_grads[:, edge_attn + hidden_units : edge_attn + 2 * hidden_units],
        weight_grads[:, edge_attn + 2 * hidden_units : edge_attn + 3 * hidden_units],
    )


def solution(mesh):
    both = ("ctx", "fsdp")
    rows = P(both, None)
    tokens = P("fsdp", "ctx", None)
    return jax.shard_map(
        fast_body if mesh.shape["ctx"] == 16 and mesh.shape["fsdp"] == 2 else general_body,
        mesh=mesh,
        in_specs=(tokens, P("fsdp", None, None), P(both), rows, rows, rows, rows, P(both), rows, rows, rows, tokens),
        out_specs=(tokens, tokens, P(both), rows, rows, rows, rows, P(both), rows, rows, rows),
        check_vma=False,
    )
```

```python
import functools
import jax, jax.numpy as jnp
from jax import lax
from jax.experimental import pallas as pl
from jax.experimental.pallas import tpu as pltpu

MESH = pl.DeviceIdType.MESH
DMA = pltpu.SemaphoreType.DMA
BF = jnp.bfloat16
F32 = jnp.float32


class Plan:
    def __init__(self):
        self.steps = []

    def at(self, when, step):
        self.steps.append((when, len(self.steps), step))

    def run(self):
        for _, _, step in sorted(self.steps, key=lambda s: s[:2]):
            step()


class Here:
    def __init__(self):
        self.me = lax.axis_index("ctx")
        self.core = lax.axis_index("fsdp")
        self.z = self.me // 4
        self.y = lax.rem(self.me // 2, 2)
        self.x = lax.rem(self.me, 2)
        self.xy = lax.rem(self.me, 4)
        self.xn = self.me + 1 - 2 * self.x
        self.yn = self.me + 2 - 4 * self.y


def remote(src, dst, send_sem, recv_sem, **device):
    return pltpu.make_async_remote_copy(
        src_ref=src, dst_ref=dst, send_sem=send_sem, recv_sem=recv_sem, device_id=device, device_id_type=MESH
    )


def greet_all(h):
    barrier = pltpu.get_barrier_semaphore()
    for step in range(1, 16):
        pl.semaphore_signal(barrier, inc=1, device_id={"ctx": jnp.bitwise_xor(h.me, step)}, device_id_type=MESH)
    pl.semaphore_signal(barrier, inc=1, device_id={"fsdp": 1 - h.core}, device_id_type=MESH)
    pl.semaphore_wait(barrier, 16)


GATHER_SEMS = [DMA((4,))] * 12 + [DMA]


def gather16(plan, h, src, out, sems, t0, tz, tx, by_plane=False):
    us, ur, ds, dr, xs, xr, ys, yr, xfs, xfr, yfs, yfr, own = sems
    half = src.shape[0] // 2

    def plane(zz, source=None):
        s = zz * 4 + h.xy
        source = out.at[s] if source is None else source
        return (
            remote(source, out.at[s], xs.at[zz], xr.at[zz], ctx=h.xn),
            remote(source, out.at[s], ys.at[zz], yr.at[zz], ctx=h.yn),
        )

    def across(zz):
        sx = zz * 4 + lax.rem(h.xn, 4)
        sy = zz * 4 + lax.rem(h.yn, 4)
        top, low = pl.ds(0, half), pl.ds(half, half)
        return (
            remote(out.at[sx, top], out.at[sx, top], yfs.at[zz], yfr.at[zz], ctx=h.yn),
            remote(out.at[sy, low], out.at[sy, low], xfs.at[zz], xfr.at[zz], ctx=h.xn),
        )

    def arrived(zz):
        sx = zz * 4 + lax.rem(h.xn, 4)
        sy = zz * 4 + lax.rem(h.yn, 4)
        return (
            remote(out.at[sx], out.at[sx], xs.at[zz], xr.at[zz], ctx=h.xn),
            remote(out.at[sy], out.at[sy], ys.at[zz], yr.at[zz], ctx=h.yn),
        )

    def hop(k, up, source=None):
        it = (h.z - k if up else h.z + k) * 4 + h.xy
        send, recv = (us, ur) if up else (ds, dr)
        source = out.at[it] if source is None else source
        to = h.me + 4 if up else h.me - 4
        return remote(source, out.at[it], send.at[k], recv.at[k + 1], ctx=to)

    def landed(k, up):
        it = (h.z - k if up else h.z + k) * 4 + h.xy
        send, recv = (us, ur) if up else (ds, dr)
        return remote(out.at[it], out.at[it], send.at[k - 1], recv.at[k], ctx=h.me)

    local = pltpu.make_async_copy(src, out.at[h.me], own)

    def first():
        pl.when(h.z < 3)(lambda: hop(0, True, src).start())
        pl.when(h.z > 0)(lambda: hop(0, False, src).start())
        for c in plane(h.z, src):
            c.start()
        local.start()

    plan.at(t0, first)

    def step(k, up):
        def go():
            landed(k, up).wait_recv()
            if k < 3:
                pl.when((h.z < 3) if up else (h.z > 0))(lambda: hop(k, up).start())
            for c in plane(h.z - k if up else h.z + k):
                c.start()

        pl.when((h.z >= k) if up else (h.z + k <= 3))(go)

    def forward(zz):
        got, on = arrived(zz), across(zz)
        for g, c in zip(got, on):
            g.wait_recv()
            c.start()

    def finish(zz):
        sx = zz * 4 + 3 - h.xy
        top, low = pl.ds(0, half), pl.ds(half, half)
        remote(out.at[sx, top], out.at[sx, top], yfs.at[zz], yfr.at[zz], ctx=h.yn).wait_recv()
        remote(out.at[sx, low], out.at[sx, low], xfs.at[zz], xfr.at[zz], ctx=h.xn).wait_recv()

    plan.at(t0 + 0.8 * tx, lambda: forward(h.z))
    for k in (1, 2, 3):
        for up in (True, False):
            valid = (lambda k=k, up=up: (h.z >= k) if up else (h.z + k <= 3))
            plan.at(t0 + k * tz, functools.partial(step, k, up))
            zz = (lambda k=k, up=up: h.z - k if up else h.z + k)
            plan.at(t0 + (k + 0.8) * tx, lambda v=valid, q=zz: pl.when(v())(lambda: forward(q())))

    def drain():
        if not by_plane:
            for zz in range(4):
                finish(zz)
        for k in range(3):
            pl.when((h.z >= k) & (h.z < 3))(lambda: hop(k, True).wait_send())
            pl.when((h.z + k <= 3) & (h.z > 0))(lambda: hop(k, False).wait_send())
        for zz in range(4):
            for c in plane(zz) + across(zz):
                c.wait_send()

    plan.at(t0 + 0.85 * tx, local.wait)
    plan.at(t0 + 4.5 * tx, drain)
    return finish


SCATTER_SEMS = [DMA((4,))] * 8 + [DMA((4,))] * 2


def scatter_scratch(rows, width):
    half = width // 2
    return [
        pltpu.VMEM((4, 2, rows, half), BF),
        pltpu.VMEM((4, 2, rows, half), BF),
        pltpu.VMEM((4, rows, half), BF),
        pltpu.VMEM((4, rows, half), BF),
        pltpu.VMEM((4, rows, half), BF),
        pltpu.VMEM((4, rows, half), BF),
        pltpu.VMEM((3, rows, width), BF),
        pltpu.VMEM((3, rows, width), BF),
    ] + SCATTER_SEMS


N_SCATTER = 18
AHEAD = 1


def scatter16(plan, h, part, out, scratch, t0, tx):
    ra, rb, sa, sb, qa, qb, sz, rz = scratch[:8]
    as_, ar, bs, br, cs, cr, es, er, zs, zr = scratch[8:]
    rows, width = part.shape[3:]
    half = width // 2
    lo, hi = pl.ds(0, half), pl.ds(half, half)
    xo, yo = 1 - h.x, 1 - h.y

    def place(k):
        return jnp.bitwise_xor(h.z, k)

    def first(i, k):
        return (
            remote(part.at[place(k), :, xo, :, lo], ra.at[i], as_.at[i], ar.at[i], ctx=h.xn),
            remote(part.at[place(k), yo, :, :, hi], rb.at[i], bs.at[i], br.at[i], ctx=h.yn),
        )

    def second(i):
        return (
            remote(sa.at[i], qa.at[i], cs.at[i], cr.at[i], ctx=h.yn),
            remote(sb.at[i], qb.at[i], es.at[i], er.at[i], ctx=h.xn),
        )

    def third(k):
        return remote(sz.at[k - 1], rz.at[k - 1], zs.at[k], zr.at[k], ctx=place(k) * 4 + h.xy)

    def start(i, k):
        for c in first(i, k):
            c.start()

    def middle(i, k):
        a, b = first(i, k)
        c, e = second(i)
        a.wait_recv()
        sa[i] = (part[place(k), yo, h.x, :, lo].astype(F32) + ra[i, yo].astype(F32)).astype(BF)
        c.start()
        b.wait_recv()
        sb[i] = (part[place(k), h.y, xo, :, hi].astype(F32) + rb[i, xo].astype(F32)).astype(BF)
        e.start()

    def total(i, k):
        c, e = second(i)
        c.wait_recv()
        e.wait_recv()
        left = part[place(k), h.y, h.x, :, lo].astype(F32) + ra[i, h.y].astype(F32) + qa[i].astype(F32)
        right = part[place(k), h.y, h.x, :, hi].astype(F32) + rb[i, h.x].astype(F32) + qb[i].astype(F32)
        if k:
            sz[k - 1, :, lo] = left.astype(BF)
            sz[k - 1, :, hi] = right.astype(BF)
            third(k).start()
        else:
            out[:, lo] = left
            out[:, hi] = right

    def last():
        for k in (1, 2, 3):
            third(k).wait_recv()
        out[...] += rz[0].astype(F32) + rz[1].astype(F32) + rz[2].astype(F32)
        for k in (1, 2, 3):
            third(k).wait_send()
        for i, k in enumerate((1, 2, 3, 0)):
            for c in first(i, k) + second(i):
                c.wait_send()

    for i, k in enumerate((1, 2, 3, 0)):
        plan.at(t0 + max(0, i - AHEAD + 0.71) * tx if i >= AHEAD else t0 + 0.01 * i, functools.partial(start, i, k))
        plan.at(t0 + i * tx + 0.7 * tx, functools.partial(middle, i, k))
        plan.at(t0 + i * tx + 1.35 * tx, functools.partial(total, i, k))
    plan.at(t0 + 5 * tx, last)


DEAL_SEMS = [DMA((16,))] * 4 + [DMA]


def deal16(plan, h, piece, put, passed, sems, t0, t1, both=True, pace=0.0, relay_from=None):
    ss, sr, fs, fr, own = sems

    def send(step):
        to = jnp.bitwise_xor(h.me, step)
        return remote(piece(to), put(h.me), ss.at[step], sr.at[step], ctx=to)

    def got(step):
        at = jnp.bitwise_xor(h.me, step)
        return remote(put(at), put(at), ss.at[step], sr.at[step], ctx=at)

    def hand(step):
        at = jnp.bitwise_xor(h.me, step)
        return remote(put(at) if step else piece(h.me), passed(at, h.core), fs.at[step], fr.at[step], fsdp=1 - h.core)

    def taken(step):
        at = jnp.bitwise_xor(h.me, step)
        return remote(passed(at, 1 - h.core), passed(at, 1 - h.core), fs.at[step], fr.at[step], fsdp=1 - h.core)

    local = pltpu.make_async_copy(piece(h.me), put(h.me), own)

    def first():
        local.start()
        if both:
            hand(0).start()

    plan.at(t0, first)
    for i, step in enumerate(ORDER):
        plan.at(t0 + pace * i, lambda step=step: send(step).start())

        def relay(step=step):
            got(step).wait_recv()
            if both:
                hand(step).start()

        since = t0 if relay_from is None else relay_from
        plan.at(since + (t1 - since) * (i + 1) / 15 if both else t1, relay)

    def drain():
        if both:
            for step in range(16):
                taken(step).wait_recv()
                hand(step).wait_send()
        for step in ORDER:
            send(step).wait_send()

    plan.at(t1, local.wait)
    plan.at(t1 + 2, drain)


ORDER = (12, 8, 13, 9, 14, 10, 15, 11, 4, 5, 6, 7, 3, 1, 2)


GATHER8_SEMS = [DMA((4,))] * 6 + [DMA]


def gather8(plan, h, src, out, sems, t0, tz, tx):
    us, ur, ds, dr, xs, xr, own = sems

    def level(zz, source=None):
        s = zz * 2 + h.x
        return remote(out.at[s] if source is None else source, out.at[s], xs.at[zz], xr.at[zz], ctx=h.xn)

    def hop(k, up, source=None):
        it = (h.z - k if up else h.z + k) * 2 + h.x
        send, recv = (us, ur) if up else (ds, dr)
        to = h.me + 4 if up else h.me - 4
        return remote(out.at[it] if source is None else source, out.at[it], send.at[k], recv.at[k + 1], ctx=to)

    def landed(k, up):
        it = (h.z - k if up else h.z + k) * 2 + h.x
        send, recv = (us, ur) if up else (ds, dr)
        return remote(out.at[it], out.at[it], send.at[k - 1], recv.at[k], ctx=h.me)

    local = pltpu.make_async_copy(src, out.at[h.z * 2 + h.x], own)

    def first():
        pl.when(h.z < 3)(lambda: hop(0, True, src).start())
        pl.when(h.z > 0)(lambda: hop(0, False, src).start())
        level(h.z, src).start()
        local.start()

    plan.at(t0, first)

    def step(k, up):
        def go():
            landed(k, up).wait_recv()
            if k < 3:
                pl.when((h.z < 3) if up else (h.z > 0))(lambda: hop(k, up).start())
            level(h.z - k if up else h.z + k).start()

        pl.when((h.z >= k) if up else (h.z + k <= 3))(go)

    for k in (1, 2, 3):
        for up in (True, False):
            plan.at(t0 + k * tz, functools.partial(step, k, up))

    def finish(zz):
        s = zz * 2 + 1 - h.x
        remote(out.at[s], out.at[s], xs.at[zz], xr.at[zz], ctx=h.xn).wait_recv()

    def drain():
        for k in range(3):
            pl.when((h.z >= k) & (h.z < 3))(lambda: hop(k, True).wait_send())
            pl.when((h.z + k <= 3) & (h.z > 0))(lambda: hop(k, False).wait_send())
        for zz in range(4):
            level(zz).wait_send()

    plan.at(t0 + 0.85 * tx, local.wait)
    plan.at(t0 + 4.5 * tx, drain)
    return finish


def scatter8_scratch(rows, width):
    few = pltpu.VMEM((3, rows, width), BF)
    return [pltpu.VMEM((4, rows, width), BF), few, few] + [DMA((4,))] * 4


N_SCATTER8 = 7


def scatter8(plan, h, part, out, scratch, starts, totals, end):
    ra, sz, rz, as_, ar, zs, zr = scratch

    def place(k):
        return jnp.bitwise_xor(h.z, k)

    def first(i, k):
        return remote(part.at[place(k), 1 - h.x], ra.at[i], as_.at[i], ar.at[i], ctx=h.xn)

    def second(k):
        return remote(sz.at[k - 1], rz.at[k - 1], zs.at[k], zr.at[k], ctx=place(k) * 4 + h.xy)

    def total(i, k):
        first(i, k).wait_recv()
        value = part[place(k), h.x].astype(F32) + ra[i].astype(F32)
        if k:
            sz[k - 1] = value.astype(BF)
            second(k).start()
        else:
            out[...] = value

    def last():
        for k in (1, 2, 3):
            second(k).wait_recv()
        out[...] += rz[0].astype(F32) + rz[1].astype(F32) + rz[2].astype(F32)
        for k in (1, 2, 3):
            second(k).wait_send()
        for i, k in enumerate((1, 2, 3, 0)):
            first(i, k).wait_send()

    for i, k in enumerate((1, 2, 3, 0)):
        plan.at(starts[i], lambda i=i, k=k: first(i, k).start())
        plan.at(totals[i], functools.partial(total, i, k))
    plan.at(end, last)


DEAL8_SEMS = [DMA((8,))] * 2 + [DMA]


def deal8(plan, h, piece, put, sems, t0, t1):
    ss, sr, own = sems
    row = h.z * 2 + h.x

    def place(r):
        return (r // 2) * 4 + h.y * 2 + lax.rem(r, 2)

    def send(step):
        to = jnp.bitwise_xor(row, step)
        return remote(piece(to), put(row), ss.at[step], sr.at[step], ctx=place(to))

    def got(step):
        at = jnp.bitwise_xor(row, step)
        return remote(put(at), put(at), ss.at[step], sr.at[step], ctx=place(at))

    local = pltpu.make_async_copy(piece(row), put(row), own)

    def start():
        for step in (7, 5, 6, 4, 3, 2, 1):
            send(step).start()
        local.start()

    def end():
        for step in (7, 5, 6, 4, 3, 2, 1):
            got(step).wait_recv()
        local.wait()

    def drain():
        for step in (7, 5, 6, 4, 3, 2, 1):
            send(step).wait_send()

    plan.at(t0, start)
    plan.at(t1, end)
    plan.at(t1 + 40, drain)

ROWS = 256


def _tri():
    i = lax.broadcasted_iota(jnp.int32, (ROWS, ROWS), 0)
    j = lax.broadcasted_iota(jnp.int32, (ROWS, ROWS), 1)
    return i <= j


def _heads(value):
    lane = lax.broadcasted_iota(jnp.int32, value.shape, 1)
    zero = jnp.zeros_like(value)
    return jnp.where(lane < 64, value, zero), jnp.where(lane >= 64, value, zero)


def _nt(a, b):
    return lax.dot_general(a, b, (((1,), (1,)), ((), ())), preferred_element_type=F32)


def _tn(a, b):
    return lax.dot_general(a, b, (((0,), (0,)), ((), ())), preferred_element_type=F32)


def _nn(a, b):
    return jnp.dot(a, b, preferred_element_type=F32)


def _scores(keys, query, tri):
    scores = _nt(keys, query)
    n = keys.shape[0]
    low = jnp.where(tri, scores[n - ROWS :], -1e30)
    return low if n == ROWS else jnp.concatenate([scores[: n - ROWS], low], 0)


def sort_rows(order_ref, src, dst):
    for b in range(src.shape[0]):
        dst[b * 64 : (b + 1) * 64, :] = src[order_ref[b]]


def attend_step(i, qs, ks, vs, os, lse):
    tri = _tri()
    n = (i + 1) * ROWS
    mine = slice(i * ROWS, n)
    total = None
    for head, query in enumerate(_heads(qs[mine, :] * BF(0.125))):
        scores = _scores(ks[:n, :], query, tri)
        top = jnp.max(scores, 0, keepdims=True)
        raw = jnp.exp(scores - top)
        size = jnp.sum(raw, 0, keepdims=True)
        lse[head : head + 1, mine] = top + jnp.log(size)
        probs = (raw * (1.0 / size)).astype(BF)
        part = _tn(probs, _heads(vs[:n, :])[head])
        total = part if total is None else total + part
    os[mine, :] = total.astype(BF)


def back_step(i, qs, ks, vs, gs, lse, dq, dk, dv):
    tri = _tri()
    n = (i + 1) * ROWS
    mine = slice(i * ROWS, n)
    total = None
    queries = _heads(qs[mine, :] * BF(0.125))
    grads = _heads(gs[mine, :])
    for head in range(2):
        scores = _scores(ks[:n, :], queries[head], tri)
        probs = jnp.exp(scores - lse[head : head + 1, mine])
        gp = _nt(vs[:n, :], grads[head])
        delta = jnp.sum(probs * gp, 0, keepdims=True)
        ds = (probs * (gp - delta)).astype(BF)
        dv[:n, :] += _nn(probs.astype(BF), grads[head])
        dk[:n, :] += _nn(ds, queries[head])
        part = _tn(ds, _heads(ks[:n, :])[head])
        total = part if total is None else total + part
    dq[mine, :] = total * 0.125


def swap_halves(values):
    lane = lax.broadcasted_iota(jnp.int32, values.shape, 1)
    return jnp.where(lax.rem(lane, 64) < 32, pltpu.roll(values, 96, 1), pltpu.roll(values, 32, 1))


from jax.sharding import PartitionSpec as P

HEADS = 32
HD = 64
EPSILON = 1e-05
THETA_BASE = 130000.0
ANY = pl.BlockSpec(memory_space=pl.ANY)
INNER = pl.BlockSpec(memory_space=pltpu.VMEM)


def comm_call(kernel, outs, out_specs, in_specs, scratch, cid, name, vmem=40):
    return pl.pallas_call(
        kernel,
        out_shape=outs,
        in_specs=in_specs,
        out_specs=out_specs,
        scratch_shapes=scratch,
        compiler_params=pltpu.CompilerParams(
            collective_id=cid, has_side_effects=True, vmem_limit_bytes=vmem << 20
        ),
        name=name,
    )


def take(refs, n):
    head, refs[:] = refs[:n], refs[n:]
    return head


def columns(src, width):
    return lambda c: src.at[:, pl.ds(pl.multiple_of(c * width, 128), width)]


def columns_of(out, width):
    return lambda c: out.at[:, pl.ds(pl.multiple_of(c * width, 128), width)]


def deal_columns(plan, h, src, out, sems, t0, t1, relay_from, lanes=None):
    lanes = pl.ds(0, out.shape[3]) if lanes is None else lanes
    deal16(
        plan, h, columns(src, lanes.size), lambda c: out.at[c, h.core, :, lanes], lambda c, core: out.at[c, core, :, lanes],
        sems, t0, t1, relay_from=relay_from,
    )


SPREAD = ((22, 83, 140, 200), (60, 97, 160, 201), (84, 125, 190, 202))


def spread_columns(plan, h, src, out, sems, t0, t1, t2, t3):
    ys, yr, cs, cr = sems[3].at[0], sems[3].at[1], sems[3].at[2], sems[3].at[3]
    w = out.shape[5]
    deal8(
        plan, h, lambda r: src.at[:, pl.ds(pl.multiple_of(r * w, 128), w)],
        lambda r: out.at[r // 2, h.y, lax.rem(r, 2), h.core], sems[:3], t0, t1,
    )
    mine, theirs = out.at[:, h.y, :, h.core], out.at[:, 1 - h.y, :, h.core]
    over_y = remote(mine, mine, ys, yr, ctx=h.yn)
    all_mine, all_other = out.at[:, :, :, h.core], out.at[:, :, :, 1 - h.core]
    over_core = remote(all_mine, all_mine, cs, cr, fsdp=1 - h.core)
    plan.at(t1 + 0.5, over_y.start)

    def pass_on():
        remote(theirs, theirs, ys, yr, ctx=h.yn).wait_recv()
        over_core.start()

    def end():
        remote(all_other, all_other, cs, cr, fsdp=1 - h.core).wait_recv()
        over_y.wait_send()
        over_core.wait_send()

    plan.at(t2, pass_on)
    plan.at(t3, end)


def front_kernel(
    order, table, x, wq, wk, wv, wg, wu, wd, wo, cot, tile, cos, sin,
    normed, w_out, gains, qs, ks, vs, lse, low, hidden, mlp_in, g_out, u_out, d_out, o_out, c_out, *refs
):
    refs = list(refs)
    xg, wqkv, tiles, stage, q, k_rows, v, o, o_rows, w_part = take(refs, 10)
    stage_sem, send, recv, w_sems = take(refs, 4)
    rows, width = x.shape
    h = Here()
    greet_all(h)
    plan = Plan()
    for i, src in enumerate((wq, wk, wv)):
        deal_columns(plan, h, src, wqkv, take(refs, 5), 0, 16, 10, pl.ds(i * 128, 128))
    deal16(
        plan, h, lambda c: tile, lambda c: tiles.at[c, h.core], lambda c, core: tiles.at[c, core], take(refs, 5), 0, 17,
        relay_from=11,
    )
    done = gather16(plan, h, x, xg, take(refs, 13), 0, 14, 20, by_plane=True)
    for i, (src, out) in enumerate(((wg, g_out), (wu, u_out), (wd, d_out))):
        spread_columns(plan, h, src, out, take(refs, 4), *SPREAD[i])
    gather16(plan, h, wo, o_out.at[:, h.core], take(refs, 13), 98, 10, 14)
    seen = gather8(plan, h, cot, c_out, take(refs, 7), 82.5, 18, 20)
    plan.at(185, lambda: [seen(zz) for zz in range(4)])
    to_sems = take(refs, 5)
    mine, other = o_out.at[:, h.core], o_out.at[:, 1 - h.core]
    across = remote(mine, mine, send, recv, fsdp=1 - h.core)
    plan.at(165, across.start)

    def plane(k):
        return jnp.bitwise_xor(h.z, k)

    def put_normed(k):
        at = pl.ds(pl.multiple_of(plane(k) * 4 * rows, 4 * rows), 4 * rows)
        return pltpu.make_async_copy(stage, normed.at[at], stage_sem)

    def spread_gains():
        gains[...] = jnp.zeros_like(gains)
        for c in range(16):
            both = tiles[c, 0].astype(F32) + tiles[c, 1].astype(F32)
            gains[:, c * 128 : (c + 1) * 128] = both[0:8]

    def work(k):
        zz = plane(k)
        done(zz)
        if k:
            put_normed(k - 1).wait()
        else:
            spread_gains()
        for p in range(2):
            at = pl.ds(pl.multiple_of((zz * 4 + p * 2) * rows, 2 * rows), 2 * rows)
            blocks = pl.ds(zz * 8 + p * 4, 4)
            value = xg[pl.ds(zz * 4 + p * 2, 2)].reshape(2 * rows, width).astype(F32)
            inverse = lax.rsqrt(jnp.mean(value * value, -1, keepdims=True) + EPSILON)
            value = (value * inverse * gains[0:1, :]).astype(BF)
            stage[p * 2 * rows : (p + 1) * 2 * rows, :] = value
            pre = _nn(value, wqkv[...].reshape(width, 384))
            for i, out in enumerate((q, k_rows)):
                part = pre[:, i * 128 : (i + 1) * 128]
                turned = part * cos[at, :] + swap_halves(part) * sin[at, :]
                out[blocks] = turned.astype(BF).reshape(4, 64, 128)
            v[blocks] = pre[:, 256:].astype(BF).reshape(4, 64, 128)
        put_normed(k).start()

    for k in range(4):
        plan.at((24, 42, 62, 82)[k], functools.partial(work, k))

    def sort():
        put_normed(3).wait()
        for a, b in ((q, qs), (k_rows, ks), (v, vs)):
            sort_rows(order, a, b)
        w_out[...] = wqkv[...].reshape(width, 384)

    plan.at(83, sort)
    for i in range(16 * rows // ROWS):
        plan.at(84 + 1.3 * i, functools.partial(attend_step, i, qs, ks, vs, o.reshape(16 * rows, 128), lse))

    def unsort():
        for b in range(32):
            o_rows[b // 2, (b % 2) * 64 : (b % 2 + 1) * 64, :] = o[table[b]]

    plan.at(96, unsort)
    deal16(plan, h, lambda c: o_rows.at[c], columns_of(low, 128), None, to_sems, 96.1, 172, both=False)

    def end():
        remote(other, other, send, recv, fsdp=1 - h.core).wait_recv()
        across.wait_send()

    def load(b):
        return pltpu.make_async_copy(o_out.at[pl.ds(4 * b, 4)], w_part.at[b % 2], w_sems.at[b % 2])

    def project():
        load(0).start()
        load(1).start()
        total = x[...].astype(F32)
        for b in range(4):
            load(b).wait()
            depth = width // 4
            total = total + _nn(low[:, b * depth : (b + 1) * depth], w_part[b % 2].reshape(depth, width))
            if b + 2 < 4:
                load(b + 2).start()
        hidden[...] = total
        inverse = lax.rsqrt(jnp.mean(total * total, -1, keepdims=True) + EPSILON)
        mlp_in[...] = (total * inverse * gains[1:2, :]).astype(BF)

    plan.at(173, end)
    plan.at(176, project)
    plan.run()


def front(order, table, x, wq, wk, wv, wg, wu, wd, wo, cot, tile, cos, sin):
    rows, width = x.shape
    length = 16 * rows
    block = jax.ShapeDtypeStruct((4, 2, 2, 2, wg.shape[0], wg.shape[1] // 8), BF)
    heads = jax.ShapeDtypeStruct((length, 128), BF)
    outs = (
        jax.ShapeDtypeStruct((length, width), BF), jax.ShapeDtypeStruct((width, 384), BF),
        jax.ShapeDtypeStruct((8, width), F32), heads, heads, heads, jax.ShapeDtypeStruct((2, length), F32),
        jax.ShapeDtypeStruct((rows, width), BF), jax.ShapeDtypeStruct((rows, width), F32),
        jax.ShapeDtypeStruct((rows, width), BF), block, block, block,
        jax.ShapeDtypeStruct((16, 2) + wo.shape, BF), jax.ShapeDtypeStruct((8, rows, width), BF),
    )
    smem = pl.BlockSpec(memory_space=pltpu.SMEM)
    scratch = [
        pltpu.VMEM((16, rows, width), BF), pltpu.VMEM((16, 2, wq.shape[0], 384), BF), pltpu.VMEM((16, 2) + tile.shape, BF),
        pltpu.VMEM((4 * rows, width), BF), *[pltpu.VMEM((32, 64, 128), BF)] * 4, pltpu.VMEM((16, rows, 128), BF),
        pltpu.VMEM((2, 4, 2) + wo.shape, BF), DMA, DMA, DMA, DMA((2,)),
    ]
    scratch += DEAL_SEMS * 4 + GATHER_SEMS + (DEAL8_SEMS + [DMA((4,))]) * 3 + GATHER_SEMS + GATHER8_SEMS + DEAL_SEMS
    return comm_call(
        front_kernel, outs, [ANY] + [INNER] * 9 + [ANY] * 5, [smem] * 2 + [INNER] + [ANY] * 8 + [INNER] * 3, scratch, 0,
        "front", 58,
    )(order, table, x, wq, wk, wv, wg, wu, wd, wo, cot, tile, cos, sin)


def mlp_kernel(src, cot, bg, bu, bd, gmi, out_part, sum_g, own_u, d_home, *refs):
    refs = list(refs)
    xm, ct, wg, wu, wd, grads, act, part, stage, cols = take(refs, 10)
    own_g, other_gu, got_gu, own_d, other_d, got_d, sum_d = take(refs, 7)
    w_sem, ct_sem, cols_sem, stage_sem, ex_sems = take(refs, 5)
    rows, width = src.shape
    hidden = wg.shape[1]
    block = own_d.shape[1]
    h = Here()
    loads = [pltpu.make_async_copy(a, b, w_sem.at[i]) for i, (a, b) in enumerate(((bg, wg), (bu, wu), (bd, wd)))]

    def plane(k):
        return jnp.bitwise_xor(h.z, k)

    def load_cot(k):
        return pltpu.make_async_copy(cot.at[pl.ds(plane(k) * 2, 2)], ct.at[k % 2], ct_sem.at[k % 2])

    def put_out(k):
        return pltpu.make_async_copy(stage, out_part.at[pl.ds(plane(k) * 2, 2)], stage_sem)

    for c in loads + [load_cot(0), load_cot(1)]:
        c.start()
    greet_all(h)
    plan = Plan()
    done = gather8(plan, h, src, xm, take(refs, 7), 0, 12, 12)

    def work(k):
        zz = plane(k)
        done(zz)
        if k == 0:
            for c in loads:
                c.wait()
        load_cot(k).wait()
        if k:
            put_out(k - 1).wait()
        at = pl.ds(pl.multiple_of(zz * 2 * rows, 2 * rows), 2 * rows)
        x = xm[pl.ds(zz * 2, 2)].reshape(2 * rows, width)
        gate, up = _nn(x, wg[...]), _nn(x, wu[...])
        sig = jax.nn.sigmoid(gate)
        silu = gate * sig
        low = (silu * up).astype(BF)
        act[at, :] = low
        stage[...] = _nt(low, wd[...]).astype(BF).reshape(2, rows, width)
        grad = _nn(ct[k % 2].reshape(2 * rows, width), wd[...])
        grad_gate = (grad * up * sig * (1.0 + gate * (1.0 - sig))).astype(BF)
        grad_up = (grad * silu).astype(BF)
        grads[at, pl.ds(0, hidden)] = grad_gate
        grads[at, pl.ds(hidden, hidden)] = grad_up
        back = _nt(grad_gate, wg[...]) + _nt(grad_up, wu[...])
        part[zz] = back.astype(BF).reshape(2, rows, width)
        put_out(k).start()
        if k + 2 < 4:
            load_cot(k + 2).start()

    for k in range(4):
        plan.at((15, 26, 38, 50)[k], functools.partial(work, k))
    plan.at(55, lambda: put_out(3).wait())
    scatter8(plan, h, part, gmi, take(refs, N_SCATTER8), (27, 39, 50.2, 50.3), (50.4, 58.5, 66.5, 75), 110)

    def split(c, both, own, other, lanes):
        both = both.astype(BF).reshape(2, block, both.shape[1])
        own[c] = jnp.where(h.core == 0, both[0], both[1])
        other[c, :, lanes] = jnp.where(h.core == 0, both[1], both[0])

    def exchange(i, other, got):
        return remote(other, got, ex_sems.at[i], ex_sems.at[2 + i], fsdp=1 - h.core)

    def load_cols(c):
        slot = lax.rem(c, 2)
        at = pl.ds(pl.multiple_of(c * 2 * block, 128), 2 * block)
        return pltpu.make_async_copy(cot.at[:, :, at], cols.at[slot], cols_sem.at[slot])

    def grads_gu(first):
        def one(c, carry):
            at = pl.ds(pl.multiple_of(c * 2 * block, 128), 2 * block)
            lhs = xm[:, :, at].reshape(8 * rows, 2 * block)
            split(c, _tn(lhs, grads[:, :hidden]), own_g, other_gu, pl.ds(0, hidden))
            split(c, _tn(lhs, grads[:, hidden:]), own_u, other_gu, pl.ds(hidden, hidden))
            return carry

        lax.fori_loop(first, first + 4, one, 0)

    def grads_d(first):
        def one(c, carry):
            pl.when(c < 15)(lambda: load_cols(c + 1).start())
            load_cols(c).wait()
            lhs = cols[lax.rem(c, 2)].reshape(8 * rows, 2 * block)
            split(c, _tn(lhs, act[...]), own_d, other_d, pl.ds(0, hidden))
            return carry

        lax.fori_loop(first, first + 4, one, 0)

    def over_y(i, own, result):
        own, result = own.reshape(4, 2, 2, *own.shape[1:]), result.reshape(4, 2, *own.shape[1:])
        return remote(own.at[:, 1 - h.y], result, ex_sems.at[4 + i], ex_sems.at[6 + i], ctx=h.yn)

    def join(i, own, other, got, result):
        exchange(i, other, got).wait_recv()
        for c in range(16):
            own[c] = (own[c].astype(F32) + got[c, :, 0:hidden].astype(F32)).astype(BF)
        over_y(i, own, result).start()

    def join_u():
        for c in range(16):
            own_u[c] = (own_u[c].astype(F32) + got_gu[c, :, hidden:].astype(F32)).astype(BF)

    def add_y(i, own, other, got, result):
        over_y(i, own, result).wait_recv()
        for r in range(8):
            z, x = r // 2, r % 2
            mine = jnp.where(h.y == 0, own[z * 4 + x], own[z * 4 + 2 + x])
            result[r] = (mine.astype(F32) + result[r].astype(F32)).astype(BF)

    def sent(i, own, other, got, result):
        exchange(i, other, got).wait_send()
        over_y(i, own, result).wait_send()

    d, g = (own_d, other_d, got_d, sum_d), (own_g, other_gu, got_gu, sum_g)
    plan.at(50.5, lambda: load_cols(0).start())
    for i in range(4):
        plan.at(56 + 2 * i, functools.partial(grads_d, 4 * i))
        plan.at(68 + 3 * i, functools.partial(grads_gu, 4 * i))
    plan.at(64, lambda: exchange(1, other_d, got_d).start())
    plan.at(68.5, lambda: join(1, *d))
    plan.at(82, lambda: exchange(0, other_gu, got_gu).start())
    plan.at(86, lambda: join(0, *g))
    plan.at(86.5, join_u)
    plan.at(90, lambda: add_y(1, *d))
    deal8(plan, h, lambda r: sum_d.at[r], columns_of(d_home, hidden), take(refs, 3), 90.1, 200)
    plan.at(112, lambda: add_y(0, *g))
    plan.at(201, lambda: [sent(1, *d), sent(0, *g)])
    plan.run()


def mlp(src, cot, bg, bu, bd):
    rows, width = src.shape
    block, hidden = bg.shape[4:]
    full = pltpu.VMEM((width, hidden), BF)
    gu, d = pltpu.VMEM((16, block, 2 * hidden), BF), pltpu.VMEM((16, block, hidden), BF)
    scratch = [
        pltpu.VMEM((8, rows, width), BF), pltpu.VMEM((2, 2, rows, width), BF), full, full, full,
        pltpu.VMEM((8 * rows, 2 * hidden), BF), pltpu.VMEM((8 * rows, hidden), BF),
        pltpu.VMEM((4, 2, rows, width), BF), pltpu.VMEM((2, rows, width), BF),
        pltpu.VMEM((2, 8, rows, 2 * block), BF), d, gu, gu, d, d, d,
        pltpu.VMEM((8, block, hidden), BF),
        DMA((3,)), DMA((2,)), DMA((2,)), DMA, DMA((8,)),
    ]
    scratch += GATHER8_SEMS + scatter8_scratch(rows, width) + DEAL8_SEMS
    outs = (
        jax.ShapeDtypeStruct((rows, width), F32), jax.ShapeDtypeStruct((8, rows, width), BF),
        jax.ShapeDtypeStruct((8, block, hidden), BF), jax.ShapeDtypeStruct((16, block, hidden), BF),
        jax.ShapeDtypeStruct((block, 8 * hidden), BF),
    )
    return comm_call(mlp_kernel, outs, [INNER, ANY, INNER, INNER, ANY], [ANY] * 5, scratch, 5, "mlp", 62)(
        src, cot, *(b.reshape(width, hidden) for b in (bg, bu, bd))
    )


def outer_home(plan, h, left, right, own, other, got, send, recv, t0, t1):
    rows = own.shape[1]
    over = remote(other, got, send, recv, fsdp=1 - h.core)

    def compute():
        mine, theirs = pl.multiple_of(h.core * rows, rows), pl.multiple_of((1 - h.core) * rows, rows)
        for c in range(16):
            lhs = left[:, c * 2 * rows : (c + 1) * 2 * rows]
            both = _tn(lhs, right[...]).astype(BF).reshape(2, rows, right.shape[1])
            own[c] = jnp.where(h.core == 0, both[0], both[1])
            other[c] = jnp.where(h.core == 0, both[1], both[0])
        over.start()

    def add():
        over.wait_recv()
        for c in range(16):
            own[c] = (own[c].astype(F32) + got[c].astype(F32)).astype(BF)
        over.wait_send()

    plan.at(t0, compute)
    plan.at(t1, add)


def back_kernel(order, table, wo, qs, ks, vs, lse, cos, sin, out_part, low, branch, sum_g, own_u, dqkv, out_sum, wo_sum, sum_u, g_home, *refs):
    refs = list(refs)
    ga, w_part, gh, gs, dq, dk, dv, own, other, got = take(refs, 10)
    w_sems = take(refs, 1)[0]
    send, recv = take(refs, 2)
    gh_rows = gh.reshape(16, ga.shape[0], 128)
    flat = [g.reshape(qs.shape) for g in (dq, dk, dv)]
    h = Here()
    depth = w_part.shape[1]

    def load(b):
        return pltpu.make_async_copy(wo.at[pl.ds(b * depth, depth)], w_part.at[b % 2], w_sems.at[b % 2])

    load(0).start()
    load(1).start()
    greet_all(h)
    plan = Plan()

    def project():
        for b in range(wo.shape[0] // depth):
            load(b).wait()
            ga[:, b * depth : (b + 1) * depth] = _nt(branch[...], w_part[b % 2]).astype(BF)
            if b + 2 < wo.shape[0] // depth:
                load(b + 2).start()

    plan.at(0.5, project)
    deal16(plan, h, columns(ga, 128), lambda c: gh_rows.at[c], None, take(refs, 5), 0.6, 14, both=False)
    gu_sems = take(refs, 3)
    scatter8(plan, h, out_part, out_sum, take(refs, N_SCATTER8), (0.1, 18, 35, 52), (18.8, 35.8, 52.8, 69.8), 94)
    outer_home(plan, h, low, branch, own, other, got, send, recv, 2, 8)
    deal8(plan, h, lambda r: sum_g.at[r], columns_of(g_home, sum_g.shape[2]), gu_sems, 0.3, 198)
    half_u, u_sems = take(refs, 2)
    split_u = own_u.reshape(4, 2, 2, *own_u.shape[1:])
    over_u = remote(split_u.at[:, 1 - h.y], sum_u, u_sems.at[0], u_sems.at[1], ctx=h.yn)
    keep_u = pltpu.make_async_copy(split_u.at[:, h.y], half_u, u_sems.at[2])

    def start_u():
        over_u.start()
        keep_u.start()

    def end_u():
        over_u.wait_recv()
        keep_u.wait()
        for z in range(4):
            sum_u[z] = (sum_u[z].astype(F32) + half_u[z].astype(F32)).astype(BF)
        over_u.wait_send()

    plan.at(0.2, start_u)
    plan.at(90, end_u)
    scatter16(plan, h, own.reshape(4, 2, 2, *own.shape[1:]), wo_sum, take(refs, N_SCATTER), 8.1, 18)

    def begin():
        sort_rows(order, gh, gs)
        dk[...] = jnp.zeros_like(dk)
        dv[...] = jnp.zeros_like(dv)

    plan.at(15, begin)
    for i in range(qs.shape[0] // ROWS):
        plan.at(16 + 2.2 * i, functools.partial(back_step, i, qs, ks, vs, gs, lse, *flat))

    def end():
        for b in range(32):
            rows = slice(b * 64, (b + 1) * 64)
            for i, grad in enumerate((dq, dk)):
                value = grad[table[b]]
                turned = swap_halves(value)
                dqkv[rows, i * 128 : (i + 1) * 128] = (value * cos[rows, :] - turned * sin[rows, :]).astype(BF)
            dqkv[rows, 256:] = dv[table[b]].astype(BF)

    plan.at(34.5, end)
    plan.run()


def back(order, table, wo, qs, ks, vs, lse, cos, sin, out_part, low, branch, sum_g, own_u):
    rows, width = low.shape
    length = qs.shape[0]
    smem = pl.BlockSpec(memory_space=pltpu.SMEM)
    half = pltpu.VMEM((16, width // 32, width), BF)
    outs = (
        jax.ShapeDtypeStruct((length, 384), BF),
        jax.ShapeDtypeStruct((rows, width), F32),
        jax.ShapeDtypeStruct((width // 32, width), F32),
        jax.ShapeDtypeStruct((4, 2) + sum_g.shape[1:], BF),
        jax.ShapeDtypeStruct((sum_g.shape[1], 8 * sum_g.shape[2]), BF),
    )
    scratch = [pltpu.VMEM((rows, width), BF), pltpu.VMEM((2, width // 4, width), BF)]
    scratch += [pltpu.VMEM((32, 64, 128), BF), pltpu.VMEM((length, 128), BF)]
    scratch += [pltpu.VMEM((32, 64, 128), F32)] * 3 + [half] * 3 + [DMA((2,))] + [DMA] * 2 + DEAL_SEMS + DEAL8_SEMS
    scratch += scatter8_scratch(rows, width) + [pltpu.VMEM((4, 2) + sum_g.shape[1:], BF), DMA((3,))]
    scratch += scatter_scratch(width // 32, width)
    return comm_call(back_kernel, outs, [INNER] * 4 + [ANY], [smem] * 2 + [ANY] + [INNER] * 9 + [ANY] * 2, scratch, 6, "back", 60)(
        order, table, wo, qs, ks, vs, lse, cos, sin, out_part.reshape(4, 2, rows, width), low, branch, sum_g, own_u
    )


def home_kernel(
    dqkv, wqkv, normed, gd, gg, gu, x, grad_hidden, gain, wq, wk, wv, wg, wu,
    input_grad, q_out, k_out, v_out, gain_a, gain_m, d_out, g_out, u_out, *refs
):
    refs = list(refs)
    part, nm, own, other, got, landed, d32, g32, u16, u32, gn = take(refs, 11)
    nm_sem, ex_sems, out_sems = take(refs, 3)
    rows, width = x.shape
    block = own.shape[1]
    h = Here()
    load = pltpu.make_async_copy(normed, nm, nm_sem)
    load.start()
    greet_all(h)
    plan = Plan()
    deal8(plan, h, lambda r: gu.at[r], columns_of(u16, gu.shape[2]), take(refs, 3), 0.4, 90)

    def plane(k):
        zz = jnp.bitwise_xor(h.z, k)
        for p in range(2):
            at = pl.ds(pl.multiple_of((zz * 4 + p * 2) * rows, 2 * rows), 2 * rows)
            part[zz, pl.ds(p, 1)] = _nt(dqkv[at, :], wqkv[...]).astype(BF).reshape(1, 2, rows, width)

    for i, k in enumerate((1, 2, 3, 0)):
        plan.at((0.1, 1, 2, 3)[i], functools.partial(plane, k))
    scatter16(plan, h, part, gn, take(refs, N_SCATTER), 0.2, 20)
    plan.at(4, load.wait)

    def grads(first):
        def one(c, carry):
            at = pl.ds(pl.multiple_of(c * 2 * block, 128), 2 * block)
            both = _tn(nm[:, at], dqkv[...]).astype(BF).reshape(2, block, 384)
            own[c] = jnp.where(h.core == 0, both[0], both[1])
            other[c] = jnp.where(h.core == 0, both[1], both[0])
            return carry

        lax.fori_loop(first, first + 4, one, 0)

    for i in range(4):
        plan.at(4.1 + i, functools.partial(grads, 4 * i))
    over = remote(other, got, ex_sems.at[0], ex_sems.at[1], fsdp=1 - h.core)
    plan.at(8, over.start)

    def join():
        over.wait_recv()
        for c in range(16):
            own[c] = (own[c].astype(F32) + got[c].astype(F32)).astype(BF)
        over.wait_send()

    plan.at(10, join)
    deal16(plan, h, lambda c: own.at[c], lambda c: landed.at[c], None, take(refs, 5), 10.1, 91, both=False)
    writes = [
        pltpu.make_async_copy(a, b, out_sems.at[i]) for i, (a, b) in enumerate(((d32, d_out), (g32, g_out), (u32, u_out)))
    ]

    def widen(i, source, target):
        target[...] = source[...].astype(F32)
        writes[i].start()

    plan.at(15, functools.partial(widen, 0, gd, d32))
    plan.at(25, functools.partial(widen, 1, gg, g32))
    plan.at(92, functools.partial(widen, 2, u16, u32))

    def finish_qkv():
        for c in range(16):
            for i, out in enumerate((q_out, k_out, v_out)):
                out[:, c * 128 : (c + 1) * 128] = landed[c, :, i * 128 : (i + 1) * 128].astype(F32)

    def sums():
        terms = ((wq, q_out), (wk, k_out), (wv, v_out))
        gain_a[...] = sum(jnp.sum(w[...].astype(F32) * g[...], -1, keepdims=True) for w, g in terms)
        terms = ((wg, g32), (wu, u32))
        gain_m[...] = sum(jnp.sum(w[...].astype(F32) * g[...], -1, keepdims=True) for w, g in terms)

    plan.at(93, finish_qkv)
    plan.at(94, sums)

    def result():
        value = x[...].astype(F32)
        inverse = lax.rsqrt(jnp.mean(value * value, -1, keepdims=True) + EPSILON)
        scaled = gn[...] * gain[0:1, :]
        inner = jnp.sum(scaled * value, -1, keepdims=True)
        input_grad[...] = (
            grad_hidden[...] + inverse * scaled - inverse * inverse * inverse / width * value * inner
        )

    plan.at(202, result)
    plan.at(300, lambda: [w.wait() for w in writes])
    plan.run()


def home(dqkv, wqkv, normed, gd, gg, gu, x, grad_hidden, gain, wq, wk, wv, wg, wu):
    rows, width = x.shape
    block, wide = gd.shape
    third = pltpu.VMEM((16, block, 384), BF)
    column = jax.ShapeDtypeStruct((block, 1), F32)
    wide32 = pltpu.VMEM((block, wide), F32)
    small = jax.ShapeDtypeStruct((block, width), F32)
    large = jax.ShapeDtypeStruct((block, wide), F32)
    outs = (
        jax.ShapeDtypeStruct((rows, width), F32), small, small, small, column, column, large, large, large
    )
    scratch = [
        pltpu.VMEM((4, 2, 2, rows, width), BF), pltpu.VMEM(normed.shape, BF), third, third, third, third, wide32, wide32,
        pltpu.VMEM((block, wide), BF), wide32, pltpu.VMEM((rows, width), F32),
        DMA, DMA((2,)), DMA((3,)),
    ]
    scratch += DEAL8_SEMS + scatter_scratch(rows, width) + DEAL_SEMS
    return comm_call(
        home_kernel, outs, [INNER] * 6 + [ANY] * 3, [INNER, INNER, ANY, INNER, INNER, ANY] + [INNER] * 8, scratch, 7, "home", 60
    )(dqkv, wqkv, normed, gd, gg, gu, x, grad_hidden, gain, wq, wk, wv, wg, wu)


def rope_tables(positions):
    inv_freq = THETA_BASE ** (-(jnp.arange(HD // 2, dtype=F32) * 2.0 / HD))
    angles = positions.astype(F32)[:, None] * inv_freq[None, :]
    return jnp.tile(jnp.cos(angles), (1, 4)), jnp.tile(jnp.sin(angles), (1, 4))


def swap(values):
    a, b, c, d = jnp.split(values, 4, -1)
    return jnp.concatenate([b, a, d, c], -1)


def fast_body(x, table, attn_gain, wq, wk, wv, wo, mlp_gain, wg, wu, wd, cot):
    x, cot, table = x[0], cot[0], table[0].reshape(32)
    rows, width = x.shape
    length = rows * 16
    core = lax.axis_index("fsdp")
    slots = jnp.arange(32, dtype=jnp.int32)
    order = jnp.sum(jnp.where(table[None, :] == slots[:, None], slots[None, :], 0), 1)
    positions = (table[:, None] * 64 + jnp.arange(64, dtype=jnp.int32)[None]).reshape(length)
    cos, sin = rope_tables(positions)
    turn = jnp.where(jnp.arange(128) % 64 < 32, -1.0, 1.0).astype(F32)
    sin = sin * turn

    def dot(a, b):
        return jnp.dot(a, b, preferred_element_type=F32)

    def dot_nt(a, b):
        return lax.dot_general(a, b, (((1,), (1,)), ((), ())), preferred_element_type=F32)

    def dot_tn(a, b):
        return lax.dot_general(a, b, (((0,), (0,)), ((), ())), preferred_element_type=F32)

    lane = jnp.arange(128) // 64
    tile = jnp.where(lane[None] == core, jnp.tile(jnp.stack([attn_gain, mlp_gain]), (1, 2)), 0)
    tile = jnp.pad(tile, ((0, 14), (0, 0)))
    normed, wqkv, gains, qs, ks, vs, lse, attn_low, hidden, mlp_in, bg, bu, bd, full_out, cot_all = front(
        order, table, x, wq, wk, wv, wg, wu, wd, wo, cot, tile, cos, sin
    )
    again, mgain = gains[0], gains[1]
    full_out = full_out.reshape(width, width)
    inv_mid = lax.rsqrt(jnp.mean(hidden * hidden, -1, keepdims=True) + EPSILON)
    gmi, out_part, sum_g, own_u, gd = mlp(mlp_in, cot_all, bg, bu, bd)

    def norm_back(grad, source, inv, gain):
        scaled = grad * gain
        inner = jnp.sum(scaled * source, -1, keepdims=True)
        return inv * scaled - inv * inv * inv / width * source * inner

    grad_hidden = cot.astype(F32) + norm_back(gmi, hidden, inv_mid, mgain)
    grad_branch = grad_hidden.astype(BF)
    grad_qkv, out_sum, wo_grad, sum_u, gg = back(
        order, table, full_out, qs, ks, vs, lse, cos, sin, out_part, attn_low, grad_branch, sum_g, own_u
    )
    layer_output = (hidden + out_sum).astype(BF)
    input_grad, gq, gk, gv, gain_a, gain_m, gd, gg, gu = home(
        grad_qkv, wqkv, normed, gd, gg, sum_u.reshape(sum_g.shape), x, grad_hidden, gains, wq, wk, wv, wg, wu
    )
    gain_a = gain_a[:, 0] / attn_gain.astype(F32)
    gain_m = gain_m[:, 0] / mlp_gain.astype(F32)
    return (layer_output[None], input_grad[None], gain_a, gq, gk, gv, wo_grad, gain_m, gg, gu, gd)


MASKED = -1e30


def general_tables(positions):
    inv_freq = THETA_BASE ** (-(jnp.arange(HD // 2, dtype=jnp.float32) * 2.0 / HD))
    angles = positions.astype(jnp.float32)[:, None] * inv_freq[None, :]
    cosine = jnp.cos(angles)
    sine_tab = jnp.sin(angles)
    return (jnp.concatenate([cosine, cosine], -1), jnp.concatenate([sine_tab, sine_tab], -1))


def rotate(values, cosine, sine_tab):
    middle = values.shape[-1] // 2
    turned = jnp.concatenate([-values[..., middle:], values[..., :middle]], -1)
    return values * cosine[:, None, :] + turned * sine_tab[:, None, :]


def rotate_back(grads_in, cosine, sine_tab):
    middle = grads_in.shape[-1] // 2
    shifted = grads_in * sine_tab[:, None, :]
    turned = jnp.concatenate([shifted[..., middle:], -shifted[..., :middle]], -1)
    return grads_in * cosine[:, None, :] + turned


def inverse_rms(rows_in):
    return lax.rsqrt(jnp.mean(rows_in * rows_in, -1, keepdims=True) + EPSILON)


def general_norm_back(grad_normed, rows_in, inverse, gain_vec):
    scaled = grad_normed * gain_vec
    inner_sum = jnp.sum(scaled * rows_in, -1, keepdims=True)
    return inverse * scaled - inverse * inverse * inverse / rows_in.shape[-1] * rows_in * inner_sum


def score_rows(query_rows, key_rows, query_pos, key_pos):
    scores = jnp.einsum(
        "qhd,khd->hqk", query_rows, key_rows, preferred_element_type=jnp.float32
    ) * HD ** (-0.5)
    visible = key_pos[None, None, :] <= query_pos[None, :, None]
    return (scores, visible)


def softmax_rows(scores, visible, log_total):
    return jnp.where(
        visible, jnp.exp(jnp.where(visible, scores - log_total[..., None], MASKED)), 0.0
    )


def walk_keys(kv_steps, top_pos, width, step_fn, initial):
    step_rows = kv_steps.shape[1]
    offsets = jnp.arange(step_rows, dtype=jnp.int32)

    def advance(carried, step_item):
        step_index, kv_block = step_item
        first_key = step_index * step_rows
        key_rows = kv_block[:, :width].reshape(step_rows, HEADS, HD)
        value_rows = kv_block[:, width:].reshape(step_rows, HEADS, HD)
        key_pos = first_key + offsets
        updated = lax.cond(
            first_key <= top_pos,
            lambda state: step_fn(state, key_rows, value_rows, key_pos),
            lambda state: state,
            carried,
        )
        return (updated, None)

    indices = jnp.arange(kv_steps.shape[0], dtype=jnp.int32)
    final_state, ignored = lax.scan(advance, initial, (indices, kv_steps))
    return final_state


def general_body(
    layer_input,
    block_table,
    attn_gain,
    query_weight,
    key_weight,
    value_weight,
    out_weight,
    mlp_gain,
    gate_weight,
    up_weight,
    down_weight,
    cotangent,
):
    tokens = layer_input.shape[1]
    width = layer_input.shape[2]
    half_rows = tokens // 2
    ranks = lax.axis_size("ctx")
    length = tokens * ranks
    score_scale = HD ** (-0.5)
    block_ids = block_table[0].reshape(2 * ranks)
    own_blocks = lax.dynamic_slice_in_dim(block_ids, lax.axis_index("ctx") * 2, 2)
    inner = jnp.arange(half_rows, dtype=jnp.int32)
    query_pos = (own_blocks[:, None] * half_rows + inner[None, :]).reshape(tokens)
    cosine, sine_tab = general_tables(query_pos)
    full_query, full_key, full_value, full_out, full_attn_gain = (
        lax.all_gather(query_weight, ("ctx", "fsdp"), axis=0, tiled=True),
        lax.all_gather(key_weight, ("ctx", "fsdp"), axis=0, tiled=True),
        lax.all_gather(value_weight, ("ctx", "fsdp"), axis=0, tiled=True),
        lax.all_gather(out_weight, ("ctx", "fsdp"), axis=0, tiled=True),
        lax.all_gather(attn_gain, ("ctx", "fsdp"), axis=0, tiled=True),
    )
    source = layer_input[0].astype(jnp.float32)
    inverse_in = inverse_rms(source)
    normed = (source * inverse_in * full_attn_gain.astype(jnp.float32)).astype(jnp.bfloat16)
    query_pre = jnp.dot(normed, full_query, preferred_element_type=jnp.float32).reshape(
        tokens, HEADS, HD
    )
    key_pre = jnp.dot(normed, full_key, preferred_element_type=jnp.float32).reshape(
        tokens, HEADS, HD
    )
    value_low = jnp.dot(normed, full_value, preferred_element_type=jnp.float32).astype(jnp.bfloat16)
    queries = rotate(query_pre, cosine, sine_tab).astype(jnp.bfloat16)
    keys_low = rotate(key_pre, cosine, sine_tab).astype(jnp.bfloat16).reshape(tokens, width)
    kv_dev = lax.all_gather(jnp.concatenate([keys_low, value_low], 1), "ctx", axis=0, tiled=True)
    slot_ids = jnp.arange(2 * ranks, dtype=jnp.int32)
    holder = jnp.sum(jnp.where(block_ids[None, :] == slot_ids[:, None], slot_ids[None, :], 0), 1)
    chosen = (holder[:, None] == slot_ids[None, :]).astype(jnp.bfloat16)
    kv_seq = jnp.einsum(
        "ab,bn->an", chosen, kv_dev.reshape(2 * ranks, half_rows * 2 * width)
    ).reshape(length, 2 * width)
    step_rows = min(512, length)
    kv_steps = kv_seq.reshape(length // step_rows, step_rows, 2 * width)
    log_totals = []
    attended_parts = []
    top_list = []
    for slot_index in range(2):
        slot_queries = queries[slot_index * half_rows : (slot_index + 1) * half_rows]
        slot_pos = query_pos[slot_index * half_rows : (slot_index + 1) * half_rows]
        top_pos = own_blocks[slot_index] * half_rows + half_rows - 1
        top_list.append(top_pos)

        def stat_step(state, key_rows, value_rows, key_pos):
            running, running_sum = state
            scores, visible = score_rows(slot_queries, key_rows, slot_pos, key_pos)
            scores = jnp.where(visible, scores, MASKED)
            newest = jnp.maximum(running, jnp.max(scores, -1))
            running_sum = running_sum * jnp.exp(running - newest) + jnp.sum(
                jnp.where(visible, jnp.exp(scores - newest[..., None]), 0.0), -1
            )
            return (newest, running_sum)

        start_state = (
            jnp.full((HEADS, half_rows), MASKED, jnp.float32),
            jnp.zeros((HEADS, half_rows), jnp.float32),
        )
        running, running_sum = walk_keys(kv_steps, top_pos, width, stat_step, start_state)
        log_total = running + jnp.log(running_sum)

        def value_step(accumulated, key_rows, value_rows, key_pos):
            scores, visible = score_rows(slot_queries, key_rows, slot_pos, key_pos)
            weights_low = softmax_rows(scores, visible, log_total).astype(jnp.bfloat16)
            return accumulated + jnp.einsum(
                "hqk,khd->qhd", weights_low, value_rows, preferred_element_type=jnp.float32
            )

        attended_parts.append(
            walk_keys(
                kv_steps, top_pos, width, value_step, jnp.zeros((half_rows, HEADS, HD), jnp.float32)
            )
        )
        log_totals.append(log_total)
    attended = jnp.concatenate(attended_parts, 0)
    log_all = jnp.concatenate(log_totals, 1)
    attn_low = attended.reshape(tokens, width).astype(jnp.bfloat16)
    hidden = source + jnp.dot(attn_low, full_out, preferred_element_type=jnp.float32)
    full_gate, full_up, full_down, full_mlp_gain = (
        lax.all_gather(gate_weight, ("ctx", "fsdp"), axis=0, tiled=True),
        lax.all_gather(up_weight, ("ctx", "fsdp"), axis=0, tiled=True),
        lax.all_gather(down_weight, ("ctx", "fsdp"), axis=0, tiled=True),
        lax.all_gather(mlp_gain, ("ctx", "fsdp"), axis=0, tiled=True),
    )
    inverse_mid = inverse_rms(hidden)
    mlp_in = (hidden * inverse_mid * full_mlp_gain.astype(jnp.float32)).astype(jnp.bfloat16)
    gate_pre = jnp.dot(mlp_in, full_gate, preferred_element_type=jnp.float32)
    up_pre = jnp.dot(mlp_in, full_up, preferred_element_type=jnp.float32)
    activation = (jax.nn.silu(gate_pre) * up_pre).astype(jnp.bfloat16)
    branch_mlp = jnp.einsum("tf,df->td", activation, full_down, preferred_element_type=jnp.float32)
    layer_output = (hidden + branch_mlp).astype(jnp.bfloat16)
    back_gate, back_up, back_down, back_mlp_gain = (
        lax.all_gather(gate_weight, ("ctx", "fsdp"), axis=0, tiled=True),
        lax.all_gather(up_weight, ("ctx", "fsdp"), axis=0, tiled=True),
        lax.all_gather(down_weight, ("ctx", "fsdp"), axis=0, tiled=True),
        lax.all_gather(mlp_gain, ("ctx", "fsdp"), axis=0, tiled=True),
    )
    grad_out_low = cotangent[0]
    grad_act = jnp.dot(grad_out_low, back_down, preferred_element_type=jnp.float32)
    sigmoid_gate = jax.nn.sigmoid(gate_pre)
    grad_gate = (grad_act * up_pre * sigmoid_gate * (1.0 + gate_pre * (1.0 - sigmoid_gate))).astype(
        jnp.bfloat16
    )
    grad_up = (grad_act * gate_pre * sigmoid_gate).astype(jnp.bfloat16)
    grad_mlp_in = jnp.einsum(
        "tf,df->td", grad_gate, back_gate, preferred_element_type=jnp.float32
    ) + jnp.einsum("tf,df->td", grad_up, back_up, preferred_element_type=jnp.float32)
    mlp_gain_term = jnp.sum(grad_mlp_in * hidden * inverse_mid, 0)
    grad_hidden = grad_out_low.astype(jnp.float32) + general_norm_back(
        grad_mlp_in, hidden, inverse_mid, back_mlp_gain.astype(jnp.float32)
    )
    grad_branch = grad_hidden.astype(jnp.bfloat16)
    back_query, back_key, back_value, back_out, back_attn_gain = (
        lax.all_gather(query_weight, ("ctx", "fsdp"), axis=0, tiled=True),
        lax.all_gather(key_weight, ("ctx", "fsdp"), axis=0, tiled=True),
        lax.all_gather(value_weight, ("ctx", "fsdp"), axis=0, tiled=True),
        lax.all_gather(out_weight, ("ctx", "fsdp"), axis=0, tiled=True),
        lax.all_gather(attn_gain, ("ctx", "fsdp"), axis=0, tiled=True),
    )
    grad_attended = (
        jnp.einsum("te,de->td", grad_branch, back_out, preferred_element_type=jnp.float32)
        .astype(jnp.bfloat16)
        .reshape(tokens, HEADS, HD)
    )
    delta_all = jnp.sum(grad_attended.astype(jnp.float32) * attended, -1).T
    grad_query_parts = []
    for slot_index in range(2):
        slot_queries = queries[slot_index * half_rows : (slot_index + 1) * half_rows]
        slot_pos = query_pos[slot_index * half_rows : (slot_index + 1) * half_rows]
        slot_grad_out = grad_attended[slot_index * half_rows : (slot_index + 1) * half_rows]
        slot_delta = delta_all[:, slot_index * half_rows : (slot_index + 1) * half_rows]
        slot_log = log_totals[slot_index]

        def query_step(accumulated, key_rows, value_rows, key_pos):
            scores, visible = score_rows(slot_queries, key_rows, slot_pos, key_pos)
            weights_full = softmax_rows(scores, visible, slot_log)
            grad_weights = jnp.einsum(
                "qhd,khd->hqk", slot_grad_out, value_rows, preferred_element_type=jnp.float32
            )
            grad_scores = (weights_full * (grad_weights - slot_delta[..., None])).astype(
                jnp.bfloat16
            )
            return accumulated + jnp.einsum(
                "hqk,khd->qhd", grad_scores, key_rows, preferred_element_type=jnp.float32
            )

        grad_query_parts.append(
            walk_keys(
                kv_steps,
                top_list[slot_index],
                width,
                query_step,
                jnp.zeros((half_rows, HEADS, HD), jnp.float32),
            )
        )
    grad_queries = jnp.concatenate(grad_query_parts, 0) * score_scale
    grad_query_low = (
        rotate_back(grad_queries, cosine, sine_tab).reshape(tokens, width).astype(jnp.bfloat16)
    )
    bottom_key = jnp.min(query_pos)
    query_both = lax.all_gather(
        jnp.concatenate([queries.reshape(tokens, width), grad_attended.reshape(tokens, width)], 1),
        "ctx",
        axis=0,
        tiled=True,
    )
    stats_both = lax.all_gather(
        jnp.stack([log_all.T, delta_all.T], 1).astype(jnp.bfloat16), "ctx", axis=0, tiled=True
    ).astype(jnp.float32)
    all_pos = (block_ids[:, None] * half_rows + inner[None, :]).reshape(length)
    own_keys = keys_low.reshape(tokens, HEADS, HD)
    own_values = value_low.reshape(tokens, HEADS, HD)

    def gather_step(carried, piece_index):
        first = piece_index * step_rows
        piece_pos = lax.dynamic_slice_in_dim(all_pos, first, step_rows)

        def live_piece(state):
            rows_here = lax.dynamic_slice_in_dim(query_both, first, step_rows, 0)
            stats_here = lax.dynamic_slice_in_dim(stats_both, first, step_rows, 0)
            piece_queries = rows_here[:, :width].reshape(step_rows, HEADS, HD)
            piece_grads = rows_here[:, width:].reshape(step_rows, HEADS, HD)
            piece_log = stats_here[:, 0, :].T
            piece_delta = stats_here[:, 1, :].T
            scores, visible = score_rows(piece_queries, own_keys, piece_pos, query_pos)
            weights_full = softmax_rows(scores, visible, piece_log)
            grad_weights = jnp.einsum(
                "qhd,khd->hqk", piece_grads, own_values, preferred_element_type=jnp.float32
            )
            grad_scores = (weights_full * (grad_weights - piece_delta[..., None])).astype(
                jnp.bfloat16
            )
            grad_keys = (
                jnp.einsum(
                    "hqk,qhd->khd", grad_scores, piece_queries, preferred_element_type=jnp.float32
                )
                * score_scale
            )
            grad_values = jnp.einsum(
                "hqk,qhd->khd",
                weights_full.astype(jnp.bfloat16),
                piece_grads,
                preferred_element_type=jnp.float32,
            )
            return (state[0] + grad_keys, state[1] + grad_values)

        updated = lax.cond(
            jnp.max(piece_pos) >= bottom_key, live_piece, lambda state: state, carried
        )
        return (updated, None)

    start_grads = (
        jnp.zeros((tokens, HEADS, HD), jnp.float32),
        jnp.zeros((tokens, HEADS, HD), jnp.float32),
    )
    summed, ignored = lax.scan(
        gather_step, start_grads, jnp.arange(length // step_rows, dtype=jnp.int32)
    )
    kv_grads = jnp.concatenate(
        [summed[0].reshape(tokens, width), summed[1].reshape(tokens, width)], 1
    )
    grad_key_low = (
        rotate_back(kv_grads[:, :width].reshape(tokens, HEADS, HD), cosine, sine_tab)
        .reshape(tokens, width)
        .astype(jnp.bfloat16)
    )
    grad_value_low = kv_grads[:, width:].astype(jnp.bfloat16)
    grad_normed = jnp.einsum(
        "te,de->td", grad_query_low, back_query, preferred_element_type=jnp.float32
    )
    grad_normed = grad_normed + jnp.einsum(
        "te,de->td", grad_key_low, back_key, preferred_element_type=jnp.float32
    )
    grad_normed = grad_normed + jnp.einsum(
        "te,de->td", grad_value_low, back_value, preferred_element_type=jnp.float32
    )
    attn_gain_term = jnp.sum(grad_normed * source * inverse_in, 0)
    input_grad = grad_hidden + general_norm_back(
        grad_normed, source, inverse_in, back_attn_gain.astype(jnp.float32)
    )

    def outer_sum(left_side, right_side):
        return jnp.einsum("tc,te->ce", left_side, right_side, preferred_element_type=jnp.float32)

    weight_grads = lax.psum_scatter(
        jnp.concatenate(
            [
                outer_sum(normed, grad_query_low),
                outer_sum(normed, grad_key_low),
                outer_sum(normed, grad_value_low),
                outer_sum(attn_low, grad_branch),
                outer_sum(mlp_in, grad_gate),
                outer_sum(mlp_in, grad_up),
                outer_sum(grad_out_low, activation),
            ],
            1,
        ),
        ("ctx", "fsdp"),
        scatter_dimension=0,
        tiled=True,
    )
    gain_grads = lax.psum_scatter(
        jnp.stack([attn_gain_term, mlp_gain_term], 1),
        ("ctx", "fsdp"),
        scatter_dimension=0,
        tiled=True,
    )
    hidden_units = gate_weight.shape[1]
    edge_attn = 4 * width
    return (
        layer_output[None],
        input_grad[None],
        gain_grads[:, 0],
        weight_grads[:, 0:width],
        weight_grads[:, width : 2 * width],
        weight_grads[:, 2 * width : 3 * width],
        weight_grads[:, 3 * width : edge_attn],
        gain_grads[:, 1],
        weight_grads[:, edge_attn : edge_attn + hidden_units],
        weight_grads[:, edge_attn + hidden_units : edge_attn + 2 * hidden_units],
        weight_grads[:, edge_attn + 2 * hidden_units : edge_attn + 3 * hidden_units],
    )


def solution(mesh):
    both = ("ctx", "fsdp")
    rows = P(both, None)
    tokens = P("fsdp", "ctx", None)
    return jax.shard_map(
        fast_body if mesh.shape["ctx"] == 16 and mesh.shape["fsdp"] == 2 else general_body,
        mesh=mesh,
        in_specs=(tokens, P("fsdp", None, None), P(both), rows, rows, rows, rows, P(both), rows, rows, rows, tokens),
        out_specs=(tokens, tokens, P(both), rows, rows, rows, rows, P(both), rows, rows, rows),
        check_vma=False,
    )
```

```python
import functools
import jax, jax.numpy as jnp
from jax import lax
from jax.experimental import pallas as pl
from jax.experimental.pallas import tpu as pltpu

MESH = pl.DeviceIdType.MESH
DMA = pltpu.SemaphoreType.DMA
BF = jnp.bfloat16
F32 = jnp.float32


class Plan:
    def __init__(self):
        self.steps = []

    def at(self, when, step):
        self.steps.append((when, len(self.steps), step))

    def run(self):
        for _, _, step in sorted(self.steps, key=lambda s: s[:2]):
            step()


class Here:
    def __init__(self):
        self.me = lax.axis_index("ctx")
        self.core = lax.axis_index("fsdp")
        self.z = self.me // 4
        self.y = lax.rem(self.me // 2, 2)
        self.x = lax.rem(self.me, 2)
        self.xy = lax.rem(self.me, 4)
        self.xn = self.me + 1 - 2 * self.x
        self.yn = self.me + 2 - 4 * self.y


def remote(src, dst, send_sem, recv_sem, **device):
    return pltpu.make_async_remote_copy(
        src_ref=src, dst_ref=dst, send_sem=send_sem, recv_sem=recv_sem, device_id=device, device_id_type=MESH
    )


def greet_all(h):
    barrier = pltpu.get_barrier_semaphore()
    for step in range(1, 16):
        pl.semaphore_signal(barrier, inc=1, device_id={"ctx": jnp.bitwise_xor(h.me, step)}, device_id_type=MESH)
    pl.semaphore_signal(barrier, inc=1, device_id={"fsdp": 1 - h.core}, device_id_type=MESH)
    pl.semaphore_wait(barrier, 16)


GATHER_SEMS = [DMA((4,))] * 12 + [DMA]


def gather16(plan, h, src, out, sems, t0, tz, tx, by_plane=False):
    us, ur, ds, dr, xs, xr, ys, yr, xfs, xfr, yfs, yfr, own = sems
    half = src.shape[0] // 2

    def plane(zz, source=None):
        s = zz * 4 + h.xy
        source = out.at[s] if source is None else source
        return (
            remote(source, out.at[s], xs.at[zz], xr.at[zz], ctx=h.xn),
            remote(source, out.at[s], ys.at[zz], yr.at[zz], ctx=h.yn),
        )

    def across(zz):
        sx = zz * 4 + lax.rem(h.xn, 4)
        sy = zz * 4 + lax.rem(h.yn, 4)
        top, low = pl.ds(0, half), pl.ds(half, half)
        return (
            remote(out.at[sx, top], out.at[sx, top], yfs.at[zz], yfr.at[zz], ctx=h.yn),
            remote(out.at[sy, low], out.at[sy, low], xfs.at[zz], xfr.at[zz], ctx=h.xn),
        )

    def arrived(zz):
        sx = zz * 4 + lax.rem(h.xn, 4)
        sy = zz * 4 + lax.rem(h.yn, 4)
        return (
            remote(out.at[sx], out.at[sx], xs.at[zz], xr.at[zz], ctx=h.xn),
            remote(out.at[sy], out.at[sy], ys.at[zz], yr.at[zz], ctx=h.yn),
        )

    def hop(k, up, source=None):
        it = (h.z - k if up else h.z + k) * 4 + h.xy
        send, recv = (us, ur) if up else (ds, dr)
        source = out.at[it] if source is None else source
        to = h.me + 4 if up else h.me - 4
        return remote(source, out.at[it], send.at[k], recv.at[k + 1], ctx=to)

    def landed(k, up):
        it = (h.z - k if up else h.z + k) * 4 + h.xy
        send, recv = (us, ur) if up else (ds, dr)
        return remote(out.at[it], out.at[it], send.at[k - 1], recv.at[k], ctx=h.me)

    local = pltpu.make_async_copy(src, out.at[h.me], own)

    def first():
        pl.when(h.z < 3)(lambda: hop(0, True, src).start())
        pl.when(h.z > 0)(lambda: hop(0, False, src).start())
        for c in plane(h.z, src):
            c.start()
        local.start()

    plan.at(t0, first)

    def step(k, up):
        def go():
            landed(k, up).wait_recv()
            if k < 3:
                pl.when((h.z < 3) if up else (h.z > 0))(lambda: hop(k, up).start())
            for c in plane(h.z - k if up else h.z + k):
                c.start()

        pl.when((h.z >= k) if up else (h.z + k <= 3))(go)

    def forward(zz):
        got, on = arrived(zz), across(zz)
        for g, c in zip(got, on):
            g.wait_recv()
            c.start()

    def finish(zz):
        sx = zz * 4 + 3 - h.xy
        top, low = pl.ds(0, half), pl.ds(half, half)
        remote(out.at[sx, top], out.at[sx, top], yfs.at[zz], yfr.at[zz], ctx=h.yn).wait_recv()
        remote(out.at[sx, low], out.at[sx, low], xfs.at[zz], xfr.at[zz], ctx=h.xn).wait_recv()

    plan.at(t0 + 0.8 * tx, lambda: forward(h.z))
    for k in (1, 2, 3):
        for up in (True, False):
            valid = (lambda k=k, up=up: (h.z >= k) if up else (h.z + k <= 3))
            plan.at(t0 + k * tz, functools.partial(step, k, up))
            zz = (lambda k=k, up=up: h.z - k if up else h.z + k)
            plan.at(t0 + (k + 0.8) * tx, lambda v=valid, q=zz: pl.when(v())(lambda: forward(q())))

    def drain():
        if not by_plane:
            for zz in range(4):
                finish(zz)
        for k in range(3):
            pl.when((h.z >= k) & (h.z < 3))(lambda: hop(k, True).wait_send())
            pl.when((h.z + k <= 3) & (h.z > 0))(lambda: hop(k, False).wait_send())
        for zz in range(4):
            for c in plane(zz) + across(zz):
                c.wait_send()

    plan.at(t0 + 0.85 * tx, local.wait)
    plan.at(t0 + 4.5 * tx, drain)
    return finish


SCATTER_SEMS = [DMA((4,))] * 8 + [DMA((4,))] * 2


def scatter_scratch(rows, width):
    half = width // 2
    return [
        pltpu.VMEM((4, 2, rows, half), BF),
        pltpu.VMEM((4, 2, rows, half), BF),
        pltpu.VMEM((4, rows, half), BF),
        pltpu.VMEM((4, rows, half), BF),
        pltpu.VMEM((4, rows, half), BF),
        pltpu.VMEM((4, rows, half), BF),
        pltpu.VMEM((3, rows, width), BF),
        pltpu.VMEM((3, rows, width), BF),
    ] + SCATTER_SEMS


N_SCATTER = 18
AHEAD = 1


def scatter16(plan, h, part, out, scratch, t0, tx):
    ra, rb, sa, sb, qa, qb, sz, rz = scratch[:8]
    as_, ar, bs, br, cs, cr, es, er, zs, zr = scratch[8:]
    rows, width = part.shape[3:]
    half = width // 2
    lo, hi = pl.ds(0, half), pl.ds(half, half)
    xo, yo = 1 - h.x, 1 - h.y

    def place(k):
        return jnp.bitwise_xor(h.z, k)

    def first(i, k):
        return (
            remote(part.at[place(k), :, xo, :, lo], ra.at[i], as_.at[i], ar.at[i], ctx=h.xn),
            remote(part.at[place(k), yo, :, :, hi], rb.at[i], bs.at[i], br.at[i], ctx=h.yn),
        )

    def second(i):
        return (
            remote(sa.at[i], qa.at[i], cs.at[i], cr.at[i], ctx=h.yn),
            remote(sb.at[i], qb.at[i], es.at[i], er.at[i], ctx=h.xn),
        )

    def third(k):
        return remote(sz.at[k - 1], rz.at[k - 1], zs.at[k], zr.at[k], ctx=place(k) * 4 + h.xy)

    def start(i, k):
        for c in first(i, k):
            c.start()

    def middle(i, k):
        a, b = first(i, k)
        c, e = second(i)
        a.wait_recv()
        sa[i] = (part[place(k), yo, h.x, :, lo].astype(F32) + ra[i, yo].astype(F32)).astype(BF)
        c.start()
        b.wait_recv()
        sb[i] = (part[place(k), h.y, xo, :, hi].astype(F32) + rb[i, xo].astype(F32)).astype(BF)
        e.start()

    def total(i, k):
        c, e = second(i)
        c.wait_recv()
        e.wait_recv()
        left = part[place(k), h.y, h.x, :, lo].astype(F32) + ra[i, h.y].astype(F32) + qa[i].astype(F32)
        right = part[place(k), h.y, h.x, :, hi].astype(F32) + rb[i, h.x].astype(F32) + qb[i].astype(F32)
        if k:
            sz[k - 1, :, lo] = left.astype(BF)
            sz[k - 1, :, hi] = right.astype(BF)
            third(k).start()
        else:
            out[:, lo] = left
            out[:, hi] = right

    def last():
        for k in (1, 2, 3):
            third(k).wait_recv()
        out[...] += rz[0].astype(F32) + rz[1].astype(F32) + rz[2].astype(F32)
        for k in (1, 2, 3):
            third(k).wait_send()
        for i, k in enumerate((1, 2, 3, 0)):
            for c in first(i, k) + second(i):
                c.wait_send()

    for i, k in enumerate((1, 2, 3, 0)):
        plan.at(t0 + max(0, i - AHEAD + 0.71) * tx if i >= AHEAD else t0 + 0.01 * i, functools.partial(start, i, k))
        plan.at(t0 + i * tx + 0.7 * tx, functools.partial(middle, i, k))
        plan.at(t0 + i * tx + 1.35 * tx, functools.partial(total, i, k))
    plan.at(t0 + 5 * tx, last)


DEAL_SEMS = [DMA((16,))] * 4 + [DMA]


def deal16(plan, h, piece, put, passed, sems, t0, t1, both=True, pace=0.0, relay_from=None):
    ss, sr, fs, fr, own = sems

    def send(step):
        to = jnp.bitwise_xor(h.me, step)
        return remote(piece(to), put(h.me), ss.at[step], sr.at[step], ctx=to)

    def got(step):
        at = jnp.bitwise_xor(h.me, step)
        return remote(put(at), put(at), ss.at[step], sr.at[step], ctx=at)

    def hand(step):
        at = jnp.bitwise_xor(h.me, step)
        return remote(put(at) if step else piece(h.me), passed(at, h.core), fs.at[step], fr.at[step], fsdp=1 - h.core)

    def taken(step):
        at = jnp.bitwise_xor(h.me, step)
        return remote(passed(at, 1 - h.core), passed(at, 1 - h.core), fs.at[step], fr.at[step], fsdp=1 - h.core)

    local = pltpu.make_async_copy(piece(h.me), put(h.me), own)

    def first():
        local.start()
        if both:
            hand(0).start()

    plan.at(t0, first)
    for i, step in enumerate(ORDER):
        plan.at(t0 + pace * i, lambda step=step: send(step).start())

        def relay(step=step):
            got(step).wait_recv()
            if both:
                hand(step).start()

        since = t0 if relay_from is None else relay_from
        plan.at(since + (t1 - since) * (i + 1) / 15 if both else t1, relay)

    def drain():
        if both:
            for step in range(16):
                taken(step).wait_recv()
                hand(step).wait_send()
        for step in ORDER:
            send(step).wait_send()

    plan.at(t1, local.wait)
    plan.at(t1 + 2, drain)


ORDER = (12, 8, 13, 9, 14, 10, 15, 11, 4, 5, 6, 7, 3, 1, 2)


GATHER8_SEMS = [DMA((4,))] * 6 + [DMA]


def gather8(plan, h, src, out, sems, t0, tz, tx):
    us, ur, ds, dr, xs, xr, own = sems

    def level(zz, source=None):
        s = zz * 2 + h.x
        return remote(out.at[s] if source is None else source, out.at[s], xs.at[zz], xr.at[zz], ctx=h.xn)

    def hop(k, up, source=None):
        it = (h.z - k if up else h.z + k) * 2 + h.x
        send, recv = (us, ur) if up else (ds, dr)
        to = h.me + 4 if up else h.me - 4
        return remote(out.at[it] if source is None else source, out.at[it], send.at[k], recv.at[k + 1], ctx=to)

    def landed(k, up):
        it = (h.z - k if up else h.z + k) * 2 + h.x
        send, recv = (us, ur) if up else (ds, dr)
        return remote(out.at[it], out.at[it], send.at[k - 1], recv.at[k], ctx=h.me)

    local = pltpu.make_async_copy(src, out.at[h.z * 2 + h.x], own)

    def first():
        pl.when(h.z < 3)(lambda: hop(0, True, src).start())
        pl.when(h.z > 0)(lambda: hop(0, False, src).start())
        level(h.z, src).start()
        local.start()

    plan.at(t0, first)

    def step(k, up):
        def go():
            landed(k, up).wait_recv()
            if k < 3:
                pl.when((h.z < 3) if up else (h.z > 0))(lambda: hop(k, up).start())
            level(h.z - k if up else h.z + k).start()

        pl.when((h.z >= k) if up else (h.z + k <= 3))(go)

    for k in (1, 2, 3):
        for up in (True, False):
            plan.at(t0 + k * tz, functools.partial(step, k, up))

    def finish(zz):
        s = zz * 2 + 1 - h.x
        remote(out.at[s], out.at[s], xs.at[zz], xr.at[zz], ctx=h.xn).wait_recv()

    def drain():
        for k in range(3):
            pl.when((h.z >= k) & (h.z < 3))(lambda: hop(k, True).wait_send())
            pl.when((h.z + k <= 3) & (h.z > 0))(lambda: hop(k, False).wait_send())
        for zz in range(4):
            level(zz).wait_send()

    plan.at(t0 + 0.85 * tx, local.wait)
    plan.at(t0 + 4.5 * tx, drain)
    return finish


def scatter8_scratch(rows, width):
    few = pltpu.VMEM((3, rows, width), BF)
    return [pltpu.VMEM((4, rows, width), BF), few, few] + [DMA((4,))] * 4


N_SCATTER8 = 7


def scatter8(plan, h, part, out, scratch, starts, totals, end):
    ra, sz, rz, as_, ar, zs, zr = scratch

    def place(k):
        return jnp.bitwise_xor(h.z, k)

    def first(i, k):
        return remote(part.at[place(k), 1 - h.x], ra.at[i], as_.at[i], ar.at[i], ctx=h.xn)

    def second(k):
        return remote(sz.at[k - 1], rz.at[k - 1], zs.at[k], zr.at[k], ctx=place(k) * 4 + h.xy)

    def total(i, k):
        first(i, k).wait_recv()
        value = part[place(k), h.x].astype(F32) + ra[i].astype(F32)
        if k:
            sz[k - 1] = value.astype(BF)
            second(k).start()
        else:
            out[...] = value

    def last():
        for k in (1, 2, 3):
            second(k).wait_recv()
        out[...] += rz[0].astype(F32) + rz[1].astype(F32) + rz[2].astype(F32)
        for k in (1, 2, 3):
            second(k).wait_send()
        for i, k in enumerate((1, 2, 3, 0)):
            first(i, k).wait_send()

    for i, k in enumerate((1, 2, 3, 0)):
        plan.at(starts[i], lambda i=i, k=k: first(i, k).start())
        plan.at(totals[i], functools.partial(total, i, k))
    plan.at(end, last)


DEAL8_SEMS = [DMA((8,))] * 2 + [DMA]


def deal8(plan, h, piece, put, sems, t0, t1):
    ss, sr, own = sems
    row = h.z * 2 + h.x

    def place(r):
        return (r // 2) * 4 + h.y * 2 + lax.rem(r, 2)

    def send(step):
        to = jnp.bitwise_xor(row, step)
        return remote(piece(to), put(row), ss.at[step], sr.at[step], ctx=place(to))

    def got(step):
        at = jnp.bitwise_xor(row, step)
        return remote(put(at), put(at), ss.at[step], sr.at[step], ctx=place(at))

    local = pltpu.make_async_copy(piece(row), put(row), own)

    def start():
        for step in (7, 5, 6, 4, 3, 2, 1):
            send(step).start()
        local.start()

    def end():
        for step in (7, 5, 6, 4, 3, 2, 1):
            got(step).wait_recv()
        local.wait()

    def drain():
        for step in (7, 5, 6, 4, 3, 2, 1):
            send(step).wait_send()

    plan.at(t0, start)
    plan.at(t1, end)
    plan.at(t1 + 40, drain)

ROWS = 256


def _tri():
    i = lax.broadcasted_iota(jnp.int32, (ROWS, ROWS), 0)
    j = lax.broadcasted_iota(jnp.int32, (ROWS, ROWS), 1)
    return i <= j


def _heads(value):
    lane = lax.broadcasted_iota(jnp.int32, value.shape, 1)
    zero = jnp.zeros_like(value)
    return jnp.where(lane < 64, value, zero), jnp.where(lane >= 64, value, zero)


def _nt(a, b):
    return lax.dot_general(a, b, (((1,), (1,)), ((), ())), preferred_element_type=F32)


def _tn(a, b):
    return lax.dot_general(a, b, (((0,), (0,)), ((), ())), preferred_element_type=F32)


def _nn(a, b):
    return jnp.dot(a, b, preferred_element_type=F32)


def _scores(keys, query, tri):
    scores = _nt(keys, query)
    n = keys.shape[0]
    low = jnp.where(tri, scores[n - ROWS :], -1e30)
    return low if n == ROWS else jnp.concatenate([scores[: n - ROWS], low], 0)


def sort_rows(order_ref, src, dst):
    for b in range(src.shape[0]):
        dst[b * 64 : (b + 1) * 64, :] = src[order_ref[b]]


def attend_step(i, qs, ks, vs, os, lse):
    tri = _tri()
    n = (i + 1) * ROWS
    mine = slice(i * ROWS, n)
    total = None
    for head, query in enumerate(_heads(qs[mine, :] * BF(0.125))):
        scores = _scores(ks[:n, :], query, tri)
        top = jnp.max(scores, 0, keepdims=True)
        raw = jnp.exp(scores - top)
        size = jnp.sum(raw, 0, keepdims=True)
        lse[head : head + 1, mine] = top + jnp.log(size)
        probs = (raw * (1.0 / size)).astype(BF)
        part = _tn(probs, _heads(vs[:n, :])[head])
        total = part if total is None else total + part
    os[mine, :] = total.astype(BF)


def back_step(i, qs, ks, vs, gs, lse, dq, dk, dv):
    tri = _tri()
    n = (i + 1) * ROWS
    mine = slice(i * ROWS, n)
    total = None
    queries = _heads(qs[mine, :] * BF(0.125))
    grads = _heads(gs[mine, :])
    for head in range(2):
        scores = _scores(ks[:n, :], queries[head], tri)
        probs = jnp.exp(scores - lse[head : head + 1, mine])
        gp = _nt(vs[:n, :], grads[head])
        delta = jnp.sum(probs * gp, 0, keepdims=True)
        ds = (probs * (gp - delta)).astype(BF)
        dv[:n, :] += _nn(probs.astype(BF), grads[head])
        dk[:n, :] += _nn(ds, queries[head])
        part = _tn(ds, _heads(ks[:n, :])[head])
        total = part if total is None else total + part
    dq[mine, :] = total * 0.125


def swap_halves(values):
    lane = lax.broadcasted_iota(jnp.int32, values.shape, 1)
    return jnp.where(lax.rem(lane, 64) < 32, pltpu.roll(values, 96, 1), pltpu.roll(values, 32, 1))


from jax.sharding import PartitionSpec as P

HEADS = 32
HD = 64
EPSILON = 1e-05
THETA_BASE = 130000.0
ANY = pl.BlockSpec(memory_space=pl.ANY)
INNER = pl.BlockSpec(memory_space=pltpu.VMEM)


def comm_call(kernel, outs, out_specs, in_specs, scratch, cid, name, vmem=40):
    return pl.pallas_call(
        kernel,
        out_shape=outs,
        in_specs=in_specs,
        out_specs=out_specs,
        scratch_shapes=scratch,
        compiler_params=pltpu.CompilerParams(
            collective_id=cid, has_side_effects=True, vmem_limit_bytes=vmem << 20
        ),
        name=name,
    )


def take(refs, n):
    head, refs[:] = refs[:n], refs[n:]
    return head


def columns(src, width):
    return lambda c: src.at[:, pl.ds(pl.multiple_of(c * width, 128), width)]


def columns_of(out, width):
    return lambda c: out.at[:, pl.ds(pl.multiple_of(c * width, 128), width)]


def deal_columns(plan, h, src, out, sems, t0, t1, relay_from, lanes=None):
    lanes = pl.ds(0, out.shape[3]) if lanes is None else lanes
    deal16(
        plan, h, columns(src, lanes.size), lambda c: out.at[c, h.core, :, lanes], lambda c, core: out.at[c, core, :, lanes],
        sems, t0, t1, relay_from=relay_from,
    )


SPREAD = ((22, 83, 140, 200), (60, 97, 160, 201), (84, 125, 190, 202))


def spread_columns(plan, h, src, out, sems, t0, t1, t2, t3):
    ys, yr, cs, cr = sems[3].at[0], sems[3].at[1], sems[3].at[2], sems[3].at[3]
    w = out.shape[5]
    deal8(
        plan, h, lambda r: src.at[:, pl.ds(pl.multiple_of(r * w, 128), w)],
        lambda r: out.at[r // 2, h.y, lax.rem(r, 2), h.core], sems[:3], t0, t1,
    )
    mine, theirs = out.at[:, h.y, :, h.core], out.at[:, 1 - h.y, :, h.core]
    over_y = remote(mine, mine, ys, yr, ctx=h.yn)
    all_mine, all_other = out.at[:, :, :, h.core], out.at[:, :, :, 1 - h.core]
    over_core = remote(all_mine, all_mine, cs, cr, fsdp=1 - h.core)
    plan.at(t1 + 0.5, over_y.start)

    def pass_on():
        remote(theirs, theirs, ys, yr, ctx=h.yn).wait_recv()
        over_core.start()

    def end():
        remote(all_other, all_other, cs, cr, fsdp=1 - h.core).wait_recv()
        over_y.wait_send()
        over_core.wait_send()

    plan.at(t2, pass_on)
    plan.at(t3, end)


def front_kernel(
    order, table, x, wq, wk, wv, wg, wu, wd, wo, cot, tile, cos, sin,
    normed, w_out, gains, qs, ks, vs, lse, low, hidden, mlp_in, g_out, u_out, d_out, o_out, c_out, *refs
):
    refs = list(refs)
    xg, wqkv, tiles, stage, q, k_rows, v, o, o_rows, w_part = take(refs, 10)
    stage_sem, send, recv, w_sems = take(refs, 4)
    rows, width = x.shape
    h = Here()
    greet_all(h)
    plan = Plan()
    for i, src in enumerate((wq, wk, wv)):
        deal_columns(plan, h, src, wqkv, take(refs, 5), 0, 16, 10, pl.ds(i * 128, 128))
    deal16(
        plan, h, lambda c: tile, lambda c: tiles.at[c, h.core], lambda c, core: tiles.at[c, core], take(refs, 5), 0, 17,
        relay_from=11,
    )
    done = gather16(plan, h, x, xg, take(refs, 13), 0, 14, 20, by_plane=True)
    for i, (src, out) in enumerate(((wg, g_out), (wu, u_out), (wd, d_out))):
        spread_columns(plan, h, src, out, take(refs, 4), *SPREAD[i])
    gather16(plan, h, wo, o_out.at[:, h.core], take(refs, 13), 98, 10, 14)
    seen = gather8(plan, h, cot, c_out, take(refs, 7), 82.5, 18, 20)
    plan.at(185, lambda: [seen(zz) for zz in range(4)])
    to_sems = take(refs, 5)
    mine, other = o_out.at[:, h.core], o_out.at[:, 1 - h.core]
    across = remote(mine, mine, send, recv, fsdp=1 - h.core)
    plan.at(165, across.start)

    def plane(k):
        return jnp.bitwise_xor(h.z, k)

    def put_normed(k):
        at = pl.ds(pl.multiple_of(plane(k) * 4 * rows, 4 * rows), 4 * rows)
        return pltpu.make_async_copy(stage, normed.at[at], stage_sem)

    def spread_gains():
        gains[...] = jnp.zeros_like(gains)
        for c in range(16):
            both = tiles[c, 0].astype(F32) + tiles[c, 1].astype(F32)
            gains[:, c * 128 : (c + 1) * 128] = both[0:8]

    def work(k):
        zz = plane(k)
        done(zz)
        if k:
            put_normed(k - 1).wait()
        else:
            spread_gains()
        for p in range(2):
            at = pl.ds(pl.multiple_of((zz * 4 + p * 2) * rows, 2 * rows), 2 * rows)
            blocks = pl.ds(zz * 8 + p * 4, 4)
            value = xg[pl.ds(zz * 4 + p * 2, 2)].reshape(2 * rows, width).astype(F32)
            inverse = lax.rsqrt(jnp.mean(value * value, -1, keepdims=True) + EPSILON)
            value = (value * inverse * gains[0:1, :]).astype(BF)
            stage[p * 2 * rows : (p + 1) * 2 * rows, :] = value
            pre = _nn(value, wqkv[...].reshape(width, 384))
            for i, out in enumerate((q, k_rows)):
                part = pre[:, i * 128 : (i + 1) * 128]
                turned = part * cos[at, :] + swap_halves(part) * sin[at, :]
                out[blocks] = turned.astype(BF).reshape(4, 64, 128)
            v[blocks] = pre[:, 256:].astype(BF).reshape(4, 64, 128)
        put_normed(k).start()

    for k in range(4):
        plan.at((24, 42, 62, 82)[k], functools.partial(work, k))

    def sort():
        put_normed(3).wait()
        for a, b in ((q, qs), (k_rows, ks), (v, vs)):
            sort_rows(order, a, b)
        w_out[...] = wqkv[...].reshape(width, 384)

    plan.at(83, sort)
    for i in range(16 * rows // ROWS):
        plan.at(84 + 1.3 * i, functools.partial(attend_step, i, qs, ks, vs, o.reshape(16 * rows, 128), lse))

    def unsort():
        for b in range(32):
            o_rows[b // 2, (b % 2) * 64 : (b % 2 + 1) * 64, :] = o[table[b]]

    plan.at(96, unsort)
    deal16(plan, h, lambda c: o_rows.at[c], columns_of(low, 128), None, to_sems, 96.1, 172, both=False)

    def end():
        remote(other, other, send, recv, fsdp=1 - h.core).wait_recv()
        across.wait_send()

    def load(b):
        return pltpu.make_async_copy(o_out.at[pl.ds(4 * b, 4)], w_part.at[b % 2], w_sems.at[b % 2])

    def project():
        load(0).start()
        load(1).start()
        total = x[...].astype(F32)
        for b in range(4):
            load(b).wait()
            depth = width // 4
            total = total + _nn(low[:, b * depth : (b + 1) * depth], w_part[b % 2].reshape(depth, width))
            if b + 2 < 4:
                load(b + 2).start()
        hidden[...] = total
        inverse = lax.rsqrt(jnp.mean(total * total, -1, keepdims=True) + EPSILON)
        mlp_in[...] = (total * inverse * gains[1:2, :]).astype(BF)

    plan.at(173, end)
    plan.at(176, project)
    plan.run()


def front(order, table, x, wq, wk, wv, wg, wu, wd, wo, cot, tile, cos, sin):
    rows, width = x.shape
    length = 16 * rows
    block = jax.ShapeDtypeStruct((4, 2, 2, 2, wg.shape[0], wg.shape[1] // 8), BF)
    heads = jax.ShapeDtypeStruct((length, 128), BF)
    outs = (
        jax.ShapeDtypeStruct((length, width), BF), jax.ShapeDtypeStruct((width, 384), BF),
        jax.ShapeDtypeStruct((8, width), F32), heads, heads, heads, jax.ShapeDtypeStruct((2, length), F32),
        jax.ShapeDtypeStruct((rows, width), BF), jax.ShapeDtypeStruct((rows, width), F32),
        jax.ShapeDtypeStruct((rows, width), BF), block, block, block,
        jax.ShapeDtypeStruct((16, 2) + wo.shape, BF), jax.ShapeDtypeStruct((8, rows, width), BF),
    )
    smem = pl.BlockSpec(memory_space=pltpu.SMEM)
    scratch = [
        pltpu.VMEM((16, rows, width), BF), pltpu.VMEM((16, 2, wq.shape[0], 384), BF), pltpu.VMEM((16, 2) + tile.shape, BF),
        pltpu.VMEM((4 * rows, width), BF), *[pltpu.VMEM((32, 64, 128), BF)] * 4, pltpu.VMEM((16, rows, 128), BF),
        pltpu.VMEM((2, 4, 2) + wo.shape, BF), DMA, DMA, DMA, DMA((2,)),
    ]
    scratch += DEAL_SEMS * 4 + GATHER_SEMS + (DEAL8_SEMS + [DMA((4,))]) * 3 + GATHER_SEMS + GATHER8_SEMS + DEAL_SEMS
    return comm_call(
        front_kernel, outs, [ANY] + [INNER] * 9 + [ANY] * 5, [smem] * 2 + [INNER] + [ANY] * 8 + [INNER] * 3, scratch, 0,
        "front", 58,
    )(order, table, x, wq, wk, wv, wg, wu, wd, wo, cot, tile, cos, sin)


def mlp_kernel(src, cot, bg, bu, bd, gmi, out_part, sum_g, own_u, d_home, *refs):
    refs = list(refs)
    xm, ct, wg, wu, wd, grads, act, part, stage, cols = take(refs, 10)
    own_g, other_g, got_g, other_u, got_u, own_d, other_d, got_d, sum_d = take(refs, 9)
    w_sem, ct_sem, cols_sem, stage_sem, ex_sems = take(refs, 5)
    rows, width = src.shape
    hidden = wg.shape[1]
    block = own_d.shape[1]
    h = Here()
    loads = [pltpu.make_async_copy(a, b, w_sem.at[i]) for i, (a, b) in enumerate(((bg, wg), (bu, wu), (bd, wd)))]

    def plane(k):
        return jnp.bitwise_xor(h.z, k)

    def load_cot(k):
        return pltpu.make_async_copy(cot.at[pl.ds(plane(k) * 2, 2)], ct.at[k % 2], ct_sem.at[k % 2])

    def put_out(k):
        return pltpu.make_async_copy(stage, out_part.at[pl.ds(plane(k) * 2, 2)], stage_sem)

    for c in loads + [load_cot(0), load_cot(1)]:
        c.start()
    greet_all(h)
    plan = Plan()
    done = gather8(plan, h, src, xm, take(refs, 7), 0, 12, 12)

    def work(k):
        zz = plane(k)
        done(zz)
        if k == 0:
            for c in loads:
                c.wait()
        load_cot(k).wait()
        if k:
            put_out(k - 1).wait()
        at = pl.ds(pl.multiple_of(zz * 2 * rows, 2 * rows), 2 * rows)
        x = xm[pl.ds(zz * 2, 2)].reshape(2 * rows, width)
        gate, up = _nn(x, wg[...]), _nn(x, wu[...])
        sig = jax.nn.sigmoid(gate)
        silu = gate * sig
        low = (silu * up).astype(BF)
        act[at, :] = low
        stage[...] = _nt(low, wd[...]).astype(BF).reshape(2, rows, width)
        grad = _nn(ct[k % 2].reshape(2 * rows, width), wd[...])
        grad_gate = (grad * up * sig * (1.0 + gate * (1.0 - sig))).astype(BF)
        grad_up = (grad * silu).astype(BF)
        grads[at, pl.ds(0, hidden)] = grad_gate
        grads[at, pl.ds(hidden, hidden)] = grad_up
        back = _nt(grad_gate, wg[...]) + _nt(grad_up, wu[...])
        part[zz] = back.astype(BF).reshape(2, rows, width)
        put_out(k).start()
        if k + 2 < 4:
            load_cot(k + 2).start()

    for k in range(4):
        plan.at((15, 26, 38, 50)[k], functools.partial(work, k))
    plan.at(55, lambda: put_out(3).wait())
    scatter8(plan, h, part, gmi, take(refs, N_SCATTER8), (27, 39, 50.2, 50.3), (50.4, 58.5, 66.5, 75), 110)

    def split(c, both, own, other):
        both = both.astype(BF).reshape(2, block, both.shape[1])
        own[c] = jnp.where(h.core == 0, both[0], both[1])
        other[c] = jnp.where(h.core == 0, both[1], both[0])

    def exchange(i, other, got):
        return remote(other, got, ex_sems.at[i], ex_sems.at[3 + i], fsdp=1 - h.core)

    def load_cols(c):
        slot = lax.rem(c, 2)
        at = pl.ds(pl.multiple_of(c * 2 * block, 128), 2 * block)
        return pltpu.make_async_copy(cot.at[:, :, at], cols.at[slot], cols_sem.at[slot])

    def grads_up(first, lanes, own, other):
        def one(c, carry):
            at = pl.ds(pl.multiple_of(c * 2 * block, 128), 2 * block)
            lhs = xm[:, :, at].reshape(8 * rows, 2 * block)
            split(c, _tn(lhs, grads[:, lanes]), own, other)
            return carry

        lax.fori_loop(first, first + 4, one, 0)

    def grads_d(first):
        def one(c, carry):
            pl.when(c < 15)(lambda: load_cols(c + 1).start())
            load_cols(c).wait()
            lhs = cols[lax.rem(c, 2)].reshape(8 * rows, 2 * block)
            split(c, _tn(lhs, act[...]), own_d, other_d)
            return carry

        lax.fori_loop(first, first + 4, one, 0)

    def over_y(i, own, result):
        own, result = own.reshape(4, 2, 2, *own.shape[1:]), result.reshape(4, 2, *own.shape[1:])
        return remote(own.at[:, 1 - h.y], result, ex_sems.at[6 + i], ex_sems.at[8 + i], ctx=h.yn)

    def join(i, own, other, got, result):
        exchange(i, other, got).wait_recv()
        for c in range(16):
            own[c] = (own[c].astype(F32) + got[c].astype(F32)).astype(BF)
        over_y(i, own, result).start()

    def join_u():
        exchange(2, other_u, got_u).wait_recv()
        for c in range(16):
            own_u[c] = (own_u[c].astype(F32) + got_u[c].astype(F32)).astype(BF)
        exchange(2, other_u, got_u).wait_send()

    def add_y(i, own, other, got, result):
        over_y(i, own, result).wait_recv()
        for r in range(8):
            z, x = r // 2, r % 2
            mine = jnp.where(h.y == 0, own[z * 4 + x], own[z * 4 + 2 + x])
            result[r] = (mine.astype(F32) + result[r].astype(F32)).astype(BF)

    def sent(i, own, other, got, result):
        exchange(i, other, got).wait_send()
        over_y(i, own, result).wait_send()

    d, g = (own_d, other_d, got_d, sum_d), (own_g, other_g, got_g, sum_g)
    lo, hi = slice(0, hidden), slice(hidden, 2 * hidden)
    plan.at(50.5, lambda: load_cols(0).start())
    for i in range(4):
        plan.at(56 + 2 * i, functools.partial(grads_d, 4 * i))
        plan.at(65 + 2 * i, functools.partial(grads_up, 4 * i, lo, own_g, other_g))
        plan.at(75 + 2 * i, functools.partial(grads_up, 4 * i, hi, own_u, other_u))
    plan.at(64, lambda: exchange(1, other_d, got_d).start())
    plan.at(68, lambda: join(1, *d))
    plan.at(73, lambda: exchange(0, other_g, got_g).start())
    plan.at(78, lambda: join(0, *g))
    plan.at(83, lambda: exchange(2, other_u, got_u).start())
    plan.at(87, join_u)
    plan.at(90, lambda: add_y(1, *d))
    deal8(plan, h, lambda r: sum_d.at[r], columns_of(d_home, hidden), take(refs, 3), 90.1, 200)
    plan.at(112, lambda: add_y(0, *g))
    plan.at(201, lambda: [sent(1, *d), sent(0, *g)])
    plan.run()


def mlp(src, cot, bg, bu, bd):
    rows, width = src.shape
    block, hidden = bg.shape[4:]
    full = pltpu.VMEM((width, hidden), BF)
    d = pltpu.VMEM((16, block, hidden), BF)
    scratch = [
        pltpu.VMEM((8, rows, width), BF), pltpu.VMEM((2, 2, rows, width), BF), full, full, full,
        pltpu.VMEM((8 * rows, 2 * hidden), BF), pltpu.VMEM((8 * rows, hidden), BF),
        pltpu.VMEM((4, 2, rows, width), BF), pltpu.VMEM((2, rows, width), BF),
        pltpu.VMEM((2, 8, rows, 2 * block), BF), *[d] * 8,
        pltpu.VMEM((8, block, hidden), BF),
        DMA((3,)), DMA((2,)), DMA((2,)), DMA, DMA((10,)),
    ]
    scratch += GATHER8_SEMS + scatter8_scratch(rows, width) + DEAL8_SEMS
    outs = (
        jax.ShapeDtypeStruct((rows, width), F32), jax.ShapeDtypeStruct((8, rows, width), BF),
        jax.ShapeDtypeStruct((8, block, hidden), BF), jax.ShapeDtypeStruct((16, block, hidden), BF),
        jax.ShapeDtypeStruct((block, 8 * hidden), BF),
    )
    return comm_call(mlp_kernel, outs, [INNER, ANY, INNER, INNER, ANY], [ANY] * 5, scratch, 5, "mlp", 62)(
        src, cot, *(b.reshape(width, hidden) for b in (bg, bu, bd))
    )


def outer_home(plan, h, left, right, own, other, got, send, recv, t0, t1):
    rows = own.shape[1]
    over = remote(other, got, send, recv, fsdp=1 - h.core)

    def compute():
        mine, theirs = pl.multiple_of(h.core * rows, rows), pl.multiple_of((1 - h.core) * rows, rows)
        for c in range(16):
            lhs = left[:, c * 2 * rows : (c + 1) * 2 * rows]
            both = _tn(lhs, right[...]).astype(BF).reshape(2, rows, right.shape[1])
            own[c] = jnp.where(h.core == 0, both[0], both[1])
            other[c] = jnp.where(h.core == 0, both[1], both[0])
        over.start()

    def add():
        over.wait_recv()
        for c in range(16):
            own[c] = (own[c].astype(F32) + got[c].astype(F32)).astype(BF)
        over.wait_send()

    plan.at(t0, compute)
    plan.at(t1, add)


def back_kernel(order, table, wo, qs, ks, vs, lse, cos, sin, out_part, low, branch, sum_g, own_u, dqkv, out_sum, wo_sum, sum_u, g_home, *refs):
    refs = list(refs)
    ga, w_part, gh, gs, dq, dk, dv, own, other, got = take(refs, 10)
    w_sems = take(refs, 1)[0]
    send, recv = take(refs, 2)
    gh_rows = gh.reshape(16, ga.shape[0], 128)
    flat = [g.reshape(qs.shape) for g in (dq, dk, dv)]
    h = Here()
    depth = w_part.shape[1]

    def load(b):
        return pltpu.make_async_copy(wo.at[pl.ds(b * depth, depth)], w_part.at[b % 2], w_sems.at[b % 2])

    load(0).start()
    load(1).start()
    greet_all(h)
    plan = Plan()

    def project():
        for b in range(wo.shape[0] // depth):
            load(b).wait()
            ga[:, b * depth : (b + 1) * depth] = _nt(branch[...], w_part[b % 2]).astype(BF)
            if b + 2 < wo.shape[0] // depth:
                load(b + 2).start()

    plan.at(0.5, project)
    deal16(plan, h, columns(ga, 128), lambda c: gh_rows.at[c], None, take(refs, 5), 0.6, 14, both=False)
    gu_sems = take(refs, 3)
    scatter8(plan, h, out_part, out_sum, take(refs, N_SCATTER8), (0.1, 15.6, 27, 40), (15.4, 27.1, 38.8, 50.8), 94)
    outer_home(plan, h, low, branch, own, other, got, send, recv, 2, 8)
    deal8(plan, h, lambda r: sum_g.at[r], columns_of(g_home, sum_g.shape[2]), gu_sems, 0.3, 198)
    half_u, u_sems = take(refs, 2)
    split_u = own_u.reshape(4, 2, 2, *own_u.shape[1:])
    over_u = remote(split_u.at[:, 1 - h.y], sum_u, u_sems.at[0], u_sems.at[1], ctx=h.yn)
    keep_u = pltpu.make_async_copy(split_u.at[:, h.y], half_u, u_sems.at[2])

    def start_u():
        over_u.start()
        keep_u.start()

    def end_u():
        over_u.wait_recv()
        keep_u.wait()
        for z in range(4):
            sum_u[z] = (sum_u[z].astype(F32) + half_u[z].astype(F32)).astype(BF)
        over_u.wait_send()

    plan.at(0.2, start_u)
    plan.at(90, end_u)
    scatter16(plan, h, own.reshape(4, 2, 2, *own.shape[1:]), wo_sum, take(refs, N_SCATTER), 8.1, 18)

    def begin():
        sort_rows(order, gh, gs)
        dk[...] = jnp.zeros_like(dk)
        dv[...] = jnp.zeros_like(dv)

    plan.at(15, begin)
    for i in range(qs.shape[0] // ROWS):
        plan.at(16 + 2.2 * i, functools.partial(back_step, i, qs, ks, vs, gs, lse, *flat))

    def end():
        for b in range(32):
            rows = slice(b * 64, (b + 1) * 64)
            for i, grad in enumerate((dq, dk)):
                value = grad[table[b]]
                turned = swap_halves(value)
                dqkv[rows, i * 128 : (i + 1) * 128] = (value * cos[rows, :] - turned * sin[rows, :]).astype(BF)
            dqkv[rows, 256:] = dv[table[b]].astype(BF)

    plan.at(34.5, end)
    plan.run()


def back(order, table, wo, qs, ks, vs, lse, cos, sin, out_part, low, branch, sum_g, own_u):
    rows, width = low.shape
    length = qs.shape[0]
    smem = pl.BlockSpec(memory_space=pltpu.SMEM)
    half = pltpu.VMEM((16, width // 32, width), BF)
    outs = (
        jax.ShapeDtypeStruct((length, 384), BF),
        jax.ShapeDtypeStruct((rows, width), F32),
        jax.ShapeDtypeStruct((width // 32, width), F32),
        jax.ShapeDtypeStruct((4, 2) + sum_g.shape[1:], BF),
        jax.ShapeDtypeStruct((sum_g.shape[1], 8 * sum_g.shape[2]), BF),
    )
    scratch = [pltpu.VMEM((rows, width), BF), pltpu.VMEM((2, width // 4, width), BF)]
    scratch += [pltpu.VMEM((32, 64, 128), BF), pltpu.VMEM((length, 128), BF)]
    scratch += [pltpu.VMEM((32, 64, 128), F32)] * 3 + [half] * 3 + [DMA((2,))] + [DMA] * 2 + DEAL_SEMS + DEAL8_SEMS
    scratch += scatter8_scratch(rows, width) + [pltpu.VMEM((4, 2) + sum_g.shape[1:], BF), DMA((3,))]
    scratch += scatter_scratch(width // 32, width)
    return comm_call(back_kernel, outs, [INNER] * 4 + [ANY], [smem] * 2 + [ANY] + [INNER] * 9 + [ANY] * 2, scratch, 6, "back", 60)(
        order, table, wo, qs, ks, vs, lse, cos, sin, out_part.reshape(4, 2, rows, width), low, branch, sum_g, own_u
    )


def home_kernel(
    dqkv, wqkv, normed, gd, gg, gu, x, grad_hidden, gain, wq, wk, wv, wg, wu,
    input_grad, q_out, k_out, v_out, gain_a, gain_m, d_out, g_out, u_out, *refs
):
    refs = list(refs)
    part, nm, own, other, got, landed, d32, g32, u16, u32, gn = take(refs, 11)
    nm_sem, ex_sems, out_sems = take(refs, 3)
    rows, width = x.shape
    block = own.shape[1]
    h = Here()
    load = pltpu.make_async_copy(normed, nm, nm_sem)
    load.start()
    greet_all(h)
    plan = Plan()
    deal8(plan, h, lambda r: gu.at[r], columns_of(u16, gu.shape[2]), take(refs, 3), 0.4, 90)

    def plane(k):
        zz = jnp.bitwise_xor(h.z, k)
        for p in range(2):
            at = pl.ds(pl.multiple_of((zz * 4 + p * 2) * rows, 2 * rows), 2 * rows)
            part[zz, pl.ds(p, 1)] = _nt(dqkv[at, :], wqkv[...]).astype(BF).reshape(1, 2, rows, width)

    for i, k in enumerate((1, 2, 3, 0)):
        plan.at((0.1, 1, 2, 3)[i], functools.partial(plane, k))
    scatter16(plan, h, part, gn, take(refs, N_SCATTER), 0.2, 20)
    plan.at(4, load.wait)

    def grads(first):
        def one(c, carry):
            at = pl.ds(pl.multiple_of(c * 2 * block, 128), 2 * block)
            both = _tn(nm[:, at], dqkv[...]).astype(BF).reshape(2, block, 384)
            own[c] = jnp.where(h.core == 0, both[0], both[1])
            other[c] = jnp.where(h.core == 0, both[1], both[0])
            return carry

        lax.fori_loop(first, first + 4, one, 0)

    for i in range(4):
        plan.at(4.1 + i, functools.partial(grads, 4 * i))
    over = remote(other, got, ex_sems.at[0], ex_sems.at[1], fsdp=1 - h.core)
    plan.at(8, over.start)

    def join():
        over.wait_recv()
        for c in range(16):
            own[c] = (own[c].astype(F32) + got[c].astype(F32)).astype(BF)
        over.wait_send()

    plan.at(10, join)
    deal16(plan, h, lambda c: own.at[c], lambda c: landed.at[c], None, take(refs, 5), 10.1, 91, both=False)
    writes = [
        pltpu.make_async_copy(a, b, out_sems.at[i]) for i, (a, b) in enumerate(((d32, d_out), (g32, g_out), (u32, u_out)))
    ]

    def widen(i, source, target):
        target[...] = source[...].astype(F32)
        writes[i].start()

    plan.at(15, functools.partial(widen, 0, gd, d32))
    plan.at(25, functools.partial(widen, 1, gg, g32))
    plan.at(92, functools.partial(widen, 2, u16, u32))

    def finish_qkv():
        for c in range(16):
            for i, out in enumerate((q_out, k_out, v_out)):
                out[:, c * 128 : (c + 1) * 128] = landed[c, :, i * 128 : (i + 1) * 128].astype(F32)

    def sums():
        terms = ((wq, q_out), (wk, k_out), (wv, v_out))
        gain_a[...] = sum(jnp.sum(w[...].astype(F32) * g[...], -1, keepdims=True) for w, g in terms)
        terms = ((wg, g32), (wu, u32))
        gain_m[...] = sum(jnp.sum(w[...].astype(F32) * g[...], -1, keepdims=True) for w, g in terms)

    plan.at(93, finish_qkv)
    plan.at(94, sums)

    def result():
        value = x[...].astype(F32)
        inverse = lax.rsqrt(jnp.mean(value * value, -1, keepdims=True) + EPSILON)
        scaled = gn[...] * gain[0:1, :]
        inner = jnp.sum(scaled * value, -1, keepdims=True)
        input_grad[...] = (
            grad_hidden[...] + inverse * scaled - inverse * inverse * inverse / width * value * inner
        )

    plan.at(202, result)
    plan.at(300, lambda: [w.wait() for w in writes])
    plan.run()


def home(dqkv, wqkv, normed, gd, gg, gu, x, grad_hidden, gain, wq, wk, wv, wg, wu):
    rows, width = x.shape
    block, wide = gd.shape
    third = pltpu.VMEM((16, block, 384), BF)
    column = jax.ShapeDtypeStruct((block, 1), F32)
    wide32 = pltpu.VMEM((block, wide), F32)
    small = jax.ShapeDtypeStruct((block, width), F32)
    large = jax.ShapeDtypeStruct((block, wide), F32)
    outs = (
        jax.ShapeDtypeStruct((rows, width), F32), small, small, small, column, column, large, large, large
    )
    scratch = [
        pltpu.VMEM((4, 2, 2, rows, width), BF), pltpu.VMEM(normed.shape, BF), third, third, third, third, wide32, wide32,
        pltpu.VMEM((block, wide), BF), wide32, pltpu.VMEM((rows, width), F32),
        DMA, DMA((2,)), DMA((3,)),
    ]
    scratch += DEAL8_SEMS + scatter_scratch(rows, width) + DEAL_SEMS
    return comm_call(
        home_kernel, outs, [INNER] * 6 + [ANY] * 3, [INNER, INNER, ANY, INNER, INNER, ANY] + [INNER] * 8, scratch, 7, "home", 60
    )(dqkv, wqkv, normed, gd, gg, gu, x, grad_hidden, gain, wq, wk, wv, wg, wu)


def rope_tables(positions):
    inv_freq = THETA_BASE ** (-(jnp.arange(HD // 2, dtype=F32) * 2.0 / HD))
    angles = positions.astype(F32)[:, None] * inv_freq[None, :]
    return jnp.tile(jnp.cos(angles), (1, 4)), jnp.tile(jnp.sin(angles), (1, 4))


def swap(values):
    a, b, c, d = jnp.split(values, 4, -1)
    return jnp.concatenate([b, a, d, c], -1)


def fast_body(x, table, attn_gain, wq, wk, wv, wo, mlp_gain, wg, wu, wd, cot):
    x, cot, table = x[0], cot[0], table[0].reshape(32)
    rows, width = x.shape
    length = rows * 16
    core = lax.axis_index("fsdp")
    slots = jnp.arange(32, dtype=jnp.int32)
    order = jnp.sum(jnp.where(table[None, :] == slots[:, None], slots[None, :], 0), 1)
    positions = (table[:, None] * 64 + jnp.arange(64, dtype=jnp.int32)[None]).reshape(length)
    cos, sin = rope_tables(positions)
    turn = jnp.where(jnp.arange(128) % 64 < 32, -1.0, 1.0).astype(F32)
    sin = sin * turn

    def dot(a, b):
        return jnp.dot(a, b, preferred_element_type=F32)

    def dot_nt(a, b):
        return lax.dot_general(a, b, (((1,), (1,)), ((), ())), preferred_element_type=F32)

    def dot_tn(a, b):
        return lax.dot_general(a, b, (((0,), (0,)), ((), ())), preferred_element_type=F32)

    lane = jnp.arange(128) // 64
    tile = jnp.where(lane[None] == core, jnp.tile(jnp.stack([attn_gain, mlp_gain]), (1, 2)), 0)
    tile = jnp.pad(tile, ((0, 14), (0, 0)))
    normed, wqkv, gains, qs, ks, vs, lse, attn_low, hidden, mlp_in, bg, bu, bd, full_out, cot_all = front(
        order, table, x, wq, wk, wv, wg, wu, wd, wo, cot, tile, cos, sin
    )
    again, mgain = gains[0], gains[1]
    full_out = full_out.reshape(width, width)
    inv_mid = lax.rsqrt(jnp.mean(hidden * hidden, -1, keepdims=True) + EPSILON)
    gmi, out_part, sum_g, own_u, gd = mlp(mlp_in, cot_all, bg, bu, bd)

    def norm_back(grad, source, inv, gain):
        scaled = grad * gain
        inner = jnp.sum(scaled * source, -1, keepdims=True)
        return inv * scaled - inv * inv * inv / width * source * inner

    grad_hidden = cot.astype(F32) + norm_back(gmi, hidden, inv_mid, mgain)
    grad_branch = grad_hidden.astype(BF)
    grad_qkv, out_sum, wo_grad, sum_u, gg = back(
        order, table, full_out, qs, ks, vs, lse, cos, sin, out_part, attn_low, grad_branch, sum_g, own_u
    )
    layer_output = (hidden + out_sum).astype(BF)
    input_grad, gq, gk, gv, gain_a, gain_m, gd, gg, gu = home(
        grad_qkv, wqkv, normed, gd, gg, sum_u.reshape(sum_g.shape), x, grad_hidden, gains, wq, wk, wv, wg, wu
    )
    gain_a = gain_a[:, 0] / attn_gain.astype(F32)
    gain_m = gain_m[:, 0] / mlp_gain.astype(F32)
    return (layer_output[None], input_grad[None], gain_a, gq, gk, gv, wo_grad, gain_m, gg, gu, gd)


MASKED = -1e30


def general_tables(positions):
    inv_freq = THETA_BASE ** (-(jnp.arange(HD // 2, dtype=jnp.float32) * 2.0 / HD))
    angles = positions.astype(jnp.float32)[:, None] * inv_freq[None, :]
    cosine = jnp.cos(angles)
    sine_tab = jnp.sin(angles)
    return (jnp.concatenate([cosine, cosine], -1), jnp.concatenate([sine_tab, sine_tab], -1))


def rotate(values, cosine, sine_tab):
    middle = values.shape[-1] // 2
    turned = jnp.concatenate([-values[..., middle:], values[..., :middle]], -1)
    return values * cosine[:, None, :] + turned * sine_tab[:, None, :]


def rotate_back(grads_in, cosine, sine_tab):
    middle = grads_in.shape[-1] // 2
    shifted = grads_in * sine_tab[:, None, :]
    turned = jnp.concatenate([shifted[..., middle:], -shifted[..., :middle]], -1)
    return grads_in * cosine[:, None, :] + turned


def inverse_rms(rows_in):
    return lax.rsqrt(jnp.mean(rows_in * rows_in, -1, keepdims=True) + EPSILON)


def general_norm_back(grad_normed, rows_in, inverse, gain_vec):
    scaled = grad_normed * gain_vec
    inner_sum = jnp.sum(scaled * rows_in, -1, keepdims=True)
    return inverse * scaled - inverse * inverse * inverse / rows_in.shape[-1] * rows_in * inner_sum


def score_rows(query_rows, key_rows, query_pos, key_pos):
    scores = jnp.einsum(
        "qhd,khd->hqk", query_rows, key_rows, preferred_element_type=jnp.float32
    ) * HD ** (-0.5)
    visible = key_pos[None, None, :] <= query_pos[None, :, None]
    return (scores, visible)


def softmax_rows(scores, visible, log_total):
    return jnp.where(
        visible, jnp.exp(jnp.where(visible, scores - log_total[..., None], MASKED)), 0.0
    )


def walk_keys(kv_steps, top_pos, width, step_fn, initial):
    step_rows = kv_steps.shape[1]
    offsets = jnp.arange(step_rows, dtype=jnp.int32)

    def advance(carried, step_item):
        step_index, kv_block = step_item
        first_key = step_index * step_rows
        key_rows = kv_block[:, :width].reshape(step_rows, HEADS, HD)
        value_rows = kv_block[:, width:].reshape(step_rows, HEADS, HD)
        key_pos = first_key + offsets
        updated = lax.cond(
            first_key <= top_pos,
            lambda state: step_fn(state, key_rows, value_rows, key_pos),
            lambda state: state,
            carried,
        )
        return (updated, None)

    indices = jnp.arange(kv_steps.shape[0], dtype=jnp.int32)
    final_state, ignored = lax.scan(advance, initial, (indices, kv_steps))
    return final_state


def general_body(
    layer_input,
    block_table,
    attn_gain,
    query_weight,
    key_weight,
    value_weight,
    out_weight,
    mlp_gain,
    gate_weight,
    up_weight,
    down_weight,
    cotangent,
):
    tokens = layer_input.shape[1]
    width = layer_input.shape[2]
    half_rows = tokens // 2
    ranks = lax.axis_size("ctx")
    length = tokens * ranks
    score_scale = HD ** (-0.5)
    block_ids = block_table[0].reshape(2 * ranks)
    own_blocks = lax.dynamic_slice_in_dim(block_ids, lax.axis_index("ctx") * 2, 2)
    inner = jnp.arange(half_rows, dtype=jnp.int32)
    query_pos = (own_blocks[:, None] * half_rows + inner[None, :]).reshape(tokens)
    cosine, sine_tab = general_tables(query_pos)
    full_query, full_key, full_value, full_out, full_attn_gain = (
        lax.all_gather(query_weight, ("ctx", "fsdp"), axis=0, tiled=True),
        lax.all_gather(key_weight, ("ctx", "fsdp"), axis=0, tiled=True),
        lax.all_gather(value_weight, ("ctx", "fsdp"), axis=0, tiled=True),
        lax.all_gather(out_weight, ("ctx", "fsdp"), axis=0, tiled=True),
        lax.all_gather(attn_gain, ("ctx", "fsdp"), axis=0, tiled=True),
    )
    source = layer_input[0].astype(jnp.float32)
    inverse_in = inverse_rms(source)
    normed = (source * inverse_in * full_attn_gain.astype(jnp.float32)).astype(jnp.bfloat16)
    query_pre = jnp.dot(normed, full_query, preferred_element_type=jnp.float32).reshape(
        tokens, HEADS, HD
    )
    key_pre = jnp.dot(normed, full_key, preferred_element_type=jnp.float32).reshape(
        tokens, HEADS, HD
    )
    value_low = jnp.dot(normed, full_value, preferred_element_type=jnp.float32).astype(jnp.bfloat16)
    queries = rotate(query_pre, cosine, sine_tab).astype(jnp.bfloat16)
    keys_low = rotate(key_pre, cosine, sine_tab).astype(jnp.bfloat16).reshape(tokens, width)
    kv_dev = lax.all_gather(jnp.concatenate([keys_low, value_low], 1), "ctx", axis=0, tiled=True)
    slot_ids = jnp.arange(2 * ranks, dtype=jnp.int32)
    holder = jnp.sum(jnp.where(block_ids[None, :] == slot_ids[:, None], slot_ids[None, :], 0), 1)
    chosen = (holder[:, None] == slot_ids[None, :]).astype(jnp.bfloat16)
    kv_seq = jnp.einsum(
        "ab,bn->an", chosen, kv_dev.reshape(2 * ranks, half_rows * 2 * width)
    ).reshape(length, 2 * width)
    step_rows = min(512, length)
    kv_steps = kv_seq.reshape(length // step_rows, step_rows, 2 * width)
    log_totals = []
    attended_parts = []
    top_list = []
    for slot_index in range(2):
        slot_queries = queries[slot_index * half_rows : (slot_index + 1) * half_rows]
        slot_pos = query_pos[slot_index * half_rows : (slot_index + 1) * half_rows]
        top_pos = own_blocks[slot_index] * half_rows + half_rows - 1
        top_list.append(top_pos)

        def stat_step(state, key_rows, value_rows, key_pos):
            running, running_sum = state
            scores, visible = score_rows(slot_queries, key_rows, slot_pos, key_pos)
            scores = jnp.where(visible, scores, MASKED)
            newest = jnp.maximum(running, jnp.max(scores, -1))
            running_sum = running_sum * jnp.exp(running - newest) + jnp.sum(
                jnp.where(visible, jnp.exp(scores - newest[..., None]), 0.0), -1
            )
            return (newest, running_sum)

        start_state = (
            jnp.full((HEADS, half_rows), MASKED, jnp.float32),
            jnp.zeros((HEADS, half_rows), jnp.float32),
        )
        running, running_sum = walk_keys(kv_steps, top_pos, width, stat_step, start_state)
        log_total = running + jnp.log(running_sum)

        def value_step(accumulated, key_rows, value_rows, key_pos):
            scores, visible = score_rows(slot_queries, key_rows, slot_pos, key_pos)
            weights_low = softmax_rows(scores, visible, log_total).astype(jnp.bfloat16)
            return accumulated + jnp.einsum(
                "hqk,khd->qhd", weights_low, value_rows, preferred_element_type=jnp.float32
            )

        attended_parts.append(
            walk_keys(
                kv_steps, top_pos, width, value_step, jnp.zeros((half_rows, HEADS, HD), jnp.float32)
            )
        )
        log_totals.append(log_total)
    attended = jnp.concatenate(attended_parts, 0)
    log_all = jnp.concatenate(log_totals, 1)
    attn_low = attended.reshape(tokens, width).astype(jnp.bfloat16)
    hidden = source + jnp.dot(attn_low, full_out, preferred_element_type=jnp.float32)
    full_gate, full_up, full_down, full_mlp_gain = (
        lax.all_gather(gate_weight, ("ctx", "fsdp"), axis=0, tiled=True),
        lax.all_gather(up_weight, ("ctx", "fsdp"), axis=0, tiled=True),
        lax.all_gather(down_weight, ("ctx", "fsdp"), axis=0, tiled=True),
        lax.all_gather(mlp_gain, ("ctx", "fsdp"), axis=0, tiled=True),
    )
    inverse_mid = inverse_rms(hidden)
    mlp_in = (hidden * inverse_mid * full_mlp_gain.astype(jnp.float32)).astype(jnp.bfloat16)
    gate_pre = jnp.dot(mlp_in, full_gate, preferred_element_type=jnp.float32)
    up_pre = jnp.dot(mlp_in, full_up, preferred_element_type=jnp.float32)
    activation = (jax.nn.silu(gate_pre) * up_pre).astype(jnp.bfloat16)
    branch_mlp = jnp.einsum("tf,df->td", activation, full_down, preferred_element_type=jnp.float32)
    layer_output = (hidden + branch_mlp).astype(jnp.bfloat16)
    back_gate, back_up, back_down, back_mlp_gain = (
        lax.all_gather(gate_weight, ("ctx", "fsdp"), axis=0, tiled=True),
        lax.all_gather(up_weight, ("ctx", "fsdp"), axis=0, tiled=True),
        lax.all_gather(down_weight, ("ctx", "fsdp"), axis=0, tiled=True),
        lax.all_gather(mlp_gain, ("ctx", "fsdp"), axis=0, tiled=True),
    )
    grad_out_low = cotangent[0]
    grad_act = jnp.dot(grad_out_low, back_down, preferred_element_type=jnp.float32)
    sigmoid_gate = jax.nn.sigmoid(gate_pre)
    grad_gate = (grad_act * up_pre * sigmoid_gate * (1.0 + gate_pre * (1.0 - sigmoid_gate))).astype(
        jnp.bfloat16
    )
    grad_up = (grad_act * gate_pre * sigmoid_gate).astype(jnp.bfloat16)
    grad_mlp_in = jnp.einsum(
        "tf,df->td", grad_gate, back_gate, preferred_element_type=jnp.float32
    ) + jnp.einsum("tf,df->td", grad_up, back_up, preferred_element_type=jnp.float32)
    mlp_gain_term = jnp.sum(grad_mlp_in * hidden * inverse_mid, 0)
    grad_hidden = grad_out_low.astype(jnp.float32) + general_norm_back(
        grad_mlp_in, hidden, inverse_mid, back_mlp_gain.astype(jnp.float32)
    )
    grad_branch = grad_hidden.astype(jnp.bfloat16)
    back_query, back_key, back_value, back_out, back_attn_gain = (
        lax.all_gather(query_weight, ("ctx", "fsdp"), axis=0, tiled=True),
        lax.all_gather(key_weight, ("ctx", "fsdp"), axis=0, tiled=True),
        lax.all_gather(value_weight, ("ctx", "fsdp"), axis=0, tiled=True),
        lax.all_gather(out_weight, ("ctx", "fsdp"), axis=0, tiled=True),
        lax.all_gather(attn_gain, ("ctx", "fsdp"), axis=0, tiled=True),
    )
    grad_attended = (
        jnp.einsum("te,de->td", grad_branch, back_out, preferred_element_type=jnp.float32)
        .astype(jnp.bfloat16)
        .reshape(tokens, HEADS, HD)
    )
    delta_all = jnp.sum(grad_attended.astype(jnp.float32) * attended, -1).T
    grad_query_parts = []
    for slot_index in range(2):
        slot_queries = queries[slot_index * half_rows : (slot_index + 1) * half_rows]
        slot_pos = query_pos[slot_index * half_rows : (slot_index + 1) * half_rows]
        slot_grad_out = grad_attended[slot_index * half_rows : (slot_index + 1) * half_rows]
        slot_delta = delta_all[:, slot_index * half_rows : (slot_index + 1) * half_rows]
        slot_log = log_totals[slot_index]

        def query_step(accumulated, key_rows, value_rows, key_pos):
            scores, visible = score_rows(slot_queries, key_rows, slot_pos, key_pos)
            weights_full = softmax_rows(scores, visible, slot_log)
            grad_weights = jnp.einsum(
                "qhd,khd->hqk", slot_grad_out, value_rows, preferred_element_type=jnp.float32
            )
            grad_scores = (weights_full * (grad_weights - slot_delta[..., None])).astype(
                jnp.bfloat16
            )
            return accumulated + jnp.einsum(
                "hqk,khd->qhd", grad_scores, key_rows, preferred_element_type=jnp.float32
            )

        grad_query_parts.append(
            walk_keys(
                kv_steps,
                top_list[slot_index],
                width,
                query_step,
                jnp.zeros((half_rows, HEADS, HD), jnp.float32),
            )
        )
    grad_queries = jnp.concatenate(grad_query_parts, 0) * score_scale
    grad_query_low = (
        rotate_back(grad_queries, cosine, sine_tab).reshape(tokens, width).astype(jnp.bfloat16)
    )
    bottom_key = jnp.min(query_pos)
    query_both = lax.all_gather(
        jnp.concatenate([queries.reshape(tokens, width), grad_attended.reshape(tokens, width)], 1),
        "ctx",
        axis=0,
        tiled=True,
    )
    stats_both = lax.all_gather(
        jnp.stack([log_all.T, delta_all.T], 1).astype(jnp.bfloat16), "ctx", axis=0, tiled=True
    ).astype(jnp.float32)
    all_pos = (block_ids[:, None] * half_rows + inner[None, :]).reshape(length)
    own_keys = keys_low.reshape(tokens, HEADS, HD)
    own_values = value_low.reshape(tokens, HEADS, HD)

    def gather_step(carried, piece_index):
        first = piece_index * step_rows
        piece_pos = lax.dynamic_slice_in_dim(all_pos, first, step_rows)

        def live_piece(state):
            rows_here = lax.dynamic_slice_in_dim(query_both, first, step_rows, 0)
            stats_here = lax.dynamic_slice_in_dim(stats_both, first, step_rows, 0)
            piece_queries = rows_here[:, :width].reshape(step_rows, HEADS, HD)
            piece_grads = rows_here[:, width:].reshape(step_rows, HEADS, HD)
            piece_log = stats_here[:, 0, :].T
            piece_delta = stats_here[:, 1, :].T
            scores, visible = score_rows(piece_queries, own_keys, piece_pos, query_pos)
            weights_full = softmax_rows(scores, visible, piece_log)
            grad_weights = jnp.einsum(
                "qhd,khd->hqk", piece_grads, own_values, preferred_element_type=jnp.float32
            )
            grad_scores = (weights_full * (grad_weights - piece_delta[..., None])).astype(
                jnp.bfloat16
            )
            grad_keys = (
                jnp.einsum(
                    "hqk,qhd->khd", grad_scores, piece_queries, preferred_element_type=jnp.float32
                )
                * score_scale
            )
            grad_values = jnp.einsum(
                "hqk,qhd->khd",
                weights_full.astype(jnp.bfloat16),
                piece_grads,
                preferred_element_type=jnp.float32,
            )
            return (state[0] + grad_keys, state[1] + grad_values)

        updated = lax.cond(
            jnp.max(piece_pos) >= bottom_key, live_piece, lambda state: state, carried
        )
        return (updated, None)

    start_grads = (
        jnp.zeros((tokens, HEADS, HD), jnp.float32),
        jnp.zeros((tokens, HEADS, HD), jnp.float32),
    )
    summed, ignored = lax.scan(
        gather_step, start_grads, jnp.arange(length // step_rows, dtype=jnp.int32)
    )
    kv_grads = jnp.concatenate(
        [summed[0].reshape(tokens, width), summed[1].reshape(tokens, width)], 1
    )
    grad_key_low = (
        rotate_back(kv_grads[:, :width].reshape(tokens, HEADS, HD), cosine, sine_tab)
        .reshape(tokens, width)
        .astype(jnp.bfloat16)
    )
    grad_value_low = kv_grads[:, width:].astype(jnp.bfloat16)
    grad_normed = jnp.einsum(
        "te,de->td", grad_query_low, back_query, preferred_element_type=jnp.float32
    )
    grad_normed = grad_normed + jnp.einsum(
        "te,de->td", grad_key_low, back_key, preferred_element_type=jnp.float32
    )
    grad_normed = grad_normed + jnp.einsum(
        "te,de->td", grad_value_low, back_value, preferred_element_type=jnp.float32
    )
    attn_gain_term = jnp.sum(grad_normed * source * inverse_in, 0)
    input_grad = grad_hidden + general_norm_back(
        grad_normed, source, inverse_in, back_attn_gain.astype(jnp.float32)
    )

    def outer_sum(left_side, right_side):
        return jnp.einsum("tc,te->ce", left_side, right_side, preferred_element_type=jnp.float32)

    weight_grads = lax.psum_scatter(
        jnp.concatenate(
            [
                outer_sum(normed, grad_query_low),
                outer_sum(normed, grad_key_low),
                outer_sum(normed, grad_value_low),
                outer_sum(attn_low, grad_branch),
                outer_sum(mlp_in, grad_gate),
                outer_sum(mlp_in, grad_up),
                outer_sum(grad_out_low, activation),
            ],
            1,
        ),
        ("ctx", "fsdp"),
        scatter_dimension=0,
        tiled=True,
    )
    gain_grads = lax.psum_scatter(
        jnp.stack([attn_gain_term, mlp_gain_term], 1),
        ("ctx", "fsdp"),
        scatter_dimension=0,
        tiled=True,
    )
    hidden_units = gate_weight.shape[1]
    edge_attn = 4 * width
    return (
        layer_output[None],
        input_grad[None],
        gain_grads[:, 0],
        weight_grads[:, 0:width],
        weight_grads[:, width : 2 * width],
        weight_grads[:, 2 * width : 3 * width],
        weight_grads[:, 3 * width : edge_attn],
        gain_grads[:, 1],
        weight_grads[:, edge_attn : edge_attn + hidden_units],
        weight_grads[:, edge_attn + hidden_units : edge_attn + 2 * hidden_units],
        weight_grads[:, edge_attn + 2 * hidden_units : edge_attn + 3 * hidden_units],
    )


def solution(mesh):
    both = ("ctx", "fsdp")
    rows = P(both, None)
    tokens = P("fsdp", "ctx", None)
    return jax.shard_map(
        fast_body if mesh.shape["ctx"] == 16 and mesh.shape["fsdp"] == 2 else general_body,
        mesh=mesh,
        in_specs=(tokens, P("fsdp", None, None), P(both), rows, rows, rows, rows, P(both), rows, rows, rows, tokens),
        out_specs=(tokens, tokens, P(both), rows, rows, rows, rows, P(both), rows, rows, rows),
        check_vma=False,
    )
```
